32 devices in a mesh: slab: 8 (over z, y), grp: 4 (over x, core).
Axes of the slice: x: 2, y: 2, z: 4, core: 2. Of those that a mesh axis runs over, the one named last changes fastest.
Arguments:
- u_now: float32 [3, 128, 32, 128], P(None, 'slab', 'grp'), may hold values from -6 to 6
- u_prev: float32 [3, 128, 32, 128], P(None, 'slab', 'grp'), may hold values from -6 to 6
- force: float32 [3, 128, 32, 128], P(None, 'slab', 'grp'), may hold values from -6 to 6
- stiffness: float32 [128, 32, 128], P('slab', 'grp'), may hold values from 0.5 to 2
- broken: int32 [32, 8, 32], P('slab', 'grp'), may hold values 0 or 1
- flags: int32 [32, 8, 32], P('slab', 'grp'), may hold values 0 or 1
Outputs:
- displacement: float32 [3, 128, 32, 128], P(None, 'slab', 'grp')
- coeffs: float32 [6, 32, 128, 128], P(None, 'grp', 'slab')
The draws below stay inside these ranges and needn't reach their ends.
All inputs are finite; a program needn't handle non-finite values. No bound on the sum of `broken` or of `flags` on one device may be relied on, other than what follows from the above.
Results may differ from the reference program's by a relative error of at most 0.0001.
Values sent between devices are 32-bit elements; how exact they have to be, the bound alone decides.
A program may use at most 64 MiB of HBM per device.

```python
import math
import jax
import jax.numpy as jnp
import numpy as np
from jax import lax

NZ = 128
STEPS = 2
ITERS = 2
LEVELS = 3
NX = 128
NY = 32


def place_ends(values, stream_key, low, largest):
    longest = values.shape.index(max(values.shape))
    spots = []
    for shift in (0, 1):
        where = [jax.random.randint(jax.random.fold_in(stream_key, axis), (), 0, length) for axis, length in enumerate(values.shape)]
        where[longest] = (where[longest] + shift) % values.shape[longest]
        spots.append(tuple(where))
    return values.at[spots[0]].set(low).at[spots[1]].set(largest)


def level_of(stream_key, extent, split, least, largest):
    gain, own = 1.0, jax.random.fold_in(stream_key, 6)
    for axis_at, parts in split:
        steps = jnp.exp(jax.random.uniform(jax.random.fold_in(own, axis_at), (parts,), jnp.float32, least / len(split), largest / len(split)))
        gain = gain * jnp.repeat(steps, extent[axis_at] // parts).reshape([-1 if axis == axis_at else 1 for axis in range(len(extent))])
    return gain


def gaussian(rng, dims, deviation, reach, split=(), held_as=jnp.bfloat16):
    loudness = level_of(rng, dims, split, -0.22, 0.18) if split else 1.0
    entries = jax.random.normal(rng, dims, jnp.float32) * deviation * loudness
    return jnp.minimum(jnp.maximum(entries, -reach), reach).astype(held_as)


def setup_inputs(seed: int = 0) -> dict:
    key_of = jax.random.split(jax.random.key(seed), 7)
    u_now = gaussian(key_of[0], (3, NX, NY, NZ), 1.0, 6.0, ((1, 8), (2, 4)), jnp.float32)
    u_prev = gaussian(key_of[1], (3, NX, NY, NZ), 1.0, 6.0, ((1, 8), (2, 4)), jnp.float32)
    force = gaussian(key_of[2], (3, NX, NY, NZ), 1.0, 6.0, ((1, 8), (2, 4)), jnp.float32)
    stiffness = jnp.clip(jnp.exp(math.log(2.0) - 1.3862944 * jax.random.uniform(key_of[3], (NX, NY, NZ), jnp.float32) ** level_of(key_of[3], (NX, NY, NZ), ((0, 8), (1, 4)), -0.2, 0.2)), 0.5, 2.0)
    broken = place_ends((jax.random.randint(key_of[4], (NX // 4, NY // 4, NZ // 4), 0, 4) < 1).astype(jnp.int32), jax.random.fold_in(key_of[4], 1), 0, 1)
    flags = place_ends((jax.random.randint(key_of[5], (NX // 4, NY // 4, NZ // 4), 0, 3) < 2).astype(jnp.int32), jax.random.fold_in(key_of[5], 1), 0, 1)
    return {"u_now": u_now, "u_prev": u_prev, "force": force, "stiffness": stiffness, "broken": broken, "flags": flags}


SPRING_NORMAL = 1.0
SPRING_SHEAR = 0.4
MASS_TERM = 1.0
CRACK_CUT = 0.9

def cosine_table():
    freq = np.arange(4)[:, None]
    place = np.arange(4)[None, :]
    factor = np.where(freq == 0, 0.5, np.sqrt(0.5))
    return factor * np.cos(np.pi * (2 * place + 1) * freq / 8.0)

def spread(mask):
    values = mask.astype(jnp.float32)
    size_a, size_b, size_c = values.shape
    wide = jnp.broadcast_to(values[:, None, :, None, :, None], (size_a, 4, size_b, 4, size_c, 4))
    return wide.reshape(size_a * 4, size_b * 4, size_c * 4)

def sides(padded, axis_index):
    leading = padded.ndim - 3

    def cut(offset):
        index_list = [slice(None)] * leading + [slice(1, -1)] * 3
        length = padded.shape[leading + axis_index]
        index_list[leading + axis_index] = slice(1 + offset, length - 1 + offset)
        return padded[tuple(index_list)]
    return (cut(1), cut(-1))

def springs(field, weight, field_pad, weight_pad):
    result = MASS_TERM * field
    for axis_index in range(3):
        upper_v, lower_v = sides(field_pad, axis_index)
        upper_w, lower_w = sides(weight_pad, axis_index)
        k_upper = 0.5 * (weight + upper_w)
        k_lower = 0.5 * (weight + lower_w)
        change = k_upper * (field - upper_v) + k_lower * (field - lower_v)
        coupling = jnp.array([SPRING_NORMAL if comp == axis_index else SPRING_SHEAR for comp in range(3)], jnp.float32).reshape(3, 1, 1, 1)
        result = result + coupling * change
    return result

def stresses(field, carry, field_pad):
    rows_out = []
    for axis_index in range(3):
        upper_v, lower_v = sides(field_pad, axis_index)
        rows_out.append(SPRING_NORMAL * carry * 0.5 * (upper_v[axis_index] - lower_v[axis_index]))
    return jnp.stack(rows_out)

def lift(signal):
    even = signal[..., 0::2]
    odd = signal[..., 1::2]
    detail = odd - 0.5 * (even + jnp.roll(even, -1, axis=-1))
    approx = even + 0.25 * (jnp.roll(detail, 1, axis=-1) + detail)
    return (approx, detail)

def wavelet(signal):
    pieces = []
    approx = signal
    for level_index in range(LEVELS):
        approx, detail = lift(approx)
        pieces.insert(0, detail)
    return jnp.concatenate([approx] + pieces, axis=-1)

def block_transform(fields):
    table = jnp.asarray(cosine_table(), jnp.float32)
    chans, size_x, size_y, size_z = fields.shape
    grid = fields.reshape(chans, size_x // 4, 4, size_y // 4, 4, size_z // 4, 4)
    grid = jnp.einsum('ai,hpiqjrk->hpaqjrk', table, grid, precision=lax.Precision.HIGHEST)
    grid = jnp.einsum('bj,hpaqjrk->hpaqbrk', table, grid, precision=lax.Precision.HIGHEST)
    grid = jnp.einsum('ck,hpaqbrk->hpaqbrc', table, grid, precision=lax.Precision.HIGHEST)
    return grid.reshape(fields.shape)

def reference(u_now, u_prev, force, stiffness, broken, flags):
    weight = stiffness * (1.0 - CRACK_CUT * spread(broken))
    carry = spread(flags) * weight
    weight_pad = jnp.pad(weight, 1)

    def operate(field):
        field_pad = jnp.pad(field, ((0, 0), (1, 1), (1, 1), (1, 1)))
        return springs(field, weight, field_pad, weight_pad)
    for step_index in range(STEPS):
        rhs = MASS_TERM * (2.0 * u_now - u_prev) + force
        guess = u_now
        residual = rhs - operate(guess)
        direction = residual
        norm_now = jnp.sum(residual * residual)
        for turn_index in range(ITERS):
            image = operate(direction)
            alpha = norm_now / jnp.sum(direction * image)
            guess = guess + alpha * direction
            residual = residual - alpha * image
            if turn_index + 1 < ITERS:
                norm_next = jnp.sum(residual * residual)
                direction = residual + norm_next / norm_now * direction
                norm_now = norm_next
        u_prev = u_now
        u_now = guess
    field_pad = jnp.pad(u_now, ((0, 0), (1, 1), (1, 1), (1, 1)))
    fields = jnp.concatenate([u_now, stresses(u_now, carry, field_pad)], axis=0)
    blockc = block_transform(fields)
    coeffs = wavelet(jnp.transpose(blockc, (0, 2, 3, 1)))
    return (u_now, coeffs)
```

```python
import jax
import jax.numpy as jnp
import numpy as np
from jax import lax
from jax.experimental import pallas as pl
from jax.experimental.pallas import tpu as pltpu
from jax.sharding import PartitionSpec as P

STEPS = 2
ITERS = 2
LEVELS = 3


SPRING_NORMAL = 1.0
SPRING_SHEAR = 0.4
MASS_TERM = 1.0
CRACK_CUT = 0.9


def with_halo(block, sides, width):
    for axis, dim in sides:
        count = lax.axis_size(axis)
        forward = [(i, i + 1) for i in range(count - 1)]
        backward = [(target, source) for source, target in forward]
        low = lax.ppermute(
            lax.slice_in_dim(block, block.shape[dim] - width, None, axis=dim), axis, forward
        )
        high = lax.ppermute(lax.slice_in_dim(block, 0, width, axis=dim), axis, backward)
        block = jnp.concatenate([low, block, high], axis=dim)
    return block


def cosine_table():
    freq = np.arange(4)[:, None]
    place = np.arange(4)[None, :]
    factor = np.where(freq == 0, 0.5, np.sqrt(0.5))
    return factor * np.cos(np.pi * (2 * place + 1) * freq / 8.0)


def block_table(count):
    return jnp.asarray(np.kron(np.eye(count // 4), cosine_table()), jnp.float32)


def spread(mask):
    values = mask.astype(jnp.float32)
    size_a, size_b, size_c = values.shape
    wide = jnp.broadcast_to(values[:, None, :, None, :, None], (size_a, 4, size_b, 4, size_c, 4))
    return wide.reshape(size_a * 4, size_b * 4, size_c * 4)


def sides(padded, axis_index):
    leading = padded.ndim - 3

    def cut(offset):
        index_list = [slice(None)] * leading + [slice(1, -1)] * 3
        length = padded.shape[leading + axis_index]
        index_list[leading + axis_index] = slice(1 + offset, length - 1 + offset)
        return padded[tuple(index_list)]

    return (cut(1), cut(-1))


def springs(field, weight, field_pad, weight_pad):
    result = MASS_TERM * field
    for axis_index in range(3):
        upper_v, lower_v = sides(field_pad, axis_index)
        upper_w, lower_w = sides(weight_pad, axis_index)
        k_upper = 0.5 * (weight + upper_w)
        k_lower = 0.5 * (weight + lower_w)
        change = k_upper * (field - upper_v) + k_lower * (field - lower_v)
        coupling = jnp.array(
            [SPRING_NORMAL if comp == axis_index else SPRING_SHEAR for comp in range(3)],
            jnp.float32,
        ).reshape(3, 1, 1, 1)
        result = result + coupling * change
    return result


def faces(field):
    padded = with_halo(field, (("slab", 1), ("grp", 2)), 1)
    return jnp.pad(padded, ((0, 0), (0, 0), (0, 0), (1, 1)))


def stresses(carry, field_pad):
    rows_out = []
    for axis_index in range(3):
        upper_v, lower_v = sides(field_pad, axis_index)
        rows_out.append(SPRING_NORMAL * carry * 0.5 * (upper_v[axis_index] - lower_v[axis_index]))
    return jnp.stack(rows_out)


def paired_sum(residual, image):
    return lax.psum((jnp.sum(residual * residual), jnp.sum(residual * image)), ("slab", "grp"))


def lift(signal):
    even = signal[..., 0::2]
    odd = signal[..., 1::2]
    detail = odd - 0.5 * (even + jnp.roll(even, -1, axis=-1))
    approx = even + 0.25 * (jnp.roll(detail, 1, axis=-1) + detail)
    return (approx, detail)


def wavelet(signal):
    pieces = []
    approx = signal
    for level_index in range(LEVELS):
        approx, detail = lift(approx)
        pieces.insert(0, detail)
    return jnp.concatenate([approx] + pieces, axis=-1)


def body(u_now, u_prev, force, stiffness, broken, flags):
    weight = stiffness * (1.0 - CRACK_CUT * spread(broken))
    carry = spread(flags) * weight
    weight_pad = with_halo(weight, (("slab", 0), ("grp", 1)), 1)
    weight_pad = jnp.pad(weight_pad, ((0, 0), (0, 0), (1, 1)))

    def operate(field):
        return springs(field, weight, faces(field), weight_pad)

    for step_index in range(STEPS):
        rhs = MASS_TERM * (2.0 * u_now - u_prev) + force
        guess = u_now
        residual = rhs - operate(guess)
        image = operate(residual)
        norm_now, product = paired_sum(residual, image)
        alpha = norm_now / product
        direction, along = (residual, image)
        for turn_index in range(ITERS):
            guess = guess + alpha * direction
            residual = residual - alpha * along
            if turn_index + 1 < ITERS:
                image = operate(residual)
                norm_next, product = paired_sum(residual, image)
                ratio = norm_next / norm_now
                alpha = norm_next / (product - ratio * norm_next / alpha)
                direction = residual + ratio * direction
                along = image + ratio * along
                norm_now = norm_next
        u_prev = u_now
        u_now = guess
    stress = stresses(carry, faces(u_now))
    fields = jnp.concatenate([u_now, stress], axis=0)
    table_x = block_table(fields.shape[1])
    table_y = block_table(fields.shape[2])
    table_z = block_table(fields.shape[3])
    blockc = jnp.einsum("ax,hxyz->hayz", table_x, fields, precision=lax.Precision.HIGHEST)
    blockc = jnp.einsum("by,hxyz->hxbz", table_y, blockc, precision=lax.Precision.HIGHEST)
    blockc = jnp.einsum("hxyz,cz->hxyc", blockc, table_z, precision=lax.Precision.HIGHEST)
    moved = jnp.transpose(blockc, (0, 2, 3, 1))
    shipped = lax.all_to_all(moved, "slab", split_axis=2, concat_axis=3, tiled=True)
    coeffs = wavelet(shipped)
    return (u_now, coeffs)


MESH = pl.DeviceIdType.MESH
HALO = 4
REACH = 3
SHEAR_REST = SPRING_NORMAL - SPRING_SHEAR


def wavelet_table(count):
    table = np.kron(np.eye(count // 4), cosine_table())
    pieces = []
    approx = table
    for level_index in range(LEVELS):
        even, odd = approx[0::2], approx[1::2]
        detail = odd - 0.5 * (even + np.roll(even, -1, axis=0))
        approx = even + 0.25 * (np.roll(detail, 1, axis=0) + detail)
        pieces.insert(0, detail)
    return np.concatenate([approx] + pieces, axis=0)


def sub_index():
    return lax.broadcasted_iota(jnp.int32, (8, 128), 0)


def lane_index():
    return lax.broadcasted_iota(jnp.int32, (8, 128), 1)


def up_y(a, b):
    ra, rb = pltpu.roll(a, 7, 0), pltpu.roll(b, 7, 0)
    last = sub_index() == 7
    return jnp.where(last, rb, ra), jnp.where(last, ra, rb)


def down_y(a, b):
    ra, rb = pltpu.roll(a, 1, 0), pltpu.roll(b, 1, 0)
    first = sub_index() == 0
    return jnp.where(first, rb, ra), jnp.where(first, ra, rb)


def up_z(v):
    return pltpu.roll(v, 127, 1)


def down_z(v):
    return pltpu.roll(v, 1, 1)


def total(v):
    return jnp.sum(jnp.sum(v, axis=0, keepdims=True), axis=1, keepdims=True)


def kernel(ns, ng, u_ref, p_ref, f_ref, k_ref, br_ref, fl_ref, ez_ref, cz_ref, gt_ref,
           disp_ref, coef_ref,
           e1a, e1b, s1, h1, e2a, e2b, s2, h2, rqa, rqb, e3a, s3, h3,
           u1a, u1b, carry, dga, dgb, kca, kcb, gath, rows, outb, inb,
           send1, recv1, send2, recv2, send3, recv3, asend, arecv, tsend, trecv):
    X, Y = u_ref.shape[1], u_ref.shape[2]
    si, gi = lax.axis_index("slab"), lax.axis_index("grp")
    me = si * ng + gi
    count = ns * ng
    barrier = pltpu.get_barrier_semaphore()

    def greet(i, _):
        other = lax.rem(me + i, count)
        pl.semaphore_signal(barrier, inc=1, device_id=(other // ng, lax.rem(other, ng)), device_id_type=MESH)
        return 0

    lax.fori_loop(1, count, greet, 0)

    sub, lane = sub_index(), lane_index()
    upper = sub < 4

    steps = [(-1, 0), (1, 0), (0, -1), (0, 1), (-1, -1), (-1, 1), (1, -1), (1, 1)]

    def inside(ds, dg):
        ok = None
        if ds:
            ok = (si >= 1) if ds < 0 else (si <= ns - 2)
        if dg:
            more = (gi >= 1) if dg < 0 else (gi <= ng - 2)
            ok = more if ok is None else jnp.logical_and(ok, more)
        return ok

    def copies(ea, dst_a, stage, land, send, recv):
        half = X // 2
        edge = HALO // 2
        made = []
        for at, (ds, dg) in enumerate(steps):
            if dg == 0:
                if ds < 0:
                    source = ea.at[:, pl.ds(HALO, REACH)]
                    target = dst_a.at[:, pl.ds(HALO + X, REACH)]
                else:
                    source = ea.at[:, pl.ds(HALO + X - REACH, REACH)]
                    target = dst_a.at[:, pl.ds(HALO - REACH, REACH)]
            else:
                side = 0 if dg < 0 else 1
                if ds == 0:
                    source, target = stage.at[side], land.at[side, :, pl.ds(edge, half)]
                elif ds < 0:
                    source = stage.at[side, :, pl.ds(0, edge)]
                    target = land.at[side, :, pl.ds(edge + half, edge)]
                else:
                    source = stage.at[side, :, pl.ds(half - edge, edge)]
                    target = land.at[side, :, pl.ds(0, edge)]
            made.append((ds, dg, pltpu.make_async_remote_copy(
                src_ref=source, dst_ref=target, send_sem=send.at[at], recv_sem=recv.at[at ^ 1 if at < 4 else 11 - at],
                device_id=(si + ds, gi + dg), device_id_type=MESH)))
        return made

    def begin(made):
        for ds, dg, copy in made:
            @pl.when(inside(ds, dg))
            def _():
                copy.start()

    def finish_recv(made, recv):
        for at, (ds, dg) in enumerate(steps):
            back = made[at ^ 1 if at < 4 else 11 - at][2]

            @pl.when(inside(ds, dg))
            def _():
                back.wait_recv()

    def finish_send(made):
        for ds, dg, copy in made:
            @pl.when(inside(ds, dg))
            def _():
                copy.wait_send()

    def blank(dst_a, land):
        zero_a = jnp.zeros((dst_a.shape[0], HALO) + dst_a.shape[2:], jnp.float32)
        half, edge = X // 2, HALO // 2
        zero_l = jnp.zeros((land.shape[1], edge, 8, 128), jnp.float32)

        @pl.when(si == 0)
        def _():
            dst_a[:, pl.ds(0, HALO)] = zero_a
            for side in range(2):
                land[side, :, pl.ds(0, edge)] = zero_l

        @pl.when(si == ns - 1)
        def _():
            dst_a[:, pl.ds(HALO + X, HALO)] = zero_a
            for side in range(2):
                land[side, :, pl.ds(edge + half, edge)] = zero_l

        for side, edge_here in ((0, gi == ng - 1), (1, gi == 0)):
            @pl.when(edge_here)
            def _(side=side):
                land[side] = jnp.zeros(land.shape[1:], jnp.float32)

    def pack(stage, ch, pair, even, odd):
        stage[0, ch, pair] = jnp.where(upper, even, pltpu.roll(odd, 4, 0))
        stage[1, ch, pair] = jnp.where(upper, pltpu.roll(even, 4, 0), odd)

    def unpack(land, ch, pair):
        high, low = land[0, ch, pair], land[1, ch, pair]
        return (jnp.where(upper, high, pltpu.roll(low, 4, 0)),
                jnp.where(upper, pltpu.roll(high, 4, 0), low))

    def spread_rows(mask):
        wide = jnp.dot(mask.astype(jnp.float32), ez_ref[...], preferred_element_type=jnp.float32)
        return jnp.where(upper, jnp.broadcast_to(wide[0:1], (8, 128)), jnp.broadcast_to(wide[1:2], (8, 128)))

    for bx in range(X // 4):
        cut = 1.0 - CRACK_CUT * spread_rows(br_ref[bx])
        flag = spread_rows(fl_ref[bx])
        for at in range(4):
            x = bx * 4 + at
            w = k_ref[x] * cut
            e1a[6, HALO + x] = w
            carry[x] = flag * w

    def own(i, _):
        for c in range(3):
            tiles = []
            for o in range(2):
                x = 2 * i + o
                u = u_ref[c, x]
                f = f_ref[c, x]
                rhs = MASS_TERM * (2.0 * u - p_ref[c, x]) + f
                e1a[c, HALO + x] = u
                e1a[3 + c, HALO + x] = rhs
                e2a[c, HALO + x] = f
                tiles.append((u, rhs, f))
            pack(s1, c, i, tiles[0][0], tiles[1][0])
            pack(s1, 3 + c, i, tiles[0][1], tiles[1][1])
            pack(s2, c, i, tiles[0][2], tiles[1][2])
        pack(s1, 6, i, e1a[6, HALO + 2 * i], e1a[6, HALO + 2 * i + 1])
        return 0

    lax.fori_loop(0, X // 2, own, 0)
    blank(e1a, h1)
    blank(e2a, h2)
    blank(e3a, h3)

    first = copies(e1a, e1a, s1, h1, send1, recv1)
    second = copies(e2a, e2a, s2, h2, send2, recv2)
    third = copies(rqa, e3a, s3, h3, send3, recv3)
    pl.semaphore_wait(barrier, count - 1)
    begin(first)
    finish_recv(first, recv1)
    begin(second)

    def open1(i, _):
        for ch in range(7):
            e1b[ch, 2 * i], e1b[ch, 2 * i + 1] = unpack(h1, ch, i)
        return 0

    lax.fori_loop(0, (X + 2 * HALO) // 2, open1, 0)

    def link(w, other):
        return jnp.where(jnp.minimum(w, other) > 0.0, 0.5 * (w + other), 0.0)

    not_last, not_first = lane < 127, lane > 0

    def coefficients(x, _):
        wa, wb = e1a[6, x], e1b[6, x]
        ya, yb = up_y(wa, wb)
        da, db = down_y(wa, wb)
        for w, wu, wd, yu, yd, dg, kc in (
            (wa, e1a[6, x + 1], e1a[6, x - 1], ya, da, dga, kca),
            (wb, e1b[6, x + 1], e1b[6, x - 1], yb, db, dgb, kcb),
        ):
            zu = jnp.where(not_last, up_z(w), 0.0)
            zd = jnp.where(not_first, down_z(w), 0.0)
            kc[0, x] = link(w, wu)
            kc[1, x] = link(w, yu)
            kc[2, x] = link(w, yd)
            kc[3, x] = link(w, zu)
            kc[4, x] = link(w, zd)
            sx = w + 0.5 * (wu + wd)
            sy = w + 0.5 * (yu + yd)
            sz = w + 0.5 * (zu + zd)
            every = MASS_TERM + SPRING_SHEAR * (sx + sy + sz)
            dg[0, x] = every + SHEAR_REST * sx
            dg[1, x] = every + SHEAR_REST * sy
            dg[2, x] = every + SHEAR_REST * sz
        return 0

    kca[0, HALO - REACH] = link(e1a[6, HALO - REACH], e1a[6, HALO - REACH + 1])
    kcb[0, HALO - REACH] = link(e1b[6, HALO - REACH], e1b[6, HALO - REACH + 1])
    lax.fori_loop(HALO - 2, HALO + X + 2, coefficients, 0)

    def operate(x, va, vb, base):
        result = []
        coef = [[kc[j, x] for j in range(5)] + [kc[0, x - 1]] for kc in (kca, kcb)]
        for c in range(3):
            a, b = va[base + c, x], vb[base + c, x]
            ua, ub = up_y(a, b)
            la, lb = down_y(a, b)
            pair = []
            for v, ref, u, l, k, dg in ((a, va, ua, la, coef[0], dga), (b, vb, ub, lb, coef[1], dgb)):
                parts = (
                    k[0] * ref[base + c, x + 1] + k[5] * ref[base + c, x - 1],
                    k[1] * u + k[2] * l,
                    k[3] * up_z(v) + k[4] * down_z(v),
                )
                every = parts[0] + parts[1] + parts[2]
                pair.append(dg[c, x] * v - (SPRING_SHEAR * every + SHEAR_REST * parts[c]))
            result.append(pair)
        return result

    def solve(step, va, vb, rhs_of):
        def residual(x, _):
            image = operate(x, va, vb, 0)
            for c in range(3):
                ra, rb = rhs_of(c, x)
                rqa[c, x] = ra - image[c][0]
                rqb[c, x] = rb - image[c][1]
            return 0

        lax.fori_loop(HALO - 2, HALO + X + 2, residual, 0)

        def apply(x, _):
            image = operate(x, rqa, rqb, 0)
            for c in range(3):
                rqa[3 + c, x] = image[c][0]
                rqb[3 + c, x] = image[c][1]
            return 0

        lax.fori_loop(HALO - 1, HALO + X + 1, apply, 0)

        def products(x, sums):
            rr, rq = sums
            for c in range(3):
                r, q = rqa[c, x], rqa[3 + c, x]
                rr, rq = rr + r * r, rq + r * q
            return rr, rq

        zero = jnp.zeros((8, 128), jnp.float32)
        rr, rq = lax.fori_loop(HALO, HALO + X, products, (zero, zero))
        rr, rq = total(rr), total(rq)
        mu = jnp.where(rr > 0.0, rq / jnp.where(rr > 0.0, rr, 1.0), 0.0)

        def centred(x, sums):
            ww, wr, mix, wt = sums
            image = operate(x, rqa, rqb, 3)
            for c in range(3):
                r, q, s = rqa[c, x], rqa[3 + c, x], image[c][0]
                w, t = q - mu * r, s - mu * q
                ww, wr, mix, wt = ww + w * w, wr + w * r, mix + (r * t + w * q), wt + w * t
            return ww, wr, mix, wt

        sums = lax.fori_loop(HALO, HALO + X, centred, (zero,) * 4)
        ww, wr, mix, wt = [total(v) for v in sums]
        one = lax.broadcasted_iota(jnp.int32, (1, 128), 1)
        row = jnp.zeros((1, 128), jnp.float32)
        for at, value in enumerate((rr, rq, mu, ww, wr, mix, wt)):
            row = jnp.where(one == at, value, row)
        gath[step, me] = row

        def share(i, _):
            other = lax.rem(me + i, count)
            pltpu.make_async_remote_copy(
                src_ref=gath.at[step, me], dst_ref=gath.at[step, me], send_sem=asend.at[step], recv_sem=arecv.at[step],
                device_id=(other // ng, lax.rem(other, ng)), device_id_type=MESH).start()
            return 0

        lax.fori_loop(1, count, share, 0)

    def collect(step):
        block = gath.at[step, pl.ds(0, count - 1)]
        pltpu.make_async_copy(block, block, arecv.at[step]).wait()
        table = gath[step].reshape(count, 128)
        rr, rq, mu, ww, wr, mix, wt = [table[:, at:at + 1] for at in range(7)]

        def down(v):
            return jnp.sum(v, axis=0, keepdims=True)

        norm = down(rr)
        alpha = norm / down(rq)
        rest = 1.0 - alpha * mu
        after = down(alpha * alpha * ww - 2.0 * alpha * rest * wr + rest * rest * rr)
        curved = down(rest * rest * rq - alpha * rest * mix + alpha * alpha * wt)
        ratio = after / norm
        beta = after / (curved - ratio * after / alpha)
        return alpha + beta * (1.0 + ratio), -beta * alpha

    def drain(step):
        block = gath.at[step, pl.ds(0, count - 1)]
        pltpu.make_async_copy(block, block, asend.at[step]).wait()

    solve(0, e1a, e1b, lambda c, x: (e1a[3 + c, x], e1b[3 + c, x]))

    def pack3(i, _):
        for ch in range(6):
            pack(s3, ch, i, rqa[ch, HALO + 2 * i], rqa[ch, HALO + 2 * i + 1])
        return 0

    lax.fori_loop(0, X // 2, pack3, 0)
    begin(third)

    finish_recv(second, recv2)

    def open2(i, _):
        for ch in range(3):
            e2b[ch, 2 * i], e2b[ch, 2 * i + 1] = unpack(h2, ch, i)
        return 0

    lax.fori_loop(0, (X + 2 * HALO) // 2, open2, 0)
    finish_recv(third, recv3)
    c0, c1 = collect(0)

    def step_b(i, _):
        for c in range(3):
            r0, r1 = unpack(h3, c, i)
            q0, q1 = unpack(h3, 3 + c, i)
            u1b[c, 2 * i] = e1b[c, 2 * i] + (c0 * r0 + c1 * q0)
            u1b[c, 2 * i + 1] = e1b[c, 2 * i + 1] + (c0 * r1 + c1 * q1)
        return 0

    lax.fori_loop(0, (X + 2 * HALO) // 2, step_b, 0)

    def step_a(x, _):
        for c in range(3):
            u1a[c, x] = e1a[c, x] + (c0 * rqa[c, x] + c1 * rqa[3 + c, x])
        return 0

    lax.fori_loop(HALO, HALO + X, step_a, 0)
    for x in list(range(HALO - REACH, HALO)) + list(range(HALO + X, HALO + X + REACH)):
        for c in range(3):
            u1a[c, x] = e1a[c, x] + (c0 * e3a[c, x] + c1 * e3a[3 + c, x])
    finish_send(first)
    finish_send(second)
    finish_send(third)

    def rhs2(c, x):
        return (MASS_TERM * (2.0 * u1a[c, x] - e1a[c, x]) + e2a[c, x],
                MASS_TERM * (2.0 * u1b[c, x] - e1b[c, x]) + e2b[c, x])

    solve(1, u1a, u1b, rhs2)
    c0, c1 = collect(1)

    def step2(x, _):
        for c in range(3):
            va = u1a[c, x] + (c0 * rqa[c, x] + c1 * rqa[3 + c, x])
            vb = u1b[c, x] + (c0 * rqb[c, x] + c1 * rqb[3 + c, x])
            u1a[c, x] = va
            u1b[c, x] = vb
        return 0

    lax.fori_loop(HALO - 1, HALO + X + 1, step2, 0)

    def finals(x, _):
        at = x - HALO
        scale = SPRING_NORMAL * carry[at] * 0.5
        values = [u1a[c, x] for c in range(3)]
        for c in range(3):
            disp_ref[c, at] = values[c]
        dx = u1a[0, x + 1] - u1a[0, x - 1]
        dy = up_y(values[1], u1b[1, x])[0] - down_y(values[1], u1b[1, x])[0]
        dz = jnp.where(not_last, up_z(values[2]), 0.0) - jnp.where(not_first, down_z(values[2]), 0.0)
        for c, v in enumerate(values + [scale * dx, scale * dy, scale * dz]):
            rows[c, pl.ds(at, 8, stride=X), :] = v
        return 0

    lax.fori_loop(HALO, HALO + X, finals, 0)

    zrows = coef_ref.shape[2]

    def transform(c, _):
        turned = lax.dot_general(cz_ref[...], rows[c], (((1,), (1,)), ((), ())),
                                 precision=lax.Precision.HIGHEST, preferred_element_type=jnp.float32)
        for j in range(ns):
            outb[j, c] = turned[j * zrows:(j + 1) * zrows]
        return 0

    lax.fori_loop(0, 6, transform, 0)

    def trade(i):
        to = lax.rem(si + i, ns)
        return pltpu.make_async_remote_copy(
            src_ref=outb.at[to], dst_ref=inb.at[i], send_sem=tsend.at[i], recv_sem=trecv.at[i],
            device_id=(to, gi), device_id_type=MESH)

    trades = [None] + [trade(i) for i in range(1, ns)]
    for i in range(1, ns):
        trades[i].start()
    inb[0] = outb[si]
    for i in range(1, ns):
        trades[i].wait_recv()

    zlane = lax.broadcasted_iota(jnp.int32, (zrows, 128), 1)
    c1t, c3t = float(np.sqrt(0.5) * np.cos(np.pi / 8)), float(np.sqrt(0.5) * np.cos(3 * np.pi / 8))

    def gather_back(c, _):
        pieces = [None] * Y
        for y in range(Y):
            joined = None
            for i in range(ns):
                origin = lax.rem(si - i + ns, ns)
                moved = pltpu.roll(inb[i, c], lax.rem((origin - y + ns) * X, 128), 1)
                here = (zlane // X) == origin
                joined = moved if joined is None else jnp.where(here, moved, joined)
            pieces[y] = joined
        for b in range(Y // 4):
            v0, v1, v2, v3 = pieces[4 * b:4 * b + 4]
            s03, s12, d03, d12 = v0 + v3, v1 + v2, v0 - v3, v1 - v2
            for k, value in enumerate((0.5 * (s03 + s12), c1t * d03 + c3t * d12,
                                       0.5 * (s03 - s12), c3t * d03 - c1t * d12)):
                coef_ref[c, 4 * b + k] = value
        block = coef_ref[c].reshape(Y * zrows, 128)
        done = jnp.dot(block, gt_ref[...], precision=lax.Precision.HIGHEST, preferred_element_type=jnp.float32)
        coef_ref[c] = done.reshape(Y, zrows, 128)
        return 0

    lax.fori_loop(0, 6, gather_back, 0)
    drain(0)
    drain(1)
    for i in range(1, ns):
        trades[i].wait_send()


def fused(mesh, u_now, u_prev, force, stiffness, broken, flags):
    ns, ng = mesh.shape["slab"], mesh.shape["grp"]
    _, X, Y, Z = u_now.shape
    xe, pairs, half = X + 2 * HALO, X // 2 + HALO, X // 2
    zrows = Z // ns
    ez = jnp.asarray(np.kron(np.eye(Z // 4), np.ones((1, 4))), jnp.float32)
    cz = jnp.asarray(np.kron(np.eye(Z // 4), cosine_table()), jnp.float32)
    gt = jnp.asarray(wavelet_table(X * ns).T, jnp.float32)

    def vm(*shape):
        return pltpu.VMEM(shape, jnp.float32)

    def ext(n):
        return vm(n, xe, Y, Z)

    def stage(n):
        return vm(2, n, half, Y, Z)

    def land(n):
        return vm(2, n, pairs, Y, Z)

    dma = pltpu.SemaphoreType.DMA
    return pl.pallas_call(
        lambda *refs: kernel(ns, ng, *refs),
        name="lattice",
        out_shape=(jax.ShapeDtypeStruct(u_now.shape, jnp.float32),
                   jax.ShapeDtypeStruct((6, Y, zrows, X * ns), jnp.float32)),
        in_specs=[pl.BlockSpec(memory_space=pltpu.VMEM)] * 9,
        out_specs=(pl.BlockSpec(memory_space=pltpu.VMEM),) * 2,
        scratch_shapes=[
            ext(7), ext(7), stage(7), land(7),
            ext(3), ext(3), stage(3), land(3),
            ext(6), ext(6), ext(6), stage(6), land(6),
            ext(3), ext(3), vm(X, Y, Z), ext(3), ext(3), ext(5), ext(5),
            vm(2, ns * ng, 1, 128), vm(6, Y * X, Z), vm(ns, 6, zrows, 128), vm(ns, 6, zrows, 128),
            dma((8,)), dma((8,)), dma((8,)), dma((8,)), dma((8,)), dma((8,)),
            dma((2,)), dma((2,)), dma((ns,)), dma((ns,)),
        ],
        compiler_params=pltpu.CompilerParams(collective_id=0, has_side_effects=True, vmem_limit_bytes=48 << 20),
    )(u_now, u_prev, force, stiffness, broken, flags, ez, cz, gt)


def fits(mesh, shape):
    ns, ng = mesh.shape["slab"], mesh.shape["grp"]
    x, y, z = shape[1] // ns, shape[2] // ng, shape[3]
    return y == 8 and z == 128 and x * y == 128 and x * ns == 128 and z % (8 * ns) == 0


def entry(mesh, *args):
    ns, ng = mesh.shape["slab"], mesh.shape["grp"]
    _, x, y, z = args[0].shape
    if fits(mesh, (3, x * ns, y * ng, z)):
        return fused(mesh, *args)
    return body(*args)


def solution(mesh):
    return jax.shard_map(
        lambda *args: entry(mesh, *args),
        mesh=mesh,
        in_specs=(
            P(None, "slab", "grp", None),
            P(None, "slab", "grp", None),
            P(None, "slab", "grp", None),
            P("slab", "grp", None),
            P("slab", "grp", None),
            P("slab", "grp", None),
        ),
        out_specs=(P(None, "slab", "grp", None), P(None, "grp", "slab", None)),
        check_vma=False,
    )
```

```python
import jax
import jax.numpy as jnp
import numpy as np
from jax import lax
from jax.experimental import pallas as pl
from jax.experimental.pallas import tpu as pltpu
from jax.sharding import PartitionSpec as P

STEPS = 2
ITERS = 2
LEVELS = 3


SPRING_NORMAL = 1.0
SPRING_SHEAR = 0.4
MASS_TERM = 1.0
CRACK_CUT = 0.9


def with_halo(block, sides, width):
    for axis, dim in sides:
        count = lax.axis_size(axis)
        forward = [(i, i + 1) for i in range(count - 1)]
        backward = [(target, source) for source, target in forward]
        low = lax.ppermute(
            lax.slice_in_dim(block, block.shape[dim] - width, None, axis=dim), axis, forward
        )
        high = lax.ppermute(lax.slice_in_dim(block, 0, width, axis=dim), axis, backward)
        block = jnp.concatenate([low, block, high], axis=dim)
    return block


def cosine_table():
    freq = np.arange(4)[:, None]
    place = np.arange(4)[None, :]
    factor = np.where(freq == 0, 0.5, np.sqrt(0.5))
    return factor * np.cos(np.pi * (2 * place + 1) * freq / 8.0)


def block_table(count):
    return jnp.asarray(np.kron(np.eye(count // 4), cosine_table()), jnp.float32)


def spread(mask):
    values = mask.astype(jnp.float32)
    size_a, size_b, size_c = values.shape
    wide = jnp.broadcast_to(values[:, None, :, None, :, None], (size_a, 4, size_b, 4, size_c, 4))
    return wide.reshape(size_a * 4, size_b * 4, size_c * 4)


def sides(padded, axis_index):
    leading = padded.ndim - 3

    def cut(offset):
        index_list = [slice(None)] * leading + [slice(1, -1)] * 3
        length = padded.shape[leading + axis_index]
        index_list[leading + axis_index] = slice(1 + offset, length - 1 + offset)
        return padded[tuple(index_list)]

    return (cut(1), cut(-1))


def springs(field, weight, field_pad, weight_pad):
    result = MASS_TERM * field
    for axis_index in range(3):
        upper_v, lower_v = sides(field_pad, axis_index)
        upper_w, lower_w = sides(weight_pad, axis_index)
        k_upper = 0.5 * (weight + upper_w)
        k_lower = 0.5 * (weight + lower_w)
        change = k_upper * (field - upper_v) + k_lower * (field - lower_v)
        coupling = jnp.array(
            [SPRING_NORMAL if comp == axis_index else SPRING_SHEAR for comp in range(3)],
            jnp.float32,
        ).reshape(3, 1, 1, 1)
        result = result + coupling * change
    return result


def faces(field):
    padded = with_halo(field, (("slab", 1), ("grp", 2)), 1)
    return jnp.pad(padded, ((0, 0), (0, 0), (0, 0), (1, 1)))


def stresses(carry, field_pad):
    rows_out = []
    for axis_index in range(3):
        upper_v, lower_v = sides(field_pad, axis_index)
        rows_out.append(SPRING_NORMAL * carry * 0.5 * (upper_v[axis_index] - lower_v[axis_index]))
    return jnp.stack(rows_out)


def paired_sum(residual, image):
    return lax.psum((jnp.sum(residual * residual), jnp.sum(residual * image)), ("slab", "grp"))


def lift(signal):
    even = signal[..., 0::2]
    odd = signal[..., 1::2]
    detail = odd - 0.5 * (even + jnp.roll(even, -1, axis=-1))
    approx = even + 0.25 * (jnp.roll(detail, 1, axis=-1) + detail)
    return (approx, detail)


def wavelet(signal):
    pieces = []
    approx = signal
    for level_index in range(LEVELS):
        approx, detail = lift(approx)
        pieces.insert(0, detail)
    return jnp.concatenate([approx] + pieces, axis=-1)


def body(u_now, u_prev, force, stiffness, broken, flags):
    weight = stiffness * (1.0 - CRACK_CUT * spread(broken))
    carry = spread(flags) * weight
    weight_pad = with_halo(weight, (("slab", 0), ("grp", 1)), 1)
    weight_pad = jnp.pad(weight_pad, ((0, 0), (0, 0), (1, 1)))

    def operate(field):
        return springs(field, weight, faces(field), weight_pad)

    for step_index in range(STEPS):
        rhs = MASS_TERM * (2.0 * u_now - u_prev) + force
        guess = u_now
        residual = rhs - operate(guess)
        image = operate(residual)
        norm_now, product = paired_sum(residual, image)
        alpha = norm_now / product
        direction, along = (residual, image)
        for turn_index in range(ITERS):
            guess = guess + alpha * direction
            residual = residual - alpha * along
            if turn_index + 1 < ITERS:
                image = operate(residual)
                norm_next, product = paired_sum(residual, image)
                ratio = norm_next / norm_now
                alpha = norm_next / (product - ratio * norm_next / alpha)
                direction = residual + ratio * direction
                along = image + ratio * along
                norm_now = norm_next
        u_prev = u_now
        u_now = guess
    stress = stresses(carry, faces(u_now))
    fields = jnp.concatenate([u_now, stress], axis=0)
    table_x = block_table(fields.shape[1])
    table_y = block_table(fields.shape[2])
    table_z = block_table(fields.shape[3])
    blockc = jnp.einsum("ax,hxyz->hayz", table_x, fields, precision=lax.Precision.HIGHEST)
    blockc = jnp.einsum("by,hxyz->hxbz", table_y, blockc, precision=lax.Precision.HIGHEST)
    blockc = jnp.einsum("hxyz,cz->hxyc", blockc, table_z, precision=lax.Precision.HIGHEST)
    moved = jnp.transpose(blockc, (0, 2, 3, 1))
    shipped = lax.all_to_all(moved, "slab", split_axis=2, concat_axis=3, tiled=True)
    coeffs = wavelet(shipped)
    return (u_now, coeffs)


MESH = pl.DeviceIdType.MESH
HALO = 4
REACH = 3
SHEAR_REST = SPRING_NORMAL - SPRING_SHEAR


def wavelet_table(count):
    table = np.kron(np.eye(count // 4), cosine_table())
    pieces = []
    approx = table
    for level_index in range(LEVELS):
        even, odd = approx[0::2], approx[1::2]
        detail = odd - 0.5 * (even + np.roll(even, -1, axis=0))
        approx = even + 0.25 * (np.roll(detail, 1, axis=0) + detail)
        pieces.insert(0, detail)
    return np.concatenate([approx] + pieces, axis=0)


def split_table(table):
    high = table.astype(jnp.bfloat16).astype(np.float64)
    return high, (table - high).astype(jnp.bfloat16).astype(np.float64)


def sub_index():
    return lax.broadcasted_iota(jnp.int32, (8, 128), 0)


def lane_index():
    return lax.broadcasted_iota(jnp.int32, (8, 128), 1)


def up_y(a, b):
    ra, rb = pltpu.roll(a, 7, 0), pltpu.roll(b, 7, 0)
    last = sub_index() == 7
    return jnp.where(last, rb, ra), jnp.where(last, ra, rb)


def down_y(a, b):
    ra, rb = pltpu.roll(a, 1, 0), pltpu.roll(b, 1, 0)
    first = sub_index() == 0
    return jnp.where(first, rb, ra), jnp.where(first, ra, rb)


def up_z(v):
    return pltpu.roll(v, 127, 1)


def down_z(v):
    return pltpu.roll(v, 1, 1)


def total(v):
    return jnp.sum(jnp.sum(v, axis=0, keepdims=True), axis=1, keepdims=True)


def kernel(ns, ng, u_in, p_in, f_in, k_in, br_in, fl_in, ez_in, cz_in, gt_in,
           disp_ref, coef_ref,
           u_ref, p_ref, f_ref, k_ref, br_ref, fl_ref, ez_ref, cz_ref, gt_ref, isem,
           e1a, e1b, s1, h1, e2a, e2b, s2, h2, rqa, rqb, e3a, s3, h3,
           u1a, u1b, carry, dga, dgb, kca, kcb, gath, rows, outb, inb,
           send1, recv1, send2, recv2, send3, recv3, asend, arecv, tsend, trecv):
    X, Y = u_ref.shape[1], u_ref.shape[2]
    si, gi = lax.axis_index("slab"), lax.axis_index("grp")
    me = si * ng + gi
    count = ns * ng
    fetched = []
    for at, (source, target) in enumerate((
        (br_in, br_ref), (fl_in, fl_ref), (ez_in, ez_ref), (k_in, k_ref), (u_in, u_ref), (p_in, p_ref),
        (f_in, f_ref), (cz_in, cz_ref), (gt_in, gt_ref),
    )):
        fetch = pltpu.make_async_copy(source, target, isem.at[at])
        fetch.start()
        fetched.append(fetch)
    barrier = pltpu.get_barrier_semaphore()

    def greet(i, _):
        other = lax.rem(me + i, count)
        pl.semaphore_signal(barrier, inc=1, device_id=(other // ng, lax.rem(other, ng)), device_id_type=MESH)
        return 0

    lax.fori_loop(1, count, greet, 0)

    sub, lane = sub_index(), lane_index()
    upper = sub < 4

    steps = [(-1, 0), (1, 0), (0, -1), (0, 1), (-1, -1), (-1, 1), (1, -1), (1, 1)]

    def inside(ds, dg):
        ok = None
        if ds:
            ok = (si >= 1) if ds < 0 else (si <= ns - 2)
        if dg:
            more = (gi >= 1) if dg < 0 else (gi <= ng - 2)
            ok = more if ok is None else jnp.logical_and(ok, more)
        return ok

    def copies(ea, dst_a, stage, land, send, recv):
        half = X // 2
        edge = HALO // 2
        made = []
        for at, (ds, dg) in enumerate(steps):
            if dg == 0:
                if ds < 0:
                    source = ea.at[:, pl.ds(HALO, REACH)]
                    target = dst_a.at[:, pl.ds(HALO + X, REACH)]
                else:
                    source = ea.at[:, pl.ds(HALO + X - REACH, REACH)]
                    target = dst_a.at[:, pl.ds(HALO - REACH, REACH)]
            else:
                side = 0 if dg < 0 else 1
                if ds == 0:
                    source, target = stage.at[side], land.at[side, :, pl.ds(edge, half)]
                elif ds < 0:
                    source = stage.at[side, :, pl.ds(0, edge)]
                    target = land.at[side, :, pl.ds(edge + half, edge)]
                else:
                    source = stage.at[side, :, pl.ds(half - edge, edge)]
                    target = land.at[side, :, pl.ds(0, edge)]
            made.append((ds, dg, pltpu.make_async_remote_copy(
                src_ref=source, dst_ref=target, send_sem=send.at[at], recv_sem=recv.at[at ^ 1 if at < 4 else 11 - at],
                device_id=(si + ds, gi + dg), device_id_type=MESH)))
        return made

    def begin(made):
        for ds, dg, copy in made:
            @pl.when(inside(ds, dg))
            def _():
                copy.start()

    def finish_recv(made, recv):
        for at, (ds, dg) in enumerate(steps):
            back = made[at ^ 1 if at < 4 else 11 - at][2]

            @pl.when(inside(ds, dg))
            def _():
                back.wait_recv()

    def finish_send(made):
        for ds, dg, copy in made:
            @pl.when(inside(ds, dg))
            def _():
                copy.wait_send()

    def blank(dst_a, land):
        zero_a = jnp.zeros((dst_a.shape[0], HALO) + dst_a.shape[2:], jnp.float32)
        half, edge = X // 2, HALO // 2
        zero_l = jnp.zeros((land.shape[1], edge, 8, 128), jnp.float32)

        @pl.when(si == 0)
        def _():
            dst_a[:, pl.ds(0, HALO)] = zero_a
            for side in range(2):
                land[side, :, pl.ds(0, edge)] = zero_l

        @pl.when(si == ns - 1)
        def _():
            dst_a[:, pl.ds(HALO + X, HALO)] = zero_a
            for side in range(2):
                land[side, :, pl.ds(edge + half, edge)] = zero_l

        for side, edge_here in ((0, gi == ng - 1), (1, gi == 0)):
            @pl.when(edge_here)
            def _(side=side):
                land[side] = jnp.zeros(land.shape[1:], jnp.float32)

    def pack(stage, ch, pair, even, odd):
        stage[0, ch, pair] = jnp.where(upper, even, pltpu.roll(odd, 4, 0))
        stage[1, ch, pair] = jnp.where(upper, pltpu.roll(even, 4, 0), odd)

    def unpack(land, ch, pair):
        high, low = land[0, ch, pair], land[1, ch, pair]
        return (jnp.where(upper, high, pltpu.roll(low, 4, 0)),
                jnp.where(upper, pltpu.roll(high, 4, 0), low))

    def spread_rows(mask):
        wide = jnp.dot(mask.astype(jnp.float32), ez_ref[...], preferred_element_type=jnp.float32)
        return jnp.where(upper, jnp.broadcast_to(wide[0:1], (8, 128)), jnp.broadcast_to(wide[1:2], (8, 128)))

    for at in range(4):
        fetched[at].wait()
    for bx in range(X // 4):
        cut = 1.0 - CRACK_CUT * spread_rows(br_ref[bx])
        flag = spread_rows(fl_ref[bx])
        for at in range(4):
            x = bx * 4 + at
            w = k_ref[x] * cut
            e1a[6, HALO + x] = w
            carry[x] = flag * w

    def own(i, _):
        for c in range(3):
            tiles = []
            for o in range(2):
                x = 2 * i + o
                u = u_ref[c, x]
                f = f_ref[c, x]
                rhs = MASS_TERM * (2.0 * u - p_ref[c, x]) + f
                e1a[c, HALO + x] = u
                e1a[3 + c, HALO + x] = rhs
                e2a[c, HALO + x] = f
                tiles.append((u, rhs, f))
            pack(s1, c, i, tiles[0][0], tiles[1][0])
            pack(s1, 3 + c, i, tiles[0][1], tiles[1][1])
            pack(s2, c, i, tiles[0][2], tiles[1][2])
        pack(s1, 6, i, e1a[6, HALO + 2 * i], e1a[6, HALO + 2 * i + 1])
        return 0

    for at in range(4, 7):
        fetched[at].wait()
    lax.fori_loop(0, X // 2, own, 0)
    blank(e1a, h1)
    blank(e2a, h2)
    blank(e3a, h3)

    first = copies(e1a, e1a, s1, h1, send1, recv1)
    second = copies(e2a, e2a, s2, h2, send2, recv2)
    third = copies(rqa, e3a, s3, h3, send3, recv3)
    pl.semaphore_wait(barrier, count - 1)
    begin(first)
    finish_recv(first, recv1)
    begin(second)

    def open1(i, _):
        for ch in range(7):
            e1b[ch, 2 * i], e1b[ch, 2 * i + 1] = unpack(h1, ch, i)
        return 0

    lax.fori_loop(0, (X + 2 * HALO) // 2, open1, 0)

    def link(w, other):
        return jnp.where(jnp.minimum(w, other) > 0.0, 0.5 * (w + other), 0.0)

    not_last, not_first = lane < 127, lane > 0

    def coefficients(x, _):
        wa, wb = e1a[6, x], e1b[6, x]
        ya, yb = up_y(wa, wb)
        da, db = down_y(wa, wb)
        for w, wu, wd, yu, yd, dg, kc in (
            (wa, e1a[6, x + 1], e1a[6, x - 1], ya, da, dga, kca),
            (wb, e1b[6, x + 1], e1b[6, x - 1], yb, db, dgb, kcb),
        ):
            zu = jnp.where(not_last, up_z(w), 0.0)
            zd = jnp.where(not_first, down_z(w), 0.0)
            kc[0, x] = link(w, wu)
            kc[1, x] = link(w, yu)
            kc[2, x] = link(w, yd)
            kc[3, x] = link(w, zu)
            kc[4, x] = link(w, zd)
            sx = w + 0.5 * (wu + wd)
            sy = w + 0.5 * (yu + yd)
            sz = w + 0.5 * (zu + zd)
            every = MASS_TERM + SPRING_SHEAR * (sx + sy + sz)
            dg[0, x] = every + SHEAR_REST * sx
            dg[1, x] = every + SHEAR_REST * sy
            dg[2, x] = every + SHEAR_REST * sz
        return 0

    kca[0, HALO - REACH] = link(e1a[6, HALO - REACH], e1a[6, HALO - REACH + 1])
    kcb[0, HALO - REACH] = link(e1b[6, HALO - REACH], e1b[6, HALO - REACH + 1])
    lax.fori_loop(HALO - 2, HALO + X + 2, coefficients, 0)

    def operate(x, va, vb, base, both=True):
        result = []
        coef = [[kc[j, x] for j in range(5)] + [kc[0, x - 1]] for kc in (kca, kcb)]
        for c in range(3):
            a, b = va[base + c, x], vb[base + c, x]
            ua, ub = up_y(a, b)
            la, lb = down_y(a, b)
            pair = []
            halves = ((a, va, ua, la, coef[0], dga), (b, vb, ub, lb, coef[1], dgb))
            for v, ref, u, l, k, dg in halves if both else halves[:1]:
                parts = (
                    k[0] * ref[base + c, x + 1] + k[5] * ref[base + c, x - 1],
                    k[1] * u + k[2] * l,
                    k[3] * up_z(v) + k[4] * down_z(v),
                )
                every = parts[0] + parts[1] + parts[2]
                pair.append(dg[c, x] * v - (SPRING_SHEAR * every + SHEAR_REST * parts[c]))
            result.append(pair)
        return result

    def solve(step, va, vb, rhs_of):
        def residual(i, _):
            done = []
            for x in (2 * i, 2 * i + 1):
                image = operate(x, va, vb, 0)
                for c in range(3):
                    ra, rb = rhs_of(c, x)
                    done.append((c, x, ra - image[c][0], rb - image[c][1]))
            for c, x, ra, rb in done:
                rqa[c, x] = ra
                rqb[c, x] = rb
            return 0

        lax.fori_loop((HALO - 2) // 2, (HALO + X + 2) // 2, residual, 0)

        def put(x, image):
            for c in range(3):
                rqa[3 + c, x] = image[c][0]
                rqb[3 + c, x] = image[c][1]

        def apply(i, sums):
            rr, rq = sums
            at = (2 * i, 2 * i + 1)
            images = [operate(x, rqa, rqb, 0) for x in at]
            for x, image in zip(at, images):
                for c in range(3):
                    r = rqa[c, x]
                    rr, rq = rr + r * r, rq + r * image[c][0]
            for x, image in zip(at, images):
                put(x, image)
            return rr, rq

        zero = jnp.zeros((8, 128), jnp.float32)
        images = [operate(x, rqa, rqb, 0) for x in (HALO - 1, HALO + X)]
        put(HALO - 1, images[0])
        put(HALO + X, images[1])
        rr, rq = lax.fori_loop(HALO // 2, (HALO + X) // 2, apply, (zero, zero))
        rr, rq = total(rr), total(rq)
        mu = jnp.where(rr > 0.0, rq / jnp.where(rr > 0.0, rr, 1.0), 0.0)

        def centred(i, sums):
            ww, wr, mix, wt = sums
            for x in (2 * i, 2 * i + 1):
                image = operate(x, rqa, rqb, 3, False)
                for c in range(3):
                    r, q, s = rqa[c, x], rqa[3 + c, x], image[c][0]
                    w, t = q - mu * r, s - mu * q
                    ww, wr, mix, wt = ww + w * w, wr + w * r, mix + (r * t + w * q), wt + w * t
            return ww, wr, mix, wt

        sums = lax.fori_loop(HALO // 2, (HALO + X) // 2, centred, (zero,) * 4)
        ww, wr, mix, wt = [total(v) for v in sums]
        one = lax.broadcasted_iota(jnp.int32, (1, 128), 1)
        row = jnp.zeros((1, 128), jnp.float32)
        for at, value in enumerate((rr, rq, mu, ww, wr, mix, wt)):
            row = jnp.where(one == at, value, row)
        gath[step, me] = row

        def share(i, _):
            other = lax.rem(me + i, count)
            pltpu.make_async_remote_copy(
                src_ref=gath.at[step, me], dst_ref=gath.at[step, me], send_sem=asend.at[step], recv_sem=arecv.at[step],
                device_id=(other // ng, lax.rem(other, ng)), device_id_type=MESH).start()
            return 0

        lax.fori_loop(1, count, share, 0)

    def collect(step):
        block = gath.at[step, pl.ds(0, count - 1)]
        pltpu.make_async_copy(block, block, arecv.at[step]).wait()
        table = gath[step].reshape(count, 128)
        rr, rq, mu, ww, wr, mix, wt = [table[:, at:at + 1] for at in range(7)]

        def down(v):
            return jnp.sum(v, axis=0, keepdims=True)

        norm = down(rr)
        alpha = norm / down(rq)
        rest = 1.0 - alpha * mu
        after = down(alpha * alpha * ww - 2.0 * alpha * rest * wr + rest * rest * rr)
        curved = down(rest * rest * rq - alpha * rest * mix + alpha * alpha * wt)
        ratio = after / norm
        beta = after / (curved - ratio * after / alpha)
        return alpha + beta * (1.0 + ratio), -beta * alpha

    def drain(step):
        block = gath.at[step, pl.ds(0, count - 1)]
        pltpu.make_async_copy(block, block, asend.at[step]).wait()

    solve(0, e1a, e1b, lambda c, x: (e1a[3 + c, x], e1b[3 + c, x]))

    def pack3(i, _):
        for ch in range(6):
            pack(s3, ch, i, rqa[ch, HALO + 2 * i], rqa[ch, HALO + 2 * i + 1])
        return 0

    lax.fori_loop(0, X // 2, pack3, 0)
    begin(third)

    finish_recv(second, recv2)

    def open2(i, _):
        for ch in range(3):
            e2b[ch, 2 * i], e2b[ch, 2 * i + 1] = unpack(h2, ch, i)
        return 0

    lax.fori_loop(0, (X + 2 * HALO) // 2, open2, 0)
    finish_recv(third, recv3)
    c0, c1 = collect(0)

    def step_b(i, _):
        for c in range(3):
            r0, r1 = unpack(h3, c, i)
            q0, q1 = unpack(h3, 3 + c, i)
            u1b[c, 2 * i] = e1b[c, 2 * i] + (c0 * r0 + c1 * q0)
            u1b[c, 2 * i + 1] = e1b[c, 2 * i + 1] + (c0 * r1 + c1 * q1)
        return 0

    lax.fori_loop(0, (X + 2 * HALO) // 2, step_b, 0)

    def step_a(x, _):
        for c in range(3):
            u1a[c, x] = e1a[c, x] + (c0 * rqa[c, x] + c1 * rqa[3 + c, x])
        return 0

    lax.fori_loop(HALO, HALO + X, step_a, 0)
    for x in list(range(HALO - REACH, HALO)) + list(range(HALO + X, HALO + X + REACH)):
        for c in range(3):
            u1a[c, x] = e1a[c, x] + (c0 * e3a[c, x] + c1 * e3a[3 + c, x])
    finish_send(first)
    finish_send(second)
    finish_send(third)

    def rhs2(c, x):
        return (MASS_TERM * (2.0 * u1a[c, x] - e1a[c, x]) + e2a[c, x],
                MASS_TERM * (2.0 * u1b[c, x] - e1b[c, x]) + e2b[c, x])

    solve(1, u1a, u1b, rhs2)
    c0, c1 = collect(1)

    def step2(x, _):
        for c in range(3):
            va = u1a[c, x] + (c0 * rqa[c, x] + c1 * rqa[3 + c, x])
            vb = u1b[c, x] + (c0 * rqb[c, x] + c1 * rqb[3 + c, x])
            u1a[c, x] = va
            u1b[c, x] = vb
        return 0

    step2(HALO - 1, 0)
    step2(HALO + X, 0)

    def step2_own(i, _):
        for x in (2 * i, 2 * i + 1):
            step2(x, 0)
            for c in range(3):
                v = u1a[c, x]
                disp_ref[c, x - HALO] = v
                rows[c, pl.ds(x - HALO, 8, stride=X), :] = v
        return 0

    lax.fori_loop(HALO // 2, (HALO + X) // 2, step2_own, 0)
    zrows = coef_ref.shape[2]
    nt = (((1,), (1,)), ((), ()))

    def halves(v):
        high = v.astype(jnp.bfloat16)
        return high, (v - high.astype(jnp.float32)).astype(jnp.bfloat16)

    def transform(c, _):
        high, low = halves(rows[c])
        turned = lax.dot_general(cz_ref[:, 0:256], jnp.concatenate([high, low], axis=1), nt,
                                 preferred_element_type=jnp.float32)
        turned += lax.dot_general(cz_ref[:, 256:384], high, nt, preferred_element_type=jnp.float32)
        for j in range(ns):
            outb[j, c] = turned[j * zrows:(j + 1) * zrows]
        return 0

    def trade(part, i):
        to = lax.rem(si + i, ns)
        return pltpu.make_async_remote_copy(
            src_ref=outb.at[to, pl.ds(3 * part, 3)], dst_ref=inb.at[si, pl.ds(3 * part, 3)],
            send_sem=tsend.at[part, i], recv_sem=trecv.at[part, i],
            device_id=(to, gi), device_id_type=MESH)

    trades = [[trade(part, i) for i in range(1, ns)] for part in range(2)]

    def ship(part):
        lax.fori_loop(3 * part, 3 * part + 3, transform, 0)
        for copy in trades[part]:
            copy.start()
        for c in range(3 * part, 3 * part + 3):
            inb[si, c] = outb[si, c]

    fetched[7].wait()
    ship(0)

    def finals(i, _):
        for x in (2 * i, 2 * i + 1):
            at = x - HALO
            scale = SPRING_NORMAL * carry[at] * 0.5
            a1, a2, b1 = u1a[1, x], u1a[2, x], u1b[1, x]
            dx = u1a[0, x + 1] - u1a[0, x - 1]
            dy = up_y(a1, b1)[0] - down_y(a1, b1)[0]
            dz = jnp.where(not_last, up_z(a2), 0.0) - jnp.where(not_first, down_z(a2), 0.0)
            for c, d in enumerate((dx, dy, dz)):
                rows[3 + c, pl.ds(at, 8, stride=X), :] = scale * d
        return 0

    lax.fori_loop(HALO // 2, (HALO + X) // 2, finals, 0)
    ship(1)
    fetched[8].wait()

    zlane = lax.broadcasted_iota(jnp.int32, (zrows, 128), 1)
    c1t, c3t = float(np.sqrt(0.5) * np.cos(np.pi / 8)), float(np.sqrt(0.5) * np.cos(3 * np.pi / 8))

    def gather_back(c, _):
        pieces = [inb[j, c] for j in range(ns)]
        gap = ns // 2
        while gap:
            keep = (zlane // (X * gap)) % 2 == 0
            mixed = list(pieces)
            for j in range(ns):
                if (j // gap) % 2 == 0:
                    a, b = pieces[j], pieces[j + gap]
                    mixed[j] = jnp.where(keep, a, pltpu.roll(b, X * gap, 1))
                    mixed[j + gap] = jnp.where(keep, pltpu.roll(a, 128 - X * gap, 1), b)
            pieces = mixed
            gap //= 2
        coded = []
        for b in range(Y // 4):
            v0, v1, v2, v3 = pieces[4 * b:4 * b + 4]
            s03, s12, d03, d12 = v0 + v3, v1 + v2, v0 - v3, v1 - v2
            coded += [0.5 * (s03 + s12), c1t * d03 + c3t * d12, 0.5 * (s03 - s12), c3t * d03 - c1t * d12]
        high, low = halves(jnp.concatenate(coded, axis=0))
        done = jnp.dot(jnp.concatenate([high, low], axis=1), gt_ref[...], preferred_element_type=jnp.float32)
        coef_ref[c] = (done[:, 0:128] + done[:, 128:256]).reshape(Y, zrows, 128)
        return 0

    for part in range(2):
        for copy in trades[part]:
            copy.wait_recv()
        lax.fori_loop(3 * part, 3 * part + 3, gather_back, 0)
    drain(0)
    drain(1)
    for part in range(2):
        for copy in trades[part]:
            copy.wait_send()


def fused(mesh, u_now, u_prev, force, stiffness, broken, flags):
    ns, ng = mesh.shape["slab"], mesh.shape["grp"]
    _, X, Y, Z = u_now.shape
    xe, pairs, half = X + 2 * HALO, X // 2 + HALO, X // 2
    zrows = Z // ns
    ez = jnp.asarray(np.kron(np.eye(Z // 4), np.ones((1, 4))), jnp.float32)
    czh, czl = split_table(np.kron(np.eye(Z // 4), cosine_table()))
    cz = jnp.asarray(np.concatenate([czh, czh, czl], axis=1), jnp.bfloat16)
    gth, gtl = split_table(wavelet_table(X * ns).T)
    gt = jnp.asarray(np.block([[gth, gtl], [gth, np.zeros_like(gtl)]]), jnp.bfloat16)

    def vm(*shape):
        return pltpu.VMEM(shape, jnp.float32)

    def ext(n):
        return vm(n, xe, Y, Z)

    def stage(n):
        return vm(2, n, half, Y, Z)

    def land(n):
        return vm(2, n, pairs, Y, Z)

    dma = pltpu.SemaphoreType.DMA
    return pl.pallas_call(
        lambda *refs: kernel(ns, ng, *refs),
        name="lattice",
        out_shape=(jax.ShapeDtypeStruct(u_now.shape, jnp.float32),
                   jax.ShapeDtypeStruct((6, Y, zrows, X * ns), jnp.float32)),
        in_specs=[pl.BlockSpec(memory_space=pltpu.MemorySpace.HBM)] * 9,
        out_specs=(pl.BlockSpec(memory_space=pltpu.VMEM),) * 2,
        scratch_shapes=[
            vm(*u_now.shape), vm(*u_now.shape), vm(*u_now.shape), vm(*stiffness.shape),
            pltpu.VMEM(broken.shape, broken.dtype), pltpu.VMEM(flags.shape, flags.dtype),
            vm(*ez.shape), pltpu.VMEM(cz.shape, cz.dtype), pltpu.VMEM(gt.shape, gt.dtype), pltpu.SemaphoreType.DMA((9,)),
            ext(7), ext(7), stage(7), land(7),
            ext(3), ext(3), stage(3), land(3),
            ext(6), ext(6), ext(6), stage(6), land(6),
            ext(3), ext(3), vm(X, Y, Z), ext(3), ext(3), ext(5), ext(5),
            vm(2, ns * ng, 1, 128), vm(6, Y * X, Z), vm(ns, 6, zrows, 128), vm(ns, 6, zrows, 128),
            dma((8,)), dma((8,)), dma((8,)), dma((8,)), dma((8,)), dma((8,)),
            dma((2,)), dma((2,)), dma((2, ns)), dma((2, ns)),
        ],
        compiler_params=pltpu.CompilerParams(collective_id=0, has_side_effects=True, vmem_limit_bytes=48 << 20),
    )(u_now, u_prev, force, stiffness, broken, flags, ez, cz, gt)


def fits(mesh, shape):
    ns, ng = mesh.shape["slab"], mesh.shape["grp"]
    x, y, z = shape[1] // ns, shape[2] // ng, shape[3]
    return y == 8 and z == 128 and x * y == 128 and x * ns == 128 and z % (8 * ns) == 0


def entry(mesh, *args):
    ns, ng = mesh.shape["slab"], mesh.shape["grp"]
    _, x, y, z = args[0].shape
    if fits(mesh, (3, x * ns, y * ng, z)):
        return fused(mesh, *args)
    return body(*args)


def solution(mesh):
    return jax.shard_map(
        lambda *args: entry(mesh, *args),
        mesh=mesh,
        in_specs=(
            P(None, "slab", "grp", None),
            P(None, "slab", "grp", None),
            P(None, "slab", "grp", None),
            P("slab", "grp", None),
            P("slab", "grp", None),
            P("slab", "grp", None),
        ),
        out_specs=(P(None, "slab", "grp", None), P(None, "grp", "slab", None)),
        check_vma=False,
    )
```

```python
import jax
import jax.numpy as jnp
import numpy as np
from jax import lax
from jax.experimental import pallas as pl
from jax.experimental.pallas import tpu as pltpu
from jax.sharding import PartitionSpec as P

STEPS = 2
ITERS = 2
LEVELS = 3


SPRING_NORMAL = 1.0
SPRING_SHEAR = 0.4
MASS_TERM = 1.0
CRACK_CUT = 0.9


def with_halo(block, sides, width):
    for axis, dim in sides:
        count = lax.axis_size(axis)
        forward = [(i, i + 1) for i in range(count - 1)]
        backward = [(target, source) for source, target in forward]
        low = lax.ppermute(
            lax.slice_in_dim(block, block.shape[dim] - width, None, axis=dim), axis, forward
        )
        high = lax.ppermute(lax.slice_in_dim(block, 0, width, axis=dim), axis, backward)
        block = jnp.concatenate([low, block, high], axis=dim)
    return block


def cosine_table():
    freq = np.arange(4)[:, None]
    place = np.arange(4)[None, :]
    factor = np.where(freq == 0, 0.5, np.sqrt(0.5))
    return factor * np.cos(np.pi * (2 * place + 1) * freq / 8.0)


def block_table(count):
    return jnp.asarray(np.kron(np.eye(count // 4), cosine_table()), jnp.float32)


def spread(mask):
    values = mask.astype(jnp.float32)
    size_a, size_b, size_c = values.shape
    wide = jnp.broadcast_to(values[:, None, :, None, :, None], (size_a, 4, size_b, 4, size_c, 4))
    return wide.reshape(size_a * 4, size_b * 4, size_c * 4)


def sides(padded, axis_index):
    leading = padded.ndim - 3

    def cut(offset):
        index_list = [slice(None)] * leading + [slice(1, -1)] * 3
        length = padded.shape[leading + axis_index]
        index_list[leading + axis_index] = slice(1 + offset, length - 1 + offset)
        return padded[tuple(index_list)]

    return (cut(1), cut(-1))


def springs(field, weight, field_pad, weight_pad):
    result = MASS_TERM * field
    for axis_index in range(3):
        upper_v, lower_v = sides(field_pad, axis_index)
        upper_w, lower_w = sides(weight_pad, axis_index)
        k_upper = 0.5 * (weight + upper_w)
        k_lower = 0.5 * (weight + lower_w)
        change = k_upper * (field - upper_v) + k_lower * (field - lower_v)
        coupling = jnp.array(
            [SPRING_NORMAL if comp == axis_index else SPRING_SHEAR for comp in range(3)],
            jnp.float32,
        ).reshape(3, 1, 1, 1)
        result = result + coupling * change
    return result


def faces(field):
    padded = with_halo(field, (("slab", 1), ("grp", 2)), 1)
    return jnp.pad(padded, ((0, 0), (0, 0), (0, 0), (1, 1)))


def stresses(carry, field_pad):
    rows_out = []
    for axis_index in range(3):
        upper_v, lower_v = sides(field_pad, axis_index)
        rows_out.append(SPRING_NORMAL * carry * 0.5 * (upper_v[axis_index] - lower_v[axis_index]))
    return jnp.stack(rows_out)


def paired_sum(residual, image):
    return lax.psum((jnp.sum(residual * residual), jnp.sum(residual * image)), ("slab", "grp"))


def lift(signal):
    even = signal[..., 0::2]
    odd = signal[..., 1::2]
    detail = odd - 0.5 * (even + jnp.roll(even, -1, axis=-1))
    approx = even + 0.25 * (jnp.roll(detail, 1, axis=-1) + detail)
    return (approx, detail)


def wavelet(signal):
    pieces = []
    approx = signal
    for level_index in range(LEVELS):
        approx, detail = lift(approx)
        pieces.insert(0, detail)
    return jnp.concatenate([approx] + pieces, axis=-1)


def body(u_now, u_prev, force, stiffness, broken, flags):
    weight = stiffness * (1.0 - CRACK_CUT * spread(broken))
    carry = spread(flags) * weight
    weight_pad = with_halo(weight, (("slab", 0), ("grp", 1)), 1)
    weight_pad = jnp.pad(weight_pad, ((0, 0), (0, 0), (1, 1)))

    def operate(field):
        return springs(field, weight, faces(field), weight_pad)

    for step_index in range(STEPS):
        rhs = MASS_TERM * (2.0 * u_now - u_prev) + force
        guess = u_now
        residual = rhs - operate(guess)
        image = operate(residual)
        norm_now, product = paired_sum(residual, image)
        alpha = norm_now / product
        direction, along = (residual, image)
        for turn_index in range(ITERS):
            guess = guess + alpha * direction
            residual = residual - alpha * along
            if turn_index + 1 < ITERS:
                image = operate(residual)
                norm_next, product = paired_sum(residual, image)
                ratio = norm_next / norm_now
                alpha = norm_next / (product - ratio * norm_next / alpha)
                direction = residual + ratio * direction
                along = image + ratio * along
                norm_now = norm_next
        u_prev = u_now
        u_now = guess
    stress = stresses(carry, faces(u_now))
    fields = jnp.concatenate([u_now, stress], axis=0)
    table_x = block_table(fields.shape[1])
    table_y = block_table(fields.shape[2])
    table_z = block_table(fields.shape[3])
    blockc = jnp.einsum("ax,hxyz->hayz", table_x, fields, precision=lax.Precision.HIGHEST)
    blockc = jnp.einsum("by,hxyz->hxbz", table_y, blockc, precision=lax.Precision.HIGHEST)
    blockc = jnp.einsum("hxyz,cz->hxyc", blockc, table_z, precision=lax.Precision.HIGHEST)
    moved = jnp.transpose(blockc, (0, 2, 3, 1))
    shipped = lax.all_to_all(moved, "slab", split_axis=2, concat_axis=3, tiled=True)
    coeffs = wavelet(shipped)
    return (u_now, coeffs)


MESH = pl.DeviceIdType.MESH
HALO = 4
REACH = 3
SHEAR_REST = SPRING_NORMAL - SPRING_SHEAR


def wavelet_table(count):
    table = np.kron(np.eye(count // 4), cosine_table())
    pieces = []
    approx = table
    for level_index in range(LEVELS):
        even, odd = approx[0::2], approx[1::2]
        detail = odd - 0.5 * (even + np.roll(even, -1, axis=0))
        approx = even + 0.25 * (np.roll(detail, 1, axis=0) + detail)
        pieces.insert(0, detail)
    return np.concatenate([approx] + pieces, axis=0)


def split_table(table):
    high = table.astype(jnp.bfloat16).astype(np.float64)
    return high, (table - high).astype(jnp.bfloat16).astype(np.float64)


def sub_index():
    return lax.broadcasted_iota(jnp.int32, (8, 128), 0)


def lane_index():
    return lax.broadcasted_iota(jnp.int32, (8, 128), 1)


def up_y(a, b):
    ra, rb = pltpu.roll(a, 7, 0), pltpu.roll(b, 7, 0)
    last = sub_index() == 7
    return jnp.where(last, rb, ra), jnp.where(last, ra, rb)


def down_y(a, b):
    ra, rb = pltpu.roll(a, 1, 0), pltpu.roll(b, 1, 0)
    first = sub_index() == 0
    return jnp.where(first, rb, ra), jnp.where(first, ra, rb)


def up_z(v):
    return pltpu.roll(v, 127, 1)


def down_z(v):
    return pltpu.roll(v, 1, 1)


def total(v):
    return jnp.sum(jnp.sum(v, axis=0, keepdims=True), axis=1, keepdims=True)


def kernel(ns, ng, u_in, p_in, f_in, k_in, br_in, fl_in, ez_in, cz_in, gt_in,
           disp_out, coef_out,
           disp_ref, coef_ref, osem, u_ref, p_ref, f_ref, k_ref, br_ref, fl_ref, ez_ref, cz_ref, gt_ref, isem,
           e1a, e1b, s1, h1, e2a, e2b, s2, h2, rqa, rqb, e3a, s3, h3,
           u1a, u1b, carry, dga, dgb, kca, kcb, gath, rows, outb, inb,
           send0, recv0, send1, recv1, send2, recv2, send3, recv3, asend, arecv, tsend, trecv):
    X, Y = u_ref.shape[1], u_ref.shape[2]
    si, gi = lax.axis_index("slab"), lax.axis_index("grp")
    me = si * ng + gi
    count = ns * ng
    fetched = []
    for at, (source, target) in enumerate((
        (br_in, br_ref), (fl_in, fl_ref), (ez_in, ez_ref), (k_in, k_ref), (u_in, u_ref), (p_in, p_ref),
        (f_in, f_ref), (cz_in, cz_ref), (gt_in, gt_ref),
    )):
        fetch = pltpu.make_async_copy(source, target, isem.at[at])
        fetch.start()
        fetched.append(fetch)
    barrier = pltpu.get_barrier_semaphore()

    def greet(i, _):
        other = lax.rem(me + i, count)
        pl.semaphore_signal(barrier, inc=1, device_id=(other // ng, lax.rem(other, ng)), device_id_type=MESH)
        return 0

    lax.fori_loop(1, count, greet, 0)

    sub, lane = sub_index(), lane_index()
    upper = sub < 4

    steps = [(-1, 0), (1, 0), (0, -1), (0, 1), (-1, -1), (-1, 1), (1, -1), (1, 1)]

    def inside(ds, dg):
        ok = None
        if ds:
            ok = (si >= 1) if ds < 0 else (si <= ns - 2)
        if dg:
            more = (gi >= 1) if dg < 0 else (gi <= ng - 2)
            ok = more if ok is None else jnp.logical_and(ok, more)
        return ok

    def copies(ea, dst_a, stage, land, send, recv, low=0, high=None):
        half = X // 2
        edge = HALO // 2
        made = []
        chans = pl.ds(low, (ea.shape[0] if high is None else high) - low)
        for at, (ds, dg) in enumerate(steps):
            if dg == 0:
                if ds < 0:
                    source = ea.at[chans, pl.ds(HALO, REACH)]
                    target = dst_a.at[chans, pl.ds(HALO + X, REACH)]
                else:
                    source = ea.at[chans, pl.ds(HALO + X - REACH, REACH)]
                    target = dst_a.at[chans, pl.ds(HALO - REACH, REACH)]
            else:
                side = 0 if dg < 0 else 1
                if ds == 0:
                    source, target = stage.at[side, chans], land.at[side, chans, pl.ds(edge, half)]
                elif ds < 0:
                    source = stage.at[side, chans, pl.ds(0, 1)]
                    target = land.at[side, chans, pl.ds(edge + half, 1)]
                else:
                    source = stage.at[side, chans, pl.ds(half - 1, 1)]
                    target = land.at[side, chans, pl.ds(edge - 1, 1)]
            made.append((ds, dg, pltpu.make_async_remote_copy(
                src_ref=source, dst_ref=target, send_sem=send.at[at], recv_sem=recv.at[at ^ 1 if at < 4 else 11 - at],
                device_id=(si + ds, gi + dg), device_id_type=MESH)))
        return made

    def begin(made):
        for ds, dg, copy in made:
            @pl.when(inside(ds, dg))
            def _():
                copy.start()

    def finish_recv(made, recv):
        for at, (ds, dg) in enumerate(steps):
            back = made[at ^ 1 if at < 4 else 11 - at][2]

            @pl.when(inside(ds, dg))
            def _():
                back.wait_recv()

    def finish_send(made):
        for ds, dg, copy in made:
            @pl.when(inside(ds, dg))
            def _():
                copy.wait_send()

    def blank(dst_a, land):
        zero_a = jnp.zeros((dst_a.shape[0], HALO) + dst_a.shape[2:], jnp.float32)
        half, edge = X // 2, HALO // 2
        zero_l = jnp.zeros((land.shape[1], edge, 8, 128), jnp.float32)

        @pl.when(si == 0)
        def _():
            dst_a[:, pl.ds(0, HALO)] = zero_a
            for side in range(2):
                land[side, :, pl.ds(0, edge)] = zero_l

        @pl.when(si == ns - 1)
        def _():
            dst_a[:, pl.ds(HALO + X, HALO)] = zero_a
            for side in range(2):
                land[side, :, pl.ds(edge + half, edge)] = zero_l

        for side, edge_here in ((0, gi == ng - 1), (1, gi == 0)):
            @pl.when(edge_here)
            def _(side=side):
                land[side] = jnp.zeros(land.shape[1:], jnp.float32)

    def pack(stage, ch, pair, even, odd):
        stage[0, ch, pair] = jnp.where(upper, even, pltpu.roll(odd, 4, 0))
        stage[1, ch, pair] = jnp.where(upper, pltpu.roll(even, 4, 0), odd)

    def unpack(land, ch, pair):
        high, low = land[0, ch, pair], land[1, ch, pair]
        return (jnp.where(upper, high, pltpu.roll(low, 4, 0)),
                jnp.where(upper, pltpu.roll(high, 4, 0), low))

    def spread_rows(mask):
        wide = jnp.dot(mask.astype(jnp.float32), ez_ref[...], preferred_element_type=jnp.float32)
        return jnp.where(upper, jnp.broadcast_to(wide[0:1], (8, 128)), jnp.broadcast_to(wide[1:2], (8, 128)))

    for at in range(4):
        fetched[at].wait()
    for bx in range(X // 4):
        cut = 1.0 - CRACK_CUT * spread_rows(br_ref[bx])
        flag = spread_rows(fl_ref[bx])
        for at in range(4):
            x = bx * 4 + at
            w = k_ref[x] * cut
            e1a[6, HALO + x] = w
            carry[x] = flag * w

    def own(i, _):
        for c in range(3):
            tiles = []
            for o in range(2):
                x = 2 * i + o
                u = u_ref[c, x]
                f = f_ref[c, x]
                rhs = MASS_TERM * (2.0 * u - p_ref[c, x]) + f
                e1a[c, HALO + x] = u
                e1a[3 + c, HALO + x] = rhs
                e2a[c, HALO + x] = f
                tiles.append((u, rhs, f))
            pack(s1, c, i, tiles[0][0], tiles[1][0])
            pack(s1, 3 + c, i, tiles[0][1], tiles[1][1])
            pack(s2, c, i, tiles[0][2], tiles[1][2])
        pack(s1, 6, i, e1a[6, HALO + 2 * i], e1a[6, HALO + 2 * i + 1])
        return 0

    for at in range(4, 7):
        fetched[at].wait()
    lax.fori_loop(0, X // 2, own, 0)
    blank(e1a, h1)
    blank(e2a, h2)
    blank(e3a, h3)

    zeroth = copies(e1a, e1a, s1, h1, send0, recv0, 6, 7)
    first = copies(e1a, e1a, s1, h1, send1, recv1, 0, 6)
    second = copies(e2a, e2a, s2, h2, send2, recv2)
    third = copies(rqa, e3a, s3, h3, send3, recv3)
    pl.semaphore_wait(barrier, count - 1)
    begin(zeroth)
    begin(first)
    finish_recv(zeroth, recv0)

    def open0(i, _):
        e1b[6, 2 * i], e1b[6, 2 * i + 1] = unpack(h1, 6, i)
        return 0

    def open1(i, _):
        for ch in range(6):
            e1b[ch, 2 * i], e1b[ch, 2 * i + 1] = unpack(h1, ch, i)
        return 0

    lax.fori_loop(0, (X + 2 * HALO) // 2, open0, 0)

    def link(w, other):
        return jnp.where(jnp.minimum(w, other) > 0.0, 0.5 * (w + other), 0.0)

    not_last, not_first = lane < 127, lane > 0

    def coefficients(x, _):
        wa, wb = e1a[6, x], e1b[6, x]
        ya, yb = up_y(wa, wb)
        da, db = down_y(wa, wb)
        for w, wu, wd, yu, yd, dg, kc in (
            (wa, e1a[6, x + 1], e1a[6, x - 1], ya, da, dga, kca),
            (wb, e1b[6, x + 1], e1b[6, x - 1], yb, db, dgb, kcb),
        ):
            zu = jnp.where(not_last, up_z(w), 0.0)
            zd = jnp.where(not_first, down_z(w), 0.0)
            kc[0, x] = link(w, wu)
            kc[1, x] = link(w, yu)
            kc[2, x] = link(w, yd)
            kc[3, x] = link(w, zu)
            kc[4, x] = link(w, zd)
            sx = w + 0.5 * (wu + wd)
            sy = w + 0.5 * (yu + yd)
            sz = w + 0.5 * (zu + zd)
            every = MASS_TERM + SPRING_SHEAR * (sx + sy + sz)
            dg[0, x] = every + SHEAR_REST * sx
            dg[1, x] = every + SHEAR_REST * sy
            dg[2, x] = every + SHEAR_REST * sz
        return 0

    kca[0, HALO - REACH] = link(e1a[6, HALO - REACH], e1a[6, HALO - REACH + 1])
    kcb[0, HALO - REACH] = link(e1b[6, HALO - REACH], e1b[6, HALO - REACH + 1])
    lax.fori_loop(HALO - 2, HALO + X + 2, coefficients, 0)
    finish_recv(first, recv1)
    begin(second)
    lax.fori_loop(0, (X + 2 * HALO) // 2, open1, 0)

    def operate(x, va, vb, base, both=True):
        result = []
        coef = [[kc[j, x] for j in range(5)] + [kc[0, x - 1]] for kc in (kca, kcb)]
        for c in range(3):
            a, b = va[base + c, x], vb[base + c, x]
            ua, ub = up_y(a, b)
            la, lb = down_y(a, b)
            pair = []
            halves = ((a, va, ua, la, coef[0], dga), (b, vb, ub, lb, coef[1], dgb))
            for v, ref, u, l, k, dg in halves if both else halves[:1]:
                parts = (
                    k[0] * ref[base + c, x + 1] + k[5] * ref[base + c, x - 1],
                    k[1] * u + k[2] * l,
                    k[3] * up_z(v) + k[4] * down_z(v),
                )
                every = parts[0] + parts[1] + parts[2]
                pair.append(dg[c, x] * v - (SPRING_SHEAR * every + SHEAR_REST * parts[c]))
            result.append(pair)
        return result

    def solve(step, va, vb, rhs_of):
        def residual(i, _):
            done = []
            for x in (2 * i, 2 * i + 1):
                image = operate(x, va, vb, 0)
                for c in range(3):
                    ra, rb = rhs_of(c, x)
                    done.append((c, x, ra - image[c][0], rb - image[c][1]))
            for c, x, ra, rb in done:
                rqa[c, x] = ra
                rqb[c, x] = rb
            return 0

        lax.fori_loop((HALO - 2) // 2, (HALO + X + 2) // 2, residual, 0)

        def put(x, image):
            for c in range(3):
                rqa[3 + c, x] = image[c][0]
                rqb[3 + c, x] = image[c][1]

        def apply(i, sums):
            rr, rq = sums
            at = (2 * i, 2 * i + 1)
            images = [operate(x, rqa, rqb, 0) for x in at]
            for x, image in zip(at, images):
                for c in range(3):
                    r = rqa[c, x]
                    rr, rq = rr + r * r, rq + r * image[c][0]
            for x, image in zip(at, images):
                put(x, image)
            return rr, rq

        zero = jnp.zeros((8, 128), jnp.float32)
        images = [operate(x, rqa, rqb, 0) for x in (HALO - 1, HALO + X)]
        put(HALO - 1, images[0])
        put(HALO + X, images[1])
        rr, rq = lax.fori_loop(HALO // 2, (HALO + X) // 2, apply, (zero, zero))
        rr, rq = total(rr), total(rq)
        mu = jnp.where(rr > 0.0, rq / jnp.where(rr > 0.0, rr, 1.0), 0.0)

        def centred(i, sums):
            ww, wr, mix, wt = sums
            for x in (2 * i, 2 * i + 1):
                image = operate(x, rqa, rqb, 3, False)
                for c in range(3):
                    r, q, s = rqa[c, x], rqa[3 + c, x], image[c][0]
                    w, t = q - mu * r, s - mu * q
                    ww, wr, mix, wt = ww + w * w, wr + w * r, mix + (r * t + w * q), wt + w * t
            return ww, wr, mix, wt

        sums = lax.fori_loop(HALO // 2, (HALO + X) // 2, centred, (zero,) * 4)
        ww, wr, mix, wt = [total(v) for v in sums]
        one = lax.broadcasted_iota(jnp.int32, (1, 128), 1)
        row = jnp.zeros((1, 128), jnp.float32)
        for at, value in enumerate((rr, rq, mu, ww, wr, mix, wt)):
            row = jnp.where(one == at, value, row)
        gath[step, me] = row

        def share(i, _):
            other = lax.rem(me + i, count)
            pltpu.make_async_remote_copy(
                src_ref=gath.at[step, me], dst_ref=gath.at[step, me], send_sem=asend.at[step], recv_sem=arecv.at[step],
                device_id=(other // ng, lax.rem(other, ng)), device_id_type=MESH).start()
            return 0

        lax.fori_loop(1, count, share, 0)

    def collect(step):
        block = gath.at[step, pl.ds(0, count - 1)]
        pltpu.make_async_copy(block, block, arecv.at[step]).wait()
        table = gath[step].reshape(count, 128)
        rr, rq, mu, ww, wr, mix, wt = [table[:, at:at + 1] for at in range(7)]

        def down(v):
            return jnp.sum(v, axis=0, keepdims=True)

        norm = down(rr)
        alpha = norm / down(rq)
        rest = 1.0 - alpha * mu
        after = down(alpha * alpha * ww - 2.0 * alpha * rest * wr + rest * rest * rr)
        curved = down(rest * rest * rq - alpha * rest * mix + alpha * alpha * wt)
        ratio = after / norm
        beta = after / (curved - ratio * after / alpha)
        return alpha + beta * (1.0 + ratio), -beta * alpha

    def drain(step):
        block = gath.at[step, pl.ds(0, count - 1)]
        pltpu.make_async_copy(block, block, asend.at[step]).wait()

    solve(0, e1a, e1b, lambda c, x: (e1a[3 + c, x], e1b[3 + c, x]))

    def pack3(i, _):
        for ch in range(6):
            pack(s3, ch, i, rqa[ch, HALO + 2 * i], rqa[ch, HALO + 2 * i + 1])
        return 0

    lax.fori_loop(0, X // 2, pack3, 0)
    begin(third)

    finish_recv(second, recv2)

    def open2(i, _):
        for ch in range(3):
            e2b[ch, 2 * i], e2b[ch, 2 * i + 1] = unpack(h2, ch, i)
        return 0

    lax.fori_loop(0, (X + 2 * HALO) // 2, open2, 0)
    finish_recv(third, recv3)
    c0, c1 = collect(0)

    def step_b(i, _):
        for c in range(3):
            r0, r1 = unpack(h3, c, i)
            q0, q1 = unpack(h3, 3 + c, i)
            u1b[c, 2 * i] = e1b[c, 2 * i] + (c0 * r0 + c1 * q0)
            u1b[c, 2 * i + 1] = e1b[c, 2 * i + 1] + (c0 * r1 + c1 * q1)
        return 0

    lax.fori_loop(0, (X + 2 * HALO) // 2, step_b, 0)

    def step_a(x, _):
        for c in range(3):
            u1a[c, x] = e1a[c, x] + (c0 * rqa[c, x] + c1 * rqa[3 + c, x])
        return 0

    lax.fori_loop(HALO, HALO + X, step_a, 0)
    for x in list(range(HALO - REACH, HALO)) + list(range(HALO + X, HALO + X + REACH)):
        for c in range(3):
            u1a[c, x] = e1a[c, x] + (c0 * e3a[c, x] + c1 * e3a[3 + c, x])
    finish_send(zeroth)
    finish_send(first)
    finish_send(second)
    finish_send(third)

    def rhs2(c, x):
        return (MASS_TERM * (2.0 * u1a[c, x] - e1a[c, x]) + e2a[c, x],
                MASS_TERM * (2.0 * u1b[c, x] - e1b[c, x]) + e2b[c, x])

    solve(1, u1a, u1b, rhs2)
    c0, c1 = collect(1)

    def step2(x, _):
        for c in range(3):
            va = u1a[c, x] + (c0 * rqa[c, x] + c1 * rqa[3 + c, x])
            vb = u1b[c, x] + (c0 * rqb[c, x] + c1 * rqb[3 + c, x])
            u1a[c, x] = va
            u1b[c, x] = vb
        return 0

    step2(HALO - 1, 0)
    step2(HALO + X, 0)

    def step2_own(i, _):
        for x in (2 * i, 2 * i + 1):
            step2(x, 0)
            for c in range(3):
                v = u1a[c, x]
                disp_ref[c, x - HALO] = v
                rows[c, pl.ds(x - HALO, 8, stride=X), :] = v
        return 0

    lax.fori_loop(HALO // 2, (HALO + X) // 2, step2_own, 0)
    outputs = [pltpu.make_async_copy(disp_ref, disp_out, osem.at[6])]
    outputs += [pltpu.make_async_copy(coef_ref.at[c], coef_out.at[c], osem.at[c]) for c in range(6)]
    zrows = coef_ref.shape[2]
    nt = (((1,), (1,)), ((), ()))

    def halves(v):
        high = v.astype(jnp.bfloat16)
        return high, (v - high.astype(jnp.float32)).astype(jnp.bfloat16)

    def transform(c, _):
        high, low = halves(rows[c])
        turned = lax.dot_general(cz_ref[:, 0:256], jnp.concatenate([high, low], axis=1), nt,
                                 preferred_element_type=jnp.float32)
        turned += lax.dot_general(cz_ref[:, 256:384], high, nt, preferred_element_type=jnp.float32)
        for j in range(ns):
            outb[j, c] = turned[j * zrows:(j + 1) * zrows]
        return 0

    def trade(part, i):
        to = lax.rem(si + i, ns)
        return pltpu.make_async_remote_copy(
            src_ref=outb.at[to, pl.ds(3 * part, 3)], dst_ref=inb.at[si, pl.ds(3 * part, 3)],
            send_sem=tsend.at[part, i], recv_sem=trecv.at[part, i],
            device_id=(to, gi), device_id_type=MESH)

    trades = [[trade(part, i) for i in range(1, ns)] for part in range(2)]

    def ship(part):
        lax.fori_loop(3 * part, 3 * part + 3, transform, 0)
        for copy in trades[part]:
            copy.start()
        for c in range(3 * part, 3 * part + 3):
            inb[si, c] = outb[si, c]

    fetched[7].wait()
    ship(0)
    outputs[0].start()

    def finals(i, _):
        for x in (2 * i, 2 * i + 1):
            at = x - HALO
            scale = SPRING_NORMAL * carry[at] * 0.5
            a1, a2, b1 = u1a[1, x], u1a[2, x], u1b[1, x]
            dx = u1a[0, x + 1] - u1a[0, x - 1]
            dy = up_y(a1, b1)[0] - down_y(a1, b1)[0]
            dz = jnp.where(not_last, up_z(a2), 0.0) - jnp.where(not_first, down_z(a2), 0.0)
            for c, d in enumerate((dx, dy, dz)):
                rows[3 + c, pl.ds(at, 8, stride=X), :] = scale * d
        return 0

    lax.fori_loop(HALO // 2, (HALO + X) // 2, finals, 0)
    ship(1)
    fetched[8].wait()

    zlane = lax.broadcasted_iota(jnp.int32, (zrows, 128), 1)
    c1t, c3t = float(np.sqrt(0.5) * np.cos(np.pi / 8)), float(np.sqrt(0.5) * np.cos(3 * np.pi / 8))

    def gather_back(c, _):
        pieces = [inb[j, c] for j in range(ns)]
        gap = ns // 2
        while gap:
            keep = (zlane // (X * gap)) % 2 == 0
            mixed = list(pieces)
            for j in range(ns):
                if (j // gap) % 2 == 0:
                    a, b = pieces[j], pieces[j + gap]
                    mixed[j] = jnp.where(keep, a, pltpu.roll(b, X * gap, 1))
                    mixed[j + gap] = jnp.where(keep, pltpu.roll(a, 128 - X * gap, 1), b)
            pieces = mixed
            gap //= 2
        coded = []
        for b in range(Y // 4):
            v0, v1, v2, v3 = pieces[4 * b:4 * b + 4]
            s03, s12, d03, d12 = v0 + v3, v1 + v2, v0 - v3, v1 - v2
            coded += [0.5 * (s03 + s12), c1t * d03 + c3t * d12, 0.5 * (s03 - s12), c3t * d03 - c1t * d12]
        high, low = halves(jnp.concatenate(coded, axis=0))
        done = jnp.dot(jnp.concatenate([high, low], axis=1), gt_ref[...], preferred_element_type=jnp.float32)
        coef_ref[c] = (done[:, 0:128] + done[:, 128:256]).reshape(Y, zrows, 128)
        return 0

    for part in range(2):
        for copy in trades[part]:
            copy.wait_recv()
        for c in range(3 * part, 3 * part + 3):
            gather_back(c, 0)
            outputs[1 + c].start()
    drain(0)
    drain(1)
    for part in range(2):
        for copy in trades[part]:
            copy.wait_send()
    for copy in outputs:
        copy.wait()


def fused(mesh, u_now, u_prev, force, stiffness, broken, flags):
    ns, ng = mesh.shape["slab"], mesh.shape["grp"]
    _, X, Y, Z = u_now.shape
    xe, pairs, half = X + 2 * HALO, X // 2 + HALO, X // 2
    zrows = Z // ns
    ez = jnp.asarray(np.kron(np.eye(Z // 4), np.ones((1, 4))), jnp.float32)
    czh, czl = split_table(np.kron(np.eye(Z // 4), cosine_table()))
    cz = jnp.asarray(np.concatenate([czh, czh, czl], axis=1), jnp.bfloat16)
    gth, gtl = split_table(wavelet_table(X * ns).T)
    gt = jnp.asarray(np.block([[gth, gtl], [gth, np.zeros_like(gtl)]]), jnp.bfloat16)

    def vm(*shape):
        return pltpu.VMEM(shape, jnp.float32)

    def ext(n):
        return vm(n, xe, Y, Z)

    def stage(n):
        return vm(2, n, half, Y, Z)

    def land(n):
        return vm(2, n, pairs, Y, Z)

    dma = pltpu.SemaphoreType.DMA
    return pl.pallas_call(
        lambda *refs: kernel(ns, ng, *refs),
        name="lattice",
        out_shape=(jax.ShapeDtypeStruct(u_now.shape, jnp.float32),
                   jax.ShapeDtypeStruct((6, Y, zrows, X * ns), jnp.float32)),
        in_specs=[pl.BlockSpec(memory_space=pltpu.MemorySpace.HBM)] * 9,
        out_specs=(pl.BlockSpec(memory_space=pltpu.MemorySpace.HBM),) * 2,
        scratch_shapes=[
            vm(*u_now.shape), vm(6, Y, zrows, X * ns), pltpu.SemaphoreType.DMA((7,)),
            vm(*u_now.shape), vm(*u_now.shape), vm(*u_now.shape), vm(*stiffness.shape),
            pltpu.VMEM(broken.shape, broken.dtype), pltpu.VMEM(flags.shape, flags.dtype),
            vm(*ez.shape), pltpu.VMEM(cz.shape, cz.dtype), pltpu.VMEM(gt.shape, gt.dtype), pltpu.SemaphoreType.DMA((9,)),
            ext(7), ext(7), stage(7), land(7),
            ext(3), ext(3), stage(3), land(3),
            ext(6), ext(6), ext(6), stage(6), land(6),
            ext(3), ext(3), vm(X, Y, Z), ext(3), ext(3), ext(5), ext(5),
            vm(2, ns * ng, 1, 128), vm(6, Y * X, Z), vm(ns, 6, zrows, 128), vm(ns, 6, zrows, 128),
            dma((8,)), dma((8,)), dma((8,)), dma((8,)), dma((8,)), dma((8,)), dma((8,)), dma((8,)),
            dma((2,)), dma((2,)), dma((2, ns)), dma((2, ns)),
        ],
        compiler_params=pltpu.CompilerParams(collective_id=0, has_side_effects=True, vmem_limit_bytes=60 << 20),
    )(u_now, u_prev, force, stiffness, broken, flags, ez, cz, gt)


def fits(mesh, shape):
    ns, ng = mesh.shape["slab"], mesh.shape["grp"]
    x, y, z = shape[1] // ns, shape[2] // ng, shape[3]
    return y == 8 and z == 128 and x * y == 128 and x * ns == 128 and z % (8 * ns) == 0


def entry(mesh, *args):
    ns, ng = mesh.shape["slab"], mesh.shape["grp"]
    _, x, y, z = args[0].shape
    if fits(mesh, (3, x * ns, y * ng, z)):
        return fused(mesh, *args)
    return body(*args)


def solution(mesh):
    return jax.shard_map(
        lambda *args: entry(mesh, *args),
        mesh=mesh,
        in_specs=(
            P(None, "slab", "grp", None),
            P(None, "slab", "grp", None),
            P(None, "slab", "grp", None),
            P("slab", "grp", None),
            P("slab", "grp", None),
            P("slab", "grp", None),
        ),
        out_specs=(P(None, "slab", "grp", None), P(None, "grp", "slab", None)),
        check_vma=False,
    )
```

```python
import jax
import jax.numpy as jnp
import numpy as np
from jax import lax
from jax.experimental import pallas as pl
from jax.experimental.pallas import tpu as pltpu
from jax.sharding import PartitionSpec as P

STEPS = 2
ITERS = 2
LEVELS = 3


SPRING_NORMAL = 1.0
SPRING_SHEAR = 0.4
MASS_TERM = 1.0
CRACK_CUT = 0.9


def with_halo(block, sides, width):
    for axis, dim in sides:
        count = lax.axis_size(axis)
        forward = [(i, i + 1) for i in range(count - 1)]
        backward = [(target, source) for source, target in forward]
        low = lax.ppermute(
            lax.slice_in_dim(block, block.shape[dim] - width, None, axis=dim), axis, forward
        )
        high = lax.ppermute(lax.slice_in_dim(block, 0, width, axis=dim), axis, backward)
        block = jnp.concatenate([low, block, high], axis=dim)
    return block


def cosine_table():
    freq = np.arange(4)[:, None]
    place = np.arange(4)[None, :]
    factor = np.where(freq == 0, 0.5, np.sqrt(0.5))
    return factor * np.cos(np.pi * (2 * place + 1) * freq / 8.0)


def block_table(count):
    return jnp.asarray(np.kron(np.eye(count // 4), cosine_table()), jnp.float32)


def spread(mask):
    values = mask.astype(jnp.float32)
    size_a, size_b, size_c = values.shape
    wide = jnp.broadcast_to(values[:, None, :, None, :, None], (size_a, 4, size_b, 4, size_c, 4))
    return wide.reshape(size_a * 4, size_b * 4, size_c * 4)


def sides(padded, axis_index):
    leading = padded.ndim - 3

    def cut(offset):
        index_list = [slice(None)] * leading + [slice(1, -1)] * 3
        length = padded.shape[leading + axis_index]
        index_list[leading + axis_index] = slice(1 + offset, length - 1 + offset)
        return padded[tuple(index_list)]

    return (cut(1), cut(-1))


def springs(field, weight, field_pad, weight_pad):
    result = MASS_TERM * field
    for axis_index in range(3):
        upper_v, lower_v = sides(field_pad, axis_index)
        upper_w, lower_w = sides(weight_pad, axis_index)
        k_upper = 0.5 * (weight + upper_w)
        k_lower = 0.5 * (weight + lower_w)
        change = k_upper * (field - upper_v) + k_lower * (field - lower_v)
        coupling = jnp.array(
            [SPRING_NORMAL if comp == axis_index else SPRING_SHEAR for comp in range(3)],
            jnp.float32,
        ).reshape(3, 1, 1, 1)
        result = result + coupling * change
    return result


def faces(field):
    padded = with_halo(field, (("slab", 1), ("grp", 2)), 1)
    return jnp.pad(padded, ((0, 0), (0, 0), (0, 0), (1, 1)))


def stresses(carry, field_pad):
    rows_out = []
    for axis_index in range(3):
        upper_v, lower_v = sides(field_pad, axis_index)
        rows_out.append(SPRING_NORMAL * carry * 0.5 * (upper_v[axis_index] - lower_v[axis_index]))
    return jnp.stack(rows_out)


def paired_sum(residual, image):
    return lax.psum((jnp.sum(residual * residual), jnp.sum(residual * image)), ("slab", "grp"))


def lift(signal):
    even = signal[..., 0::2]
    odd = signal[..., 1::2]
    detail = odd - 0.5 * (even + jnp.roll(even, -1, axis=-1))
    approx = even + 0.25 * (jnp.roll(detail, 1, axis=-1) + detail)
    return (approx, detail)


def wavelet(signal):
    pieces = []
    approx = signal
    for level_index in range(LEVELS):
        approx, detail = lift(approx)
        pieces.insert(0, detail)
    return jnp.concatenate([approx] + pieces, axis=-1)


def body(u_now, u_prev, force, stiffness, broken, flags):
    weight = stiffness * (1.0 - CRACK_CUT * spread(broken))
    carry = spread(flags) * weight
    weight_pad = with_halo(weight, (("slab", 0), ("grp", 1)), 1)
    weight_pad = jnp.pad(weight_pad, ((0, 0), (0, 0), (1, 1)))

    def operate(field):
        return springs(field, weight, faces(field), weight_pad)

    for step_index in range(STEPS):
        rhs = MASS_TERM * (2.0 * u_now - u_prev) + force
        guess = u_now
        residual = rhs - operate(guess)
        image = operate(residual)
        norm_now, product = paired_sum(residual, image)
        alpha = norm_now / product
        direction, along = (residual, image)
        for turn_index in range(ITERS):
            guess = guess + alpha * direction
            residual = residual - alpha * along
            if turn_index + 1 < ITERS:
                image = operate(residual)
                norm_next, product = paired_sum(residual, image)
                ratio = norm_next / norm_now
                alpha = norm_next / (product - ratio * norm_next / alpha)
                direction = residual + ratio * direction
                along = image + ratio * along
                norm_now = norm_next
        u_prev = u_now
        u_now = guess
    stress = stresses(carry, faces(u_now))
    fields = jnp.concatenate([u_now, stress], axis=0)
    table_x = block_table(fields.shape[1])
    table_y = block_table(fields.shape[2])
    table_z = block_table(fields.shape[3])
    blockc = jnp.einsum("ax,hxyz->hayz", table_x, fields, precision=lax.Precision.HIGHEST)
    blockc = jnp.einsum("by,hxyz->hxbz", table_y, blockc, precision=lax.Precision.HIGHEST)
    blockc = jnp.einsum("hxyz,cz->hxyc", blockc, table_z, precision=lax.Precision.HIGHEST)
    moved = jnp.transpose(blockc, (0, 2, 3, 1))
    shipped = lax.all_to_all(moved, "slab", split_axis=2, concat_axis=3, tiled=True)
    coeffs = wavelet(shipped)
    return (u_now, coeffs)


MESH = pl.DeviceIdType.MESH
HALO = 4
REACH = 3
SHEAR_REST = SPRING_NORMAL - SPRING_SHEAR


def wavelet_table(count):
    table = np.kron(np.eye(count // 4), cosine_table())
    pieces = []
    approx = table
    for level_index in range(LEVELS):
        even, odd = approx[0::2], approx[1::2]
        detail = odd - 0.5 * (even + np.roll(even, -1, axis=0))
        approx = even + 0.25 * (np.roll(detail, 1, axis=0) + detail)
        pieces.insert(0, detail)
    return np.concatenate([approx] + pieces, axis=0)


def split_table(table):
    high = table.astype(jnp.bfloat16).astype(np.float64)
    return high, (table - high).astype(jnp.bfloat16).astype(np.float64)


def sub_index():
    return lax.broadcasted_iota(jnp.int32, (8, 128), 0)


def lane_index():
    return lax.broadcasted_iota(jnp.int32, (8, 128), 1)


def up_y(a, b):
    ra, rb = pltpu.roll(a, 7, 0), pltpu.roll(b, 7, 0)
    last = sub_index() == 7
    return jnp.where(last, rb, ra), jnp.where(last, ra, rb)


def down_y(a, b):
    ra, rb = pltpu.roll(a, 1, 0), pltpu.roll(b, 1, 0)
    first = sub_index() == 0
    return jnp.where(first, rb, ra), jnp.where(first, ra, rb)


def up_z(v):
    return pltpu.roll(v, 127, 1)


def down_z(v):
    return pltpu.roll(v, 1, 1)


def total(v):
    return jnp.sum(jnp.sum(v, axis=0, keepdims=True), axis=1, keepdims=True)


def kernel(ns, ng, u_in, p_in, f_in, k_in, br_in, fl_in, ez_in, cz_in, gt_in,
           disp_out, coef_out,
           disp_ref, coef_ref, osem, u_ref, p_ref, f_ref, k_ref, br_ref, fl_ref, ez_ref, cz_ref, gt_ref, isem,
           e1a, e1b, s1, h1, e2a, e2b, s2, h2, rqa, rqb, e3a, s3, h3,
           u1a, u1b, carry, dga, dgb, kca, kcb, gath, rows, outb, inb,
           ctake, cland, csend, crecv, send4, recv4, send0, recv0, send1, recv1, send2, recv2, send3, recv3, asend, arecv, tsend, trecv):
    X, Y = u_ref.shape[1], u_ref.shape[2]
    si, gi = lax.axis_index("slab"), lax.axis_index("grp")
    me = si * ng + gi
    count = ns * ng
    fetched = []
    for at, (source, target) in enumerate((
        (br_in, br_ref), (fl_in, fl_ref), (ez_in, ez_ref), (k_in, k_ref), (u_in, u_ref), (p_in, p_ref),
        (f_in, f_ref), (cz_in, cz_ref), (gt_in, gt_ref),
    )):
        fetch = pltpu.make_async_copy(source, target, isem.at[at])
        fetch.start()
        fetched.append(fetch)
    barrier = pltpu.get_barrier_semaphore()

    def greet(i, _):
        other = lax.rem(me + i, count)
        pl.semaphore_signal(barrier, inc=1, device_id=(other // ng, lax.rem(other, ng)), device_id_type=MESH)
        return 0

    lax.fori_loop(1, count, greet, 0)

    sub, lane = sub_index(), lane_index()
    upper = sub < 4

    steps = [(-1, 0), (1, 0), (0, -1), (0, 1), (-1, -1), (-1, 1), (1, -1), (1, 1)]

    def inside(ds, dg):
        ok = None
        if ds:
            ok = (si >= 1) if ds < 0 else (si <= ns - 2)
        if dg:
            more = (gi >= 1) if dg < 0 else (gi <= ng - 2)
            ok = more if ok is None else jnp.logical_and(ok, more)
        return ok

    def copies(ea, dst_a, stage, land, send, recv, low=0, high=None, ways=8, reach=REACH):
        half = X // 2
        edge = HALO // 2
        made = []
        chans = pl.ds(low, (ea.shape[0] if high is None else high) - low)
        for at, (ds, dg) in enumerate(steps[:ways]):
            if dg == 0:
                if ds < 0:
                    source = ea.at[chans, pl.ds(HALO, reach)]
                    target = dst_a.at[chans, pl.ds(HALO + X, reach)]
                else:
                    source = ea.at[chans, pl.ds(HALO + X - reach, reach)]
                    target = dst_a.at[chans, pl.ds(HALO - reach, reach)]
            else:
                side = 0 if dg < 0 else 1
                if ds == 0:
                    source, target = stage.at[side, chans], land.at[side, chans, pl.ds(edge, half)]
                elif ds < 0:
                    source = stage.at[side, chans, pl.ds(0, 1)]
                    target = land.at[side, chans, pl.ds(edge + half, 1)]
                else:
                    source = stage.at[side, chans, pl.ds(half - 1, 1)]
                    target = land.at[side, chans, pl.ds(edge - 1, 1)]
            made.append((ds, dg, pltpu.make_async_remote_copy(
                src_ref=source, dst_ref=target, send_sem=send.at[at], recv_sem=recv.at[at ^ 1 if at < 4 else 11 - at],
                device_id=(si + ds, gi + dg), device_id_type=MESH)))
        return made

    def begin(made):
        for ds, dg, copy in made:
            @pl.when(inside(ds, dg))
            def _():
                copy.start()

    def finish_recv(made, recv):
        for at, (ds, dg) in enumerate(steps[:len(made)]):
            back = made[at ^ 1 if at < 4 else 11 - at][2]

            @pl.when(inside(ds, dg))
            def _():
                back.wait_recv()

    def finish_send(made):
        for ds, dg, copy in made:
            @pl.when(inside(ds, dg))
            def _():
                copy.wait_send()

    def blank(dst_a, land):
        zero_a = jnp.zeros((dst_a.shape[0], HALO) + dst_a.shape[2:], jnp.float32)
        half, edge = X // 2, HALO // 2
        zero_l = jnp.zeros((land.shape[1], edge, 8, 128), jnp.float32)

        @pl.when(si == 0)
        def _():
            dst_a[:, pl.ds(0, HALO)] = zero_a
            for side in range(2):
                land[side, :, pl.ds(0, edge)] = zero_l

        @pl.when(si == ns - 1)
        def _():
            dst_a[:, pl.ds(HALO + X, HALO)] = zero_a
            for side in range(2):
                land[side, :, pl.ds(edge + half, edge)] = zero_l

        for side, edge_here in ((0, gi == ng - 1), (1, gi == 0)):
            @pl.when(edge_here)
            def _(side=side):
                land[side] = jnp.zeros(land.shape[1:], jnp.float32)

    def pack(stage, ch, pair, even, odd):
        stage[0, ch, pair] = jnp.where(upper, even, pltpu.roll(odd, 4, 0))
        stage[1, ch, pair] = jnp.where(upper, pltpu.roll(even, 4, 0), odd)

    def unpack(land, ch, pair):
        high, low = land[0, ch, pair], land[1, ch, pair]
        return (jnp.where(upper, high, pltpu.roll(low, 4, 0)),
                jnp.where(upper, pltpu.roll(high, 4, 0), low))

    def spread_rows(mask):
        wide = jnp.dot(mask.astype(jnp.float32), ez_ref[...], preferred_element_type=jnp.float32)
        return jnp.where(upper, jnp.broadcast_to(wide[0:1], (8, 128)), jnp.broadcast_to(wide[1:2], (8, 128)))

    for at in range(4):
        fetched[at].wait()
    for bx in range(X // 4):
        cut = 1.0 - CRACK_CUT * spread_rows(br_ref[bx])
        flag = spread_rows(fl_ref[bx])
        for at in range(4):
            x = bx * 4 + at
            w = k_ref[x] * cut
            e1a[6, HALO + x] = w
            carry[x] = flag * w

    def own(i, _):
        for c in range(3):
            tiles = []
            for o in range(2):
                x = 2 * i + o
                u = u_ref[c, x]
                f = f_ref[c, x]
                rhs = MASS_TERM * (2.0 * u - p_ref[c, x]) + f
                e1a[c, HALO + x] = u
                e1a[3 + c, HALO + x] = rhs
                e2a[c, HALO + x] = f
                tiles.append((u, rhs, f))
            pack(s1, c, i, tiles[0][0], tiles[1][0])
            pack(s1, 3 + c, i, tiles[0][1], tiles[1][1])
            pack(s2, c, i, tiles[0][2], tiles[1][2])
        pack(s1, 6, i, e1a[6, HALO + 2 * i], e1a[6, HALO + 2 * i + 1])
        return 0

    for at in range(4, 7):
        fetched[at].wait()
    lax.fori_loop(0, X // 2, own, 0)
    blank(e1a, h1)
    blank(e2a, h2)
    blank(e3a, h3)

    def corner_copies():
        made = []
        for at, (ds, dg) in enumerate(steps[4:]):
            side, end = (0 if dg < 0 else 1), (0 if ds < 0 else 1)
            made.append((ds, dg, pltpu.make_async_remote_copy(
                src_ref=ctake.at[side, end], dst_ref=cland.at[side, 1 - end],
                send_sem=csend.at[at], recv_sem=crecv.at[3 - at],
                device_id=(si + ds, gi + dg), device_id_type=MESH)))
        return made

    near = sub % 4 < 2
    for side in range(2):
        for end in range(2):
            for t in range((7 + 1) // 2):
                tile = s1[side, 2 * t, end * (X // 2 - 1)]
                if 2 * t + 1 < 7:
                    other = s1[side, 2 * t + 1, end * (X // 2 - 1)]
                    tile = (jnp.where(near, tile, pltpu.roll(other, 2, 0)) if side == 0
                            else jnp.where(near, pltpu.roll(other, 6, 0), tile))
                ctake[side, end, t] = tile

    def corner_unpack(made):
        for at, (ds, dg) in enumerate(steps[4:]):
            side, end = (0 if dg > 0 else 1), (1 if ds > 0 else 0)
            pair = HALO // 2 + X // 2 if ds > 0 else HALO // 2 - 1
            back = made[3 - at][2]

            @pl.when(inside(ds, dg))
            def _():
                back.wait_recv()
                for ch in range(7):
                    tile = cland[side, end, ch // 2]
                    h1[side, ch, pair] = tile if ch % 2 == 0 else pltpu.roll(tile, 6 if side == 0 else 2, 0)

    corners = corner_copies()
    zeroth = copies(e1a, e1a, s1, h1, send0, recv0, 6, 7, 4)
    first = copies(e1a, e1a, s1, h1, send1, recv1, 0, 3, 4)
    rest = copies(e1a, e1a, s1, h1, send4, recv4, 3, 6, 4, REACH - 1)
    second = copies(e2a, e2a, s2, h2, send2, recv2)
    third = copies(rqa, e3a, s3, h3, send3, recv3)
    pl.semaphore_wait(barrier, count - 1)
    begin(zeroth)
    begin(corners)
    begin(first)
    begin(rest)
    finish_recv(zeroth, recv0)
    corner_unpack(corners)

    def open0(i, _):
        e1b[6, 2 * i], e1b[6, 2 * i + 1] = unpack(h1, 6, i)
        return 0

    def open1(i, _):
        for ch in range(6):
            e1b[ch, 2 * i], e1b[ch, 2 * i + 1] = unpack(h1, ch, i)
        return 0

    lax.fori_loop(0, (X + 2 * HALO) // 2, open0, 0)

    def link(w, other):
        return jnp.where(jnp.minimum(w, other) > 0.0, 0.5 * (w + other), 0.0)

    not_last, not_first = lane < 127, lane > 0

    def coefficients(x, _):
        wa, wb = e1a[6, x], e1b[6, x]
        ya, yb = up_y(wa, wb)
        da, db = down_y(wa, wb)
        for w, wu, wd, yu, yd, dg, kc in (
            (wa, e1a[6, x + 1], e1a[6, x - 1], ya, da, dga, kca),
            (wb, e1b[6, x + 1], e1b[6, x - 1], yb, db, dgb, kcb),
        ):
            zu = jnp.where(not_last, up_z(w), 0.0)
            zd = jnp.where(not_first, down_z(w), 0.0)
            kc[0, x] = link(w, wu)
            kc[1, x] = link(w, yu)
            kc[2, x] = link(w, yd)
            kc[3, x] = link(w, zu)
            kc[4, x] = link(w, zd)
            sx = w + 0.5 * (wu + wd)
            sy = w + 0.5 * (yu + yd)
            sz = w + 0.5 * (zu + zd)
            every = MASS_TERM + SPRING_SHEAR * (sx + sy + sz)
            dg[0, x] = every + SHEAR_REST * sx
            dg[1, x] = every + SHEAR_REST * sy
            dg[2, x] = every + SHEAR_REST * sz
        return 0

    kca[0, HALO - REACH] = link(e1a[6, HALO - REACH], e1a[6, HALO - REACH + 1])
    kcb[0, HALO - REACH] = link(e1b[6, HALO - REACH], e1b[6, HALO - REACH + 1])
    lax.fori_loop(HALO - 2, HALO + X + 2, coefficients, 0)
    finish_recv(first, recv1)
    finish_recv(rest, recv4)
    begin(second)
    lax.fori_loop(0, (X + 2 * HALO) // 2, open1, 0)

    def operate(x, va, vb, base, both=True):
        result = []
        coef = [[kc[j, x] for j in range(5)] + [kc[0, x - 1]] for kc in (kca, kcb)]
        for c in range(3):
            a, b = va[base + c, x], vb[base + c, x]
            ua, ub = up_y(a, b)
            la, lb = down_y(a, b)
            pair = []
            halves = ((a, va, ua, la, coef[0], dga), (b, vb, ub, lb, coef[1], dgb))
            for v, ref, u, l, k, dg in halves if both else halves[:1]:
                parts = (
                    k[0] * ref[base + c, x + 1] + k[5] * ref[base + c, x - 1],
                    k[1] * u + k[2] * l,
                    k[3] * up_z(v) + k[4] * down_z(v),
                )
                every = parts[0] + parts[1] + parts[2]
                pair.append(dg[c, x] * v - (SPRING_SHEAR * every + SHEAR_REST * parts[c]))
            result.append(pair)
        return result

    def solve(step, va, vb, rhs_of):
        def residual(i, _):
            done = []
            for x in (2 * i, 2 * i + 1):
                image = operate(x, va, vb, 0)
                for c in range(3):
                    ra, rb = rhs_of(c, x)
                    done.append((c, x, ra - image[c][0], rb - image[c][1]))
            for c, x, ra, rb in done:
                rqa[c, x] = ra
                rqb[c, x] = rb
            return 0

        lax.fori_loop((HALO - 2) // 2, (HALO + X + 2) // 2, residual, 0)

        def put(x, image):
            for c in range(3):
                rqa[3 + c, x] = image[c][0]
                rqb[3 + c, x] = image[c][1]

        def apply(i, sums):
            rr, rq = sums
            at = (2 * i, 2 * i + 1)
            images = [operate(x, rqa, rqb, 0) for x in at]
            for x, image in zip(at, images):
                for c in range(3):
                    r = rqa[c, x]
                    rr, rq = rr + r * r, rq + r * image[c][0]
            for x, image in zip(at, images):
                put(x, image)
            return rr, rq

        zero = jnp.zeros((8, 128), jnp.float32)
        images = [operate(x, rqa, rqb, 0) for x in (HALO - 1, HALO + X)]
        put(HALO - 1, images[0])
        put(HALO + X, images[1])
        rr, rq = lax.fori_loop(HALO // 2, (HALO + X) // 2, apply, (zero, zero))
        rr, rq = total(rr), total(rq)
        mu = jnp.where(rr > 0.0, rq / jnp.where(rr > 0.0, rr, 1.0), 0.0)

        def centred(i, sums):
            ww, wr, mix, wt = sums
            for x in (2 * i, 2 * i + 1):
                image = operate(x, rqa, rqb, 3, False)
                for c in range(3):
                    r, q, s = rqa[c, x], rqa[3 + c, x], image[c][0]
                    w, t = q - mu * r, s - mu * q
                    ww, wr, mix, wt = ww + w * w, wr + w * r, mix + (r * t + w * q), wt + w * t
            return ww, wr, mix, wt

        sums = lax.fori_loop(HALO // 2, (HALO + X) // 2, centred, (zero,) * 4)
        ww, wr, mix, wt = [total(v) for v in sums]
        one = lax.broadcasted_iota(jnp.int32, (1, 128), 1)
        row = jnp.zeros((1, 128), jnp.float32)
        for at, value in enumerate((rr, rq, mu, ww, wr, mix, wt)):
            row = jnp.where(one == at, value, row)
        gath[step, me] = row

        def share(i, _):
            other = lax.rem(me + i, count)
            pltpu.make_async_remote_copy(
                src_ref=gath.at[step, me], dst_ref=gath.at[step, me], send_sem=asend.at[step], recv_sem=arecv.at[step],
                device_id=(other // ng, lax.rem(other, ng)), device_id_type=MESH).start()
            return 0

        lax.fori_loop(1, count, share, 0)

    def collect(step):
        block = gath.at[step, pl.ds(0, count - 1)]
        pltpu.make_async_copy(block, block, arecv.at[step]).wait()
        table = gath[step].reshape(count, 128)
        rr, rq, mu, ww, wr, mix, wt = [table[:, at:at + 1] for at in range(7)]

        def down(v):
            return jnp.sum(v, axis=0, keepdims=True)

        norm = down(rr)
        alpha = norm / down(rq)
        rest = 1.0 - alpha * mu
        after = down(alpha * alpha * ww - 2.0 * alpha * rest * wr + rest * rest * rr)
        curved = down(rest * rest * rq - alpha * rest * mix + alpha * alpha * wt)
        ratio = after / norm
        beta = after / (curved - ratio * after / alpha)
        return alpha + beta * (1.0 + ratio), -beta * alpha

    def drain(step):
        block = gath.at[step, pl.ds(0, count - 1)]
        pltpu.make_async_copy(block, block, asend.at[step]).wait()

    solve(0, e1a, e1b, lambda c, x: (e1a[3 + c, x], e1b[3 + c, x]))

    def pack3(i, _):
        for ch in range(6):
            pack(s3, ch, i, rqa[ch, HALO + 2 * i], rqa[ch, HALO + 2 * i + 1])
        return 0

    lax.fori_loop(0, X // 2, pack3, 0)
    begin(third)

    finish_recv(second, recv2)

    def open2(i, _):
        for ch in range(3):
            e2b[ch, 2 * i], e2b[ch, 2 * i + 1] = unpack(h2, ch, i)
        return 0

    lax.fori_loop(0, (X + 2 * HALO) // 2, open2, 0)
    finish_recv(third, recv3)
    c0, c1 = collect(0)

    def step_b(i, _):
        for c in range(3):
            r0, r1 = unpack(h3, c, i)
            q0, q1 = unpack(h3, 3 + c, i)
            u1b[c, 2 * i] = e1b[c, 2 * i] + (c0 * r0 + c1 * q0)
            u1b[c, 2 * i + 1] = e1b[c, 2 * i + 1] + (c0 * r1 + c1 * q1)
        return 0

    lax.fori_loop(0, (X + 2 * HALO) // 2, step_b, 0)

    def step_a(x, _):
        for c in range(3):
            u1a[c, x] = e1a[c, x] + (c0 * rqa[c, x] + c1 * rqa[3 + c, x])
        return 0

    lax.fori_loop(HALO, HALO + X, step_a, 0)
    for x in list(range(HALO - REACH, HALO)) + list(range(HALO + X, HALO + X + REACH)):
        for c in range(3):
            u1a[c, x] = e1a[c, x] + (c0 * e3a[c, x] + c1 * e3a[3 + c, x])
    finish_send(zeroth)
    finish_send(corners)
    finish_send(rest)
    finish_send(first)
    finish_send(second)
    finish_send(third)

    def rhs2(c, x):
        return (MASS_TERM * (2.0 * u1a[c, x] - e1a[c, x]) + e2a[c, x],
                MASS_TERM * (2.0 * u1b[c, x] - e1b[c, x]) + e2b[c, x])

    solve(1, u1a, u1b, rhs2)
    c0, c1 = collect(1)

    def step2(x, _):
        for c in range(3):
            va = u1a[c, x] + (c0 * rqa[c, x] + c1 * rqa[3 + c, x])
            vb = u1b[c, x] + (c0 * rqb[c, x] + c1 * rqb[3 + c, x])
            u1a[c, x] = va
            u1b[c, x] = vb
        return 0

    step2(HALO - 1, 0)
    step2(HALO + X, 0)

    def step2_own(i, _):
        for x in (2 * i, 2 * i + 1):
            step2(x, 0)
            for c in range(3):
                v = u1a[c, x]
                disp_ref[c, x - HALO] = v
                rows[c, pl.ds(x - HALO, 8, stride=X), :] = v
        return 0

    lax.fori_loop(HALO // 2, (HALO + X) // 2, step2_own, 0)
    outputs = [pltpu.make_async_copy(disp_ref, disp_out, osem.at[6])]
    outputs += [pltpu.make_async_copy(coef_ref.at[c], coef_out.at[c], osem.at[c]) for c in range(6)]
    zrows = coef_ref.shape[2]
    nt = (((1,), (1,)), ((), ()))

    def halves(v):
        high = v.astype(jnp.bfloat16)
        return high, (v - high.astype(jnp.float32)).astype(jnp.bfloat16)

    def transform(c, _):
        high, low = halves(rows[c])
        turned = lax.dot_general(cz_ref[:, 0:256], jnp.concatenate([high, low], axis=1), nt,
                                 preferred_element_type=jnp.float32)
        turned += lax.dot_general(cz_ref[:, 256:384], high, nt, preferred_element_type=jnp.float32)
        for j in range(ns):
            outb[j, c] = turned[j * zrows:(j + 1) * zrows]
        return 0

    def trade(part, i):
        to = lax.rem(si + i, ns)
        return pltpu.make_async_remote_copy(
            src_ref=outb.at[to, pl.ds(3 * part, 3)], dst_ref=inb.at[si, pl.ds(3 * part, 3)],
            send_sem=tsend.at[part, i], recv_sem=trecv.at[part, i],
            device_id=(to, gi), device_id_type=MESH)

    trades = [[trade(part, i) for i in range(1, ns)] for part in range(2)]

    def ship(part):
        lax.fori_loop(3 * part, 3 * part + 3, transform, 0)
        for copy in trades[part]:
            copy.start()
        for c in range(3 * part, 3 * part + 3):
            inb[si, c] = outb[si, c]

    fetched[7].wait()
    ship(0)
    outputs[0].start()

    def finals(i, _):
        for x in (2 * i, 2 * i + 1):
            at = x - HALO
            scale = SPRING_NORMAL * carry[at] * 0.5
            a1, a2, b1 = u1a[1, x], u1a[2, x], u1b[1, x]
            dx = u1a[0, x + 1] - u1a[0, x - 1]
            dy = up_y(a1, b1)[0] - down_y(a1, b1)[0]
            dz = jnp.where(not_last, up_z(a2), 0.0) - jnp.where(not_first, down_z(a2), 0.0)
            for c, d in enumerate((dx, dy, dz)):
                rows[3 + c, pl.ds(at, 8, stride=X), :] = scale * d
        return 0

    lax.fori_loop(HALO // 2, (HALO + X) // 2, finals, 0)
    ship(1)
    fetched[8].wait()

    zlane = lax.broadcasted_iota(jnp.int32, (zrows, 128), 1)
    c1t, c3t = float(np.sqrt(0.5) * np.cos(np.pi / 8)), float(np.sqrt(0.5) * np.cos(3 * np.pi / 8))

    def gather_back(c, _):
        pieces = [inb[j, c] for j in range(ns)]
        gap = ns // 2
        while gap:
            keep = (zlane // (X * gap)) % 2 == 0
            mixed = list(pieces)
            for j in range(ns):
                if (j // gap) % 2 == 0:
                    a, b = pieces[j], pieces[j + gap]
                    mixed[j] = jnp.where(keep, a, pltpu.roll(b, X * gap, 1))
                    mixed[j + gap] = jnp.where(keep, pltpu.roll(a, 128 - X * gap, 1), b)
            pieces = mixed
            gap //= 2
        coded = []
        for b in range(Y // 4):
            v0, v1, v2, v3 = pieces[4 * b:4 * b + 4]
            s03, s12, d03, d12 = v0 + v3, v1 + v2, v0 - v3, v1 - v2
            coded += [0.5 * (s03 + s12), c1t * d03 + c3t * d12, 0.5 * (s03 - s12), c3t * d03 - c1t * d12]
        high, low = halves(jnp.concatenate(coded, axis=0))
        done = jnp.dot(jnp.concatenate([high, low], axis=1), gt_ref[...], preferred_element_type=jnp.float32)
        coef_ref[c] = (done[:, 0:128] + done[:, 128:256]).reshape(Y, zrows, 128)
        return 0

    for part in range(2):
        for copy in trades[part]:
            copy.wait_recv()
        for c in range(3 * part, 3 * part + 3):
            gather_back(c, 0)
            outputs[1 + c].start()
    drain(0)
    drain(1)
    for part in range(2):
        for copy in trades[part]:
            copy.wait_send()
    for copy in outputs:
        copy.wait()


def fused(mesh, u_now, u_prev, force, stiffness, broken, flags):
    ns, ng = mesh.shape["slab"], mesh.shape["grp"]
    _, X, Y, Z = u_now.shape
    xe, pairs, half = X + 2 * HALO, X // 2 + HALO, X // 2
    zrows = Z // ns
    ez = jnp.asarray(np.kron(np.eye(Z // 4), np.ones((1, 4))), jnp.float32)
    czh, czl = split_table(np.kron(np.eye(Z // 4), cosine_table()))
    cz = jnp.asarray(np.concatenate([czh, czh, czl], axis=1), jnp.bfloat16)
    gth, gtl = split_table(wavelet_table(X * ns).T)
    gt = jnp.asarray(np.block([[gth, gtl], [gth, np.zeros_like(gtl)]]), jnp.bfloat16)

    def vm(*shape):
        return pltpu.VMEM(shape, jnp.float32)

    def ext(n):
        return vm(n, xe, Y, Z)

    def stage(n):
        return vm(2, n, half, Y, Z)

    def land(n):
        return vm(2, n, pairs, Y, Z)

    dma = pltpu.SemaphoreType.DMA
    return pl.pallas_call(
        lambda *refs: kernel(ns, ng, *refs),
        name="lattice",
        out_shape=(jax.ShapeDtypeStruct(u_now.shape, jnp.float32),
                   jax.ShapeDtypeStruct((6, Y, zrows, X * ns), jnp.float32)),
        in_specs=[pl.BlockSpec(memory_space=pltpu.MemorySpace.HBM)] * 9,
        out_specs=(pl.BlockSpec(memory_space=pltpu.MemorySpace.HBM),) * 2,
        scratch_shapes=[
            vm(*u_now.shape), vm(6, Y, zrows, X * ns), pltpu.SemaphoreType.DMA((7,)),
            vm(*u_now.shape), vm(*u_now.shape), vm(*u_now.shape), vm(*stiffness.shape),
            pltpu.VMEM(broken.shape, broken.dtype), pltpu.VMEM(flags.shape, flags.dtype),
            vm(*ez.shape), pltpu.VMEM(cz.shape, cz.dtype), pltpu.VMEM(gt.shape, gt.dtype), pltpu.SemaphoreType.DMA((9,)),
            ext(7), ext(7), stage(7), land(7),
            ext(3), ext(3), stage(3), land(3),
            ext(6), ext(6), ext(6), stage(6), land(6),
            ext(3), ext(3), vm(X, Y, Z), ext(3), ext(3), ext(5), ext(5),
            vm(2, ns * ng, 1, 128), vm(6, Y * X, Z), vm(ns, 6, zrows, 128), vm(ns, 6, zrows, 128),
            vm(2, 2, 4, Y, Z), vm(2, 2, 4, Y, Z), dma((4,)), dma((4,)), dma((8,)), dma((8,)),
            dma((8,)), dma((8,)), dma((8,)), dma((8,)), dma((8,)), dma((8,)), dma((8,)), dma((8,)),
            dma((2,)), dma((2,)), dma((2, ns)), dma((2, ns)),
        ],
        compiler_params=pltpu.CompilerParams(collective_id=0, has_side_effects=True, vmem_limit_bytes=60 << 20),
    )(u_now, u_prev, force, stiffness, broken, flags, ez, cz, gt)


def fits(mesh, shape):
    ns, ng = mesh.shape["slab"], mesh.shape["grp"]
    x, y, z = shape[1] // ns, shape[2] // ng, shape[3]
    return y == 8 and z == 128 and x * y == 128 and x * ns == 128 and z % (8 * ns) == 0


def entry(mesh, *args):
    ns, ng = mesh.shape["slab"], mesh.shape["grp"]
    _, x, y, z = args[0].shape
    if fits(mesh, (3, x * ns, y * ng, z)):
        return fused(mesh, *args)
    return body(*args)


def solution(mesh):
    return jax.shard_map(
        lambda *args: entry(mesh, *args),
        mesh=mesh,
        in_specs=(
            P(None, "slab", "grp", None),
            P(None, "slab", "grp", None),
            P(None, "slab", "grp", None),
            P("slab", "grp", None),
            P("slab", "grp", None),
            P("slab", "grp", None),
        ),
        out_specs=(P(None, "slab", "grp", None), P(None, "grp", "slab", None)),
        check_vma=False,
    )
```

```python
import jax
import jax.numpy as jnp
import numpy as np
from jax import lax
from jax.experimental import pallas as pl
from jax.experimental.pallas import tpu as pltpu
from jax.sharding import PartitionSpec as P

STEPS = 2
ITERS = 2
LEVELS = 3


SPRING_NORMAL = 1.0
SPRING_SHEAR = 0.4
MASS_TERM = 1.0
CRACK_CUT = 0.9


def with_halo(block, sides, width):
    for axis, dim in sides:
        count = lax.axis_size(axis)
        forward = [(i, i + 1) for i in range(count - 1)]
        backward = [(target, source) for source, target in forward]
        low = lax.ppermute(
            lax.slice_in_dim(block, block.shape[dim] - width, None, axis=dim), axis, forward
        )
        high = lax.ppermute(lax.slice_in_dim(block, 0, width, axis=dim), axis, backward)
        block = jnp.concatenate([low, block, high], axis=dim)
    return block


def cosine_table():
    freq = np.arange(4)[:, None]
    place = np.arange(4)[None, :]
    factor = np.where(freq == 0, 0.5, np.sqrt(0.5))
    return factor * np.cos(np.pi * (2 * place + 1) * freq / 8.0)


def block_table(count):
    return jnp.asarray(np.kron(np.eye(count // 4), cosine_table()), jnp.float32)


def spread(mask):
    values = mask.astype(jnp.float32)
    size_a, size_b, size_c = values.shape
    wide = jnp.broadcast_to(values[:, None, :, None, :, None], (size_a, 4, size_b, 4, size_c, 4))
    return wide.reshape(size_a * 4, size_b * 4, size_c * 4)


def sides(padded, axis_index):
    leading = padded.ndim - 3

    def cut(offset):
        index_list = [slice(None)] * leading + [slice(1, -1)] * 3
        length = padded.shape[leading + axis_index]
        index_list[leading + axis_index] = slice(1 + offset, length - 1 + offset)
        return padded[tuple(index_list)]

    return (cut(1), cut(-1))


def springs(field, weight, field_pad, weight_pad):
    result = MASS_TERM * field
    for axis_index in range(3):
        upper_v, lower_v = sides(field_pad, axis_index)
        upper_w, lower_w = sides(weight_pad, axis_index)
        k_upper = 0.5 * (weight + upper_w)
        k_lower = 0.5 * (weight + lower_w)
        change = k_upper * (field - upper_v) + k_lower * (field - lower_v)
        coupling = jnp.array(
            [SPRING_NORMAL if comp == axis_index else SPRING_SHEAR for comp in range(3)],
            jnp.float32,
        ).reshape(3, 1, 1, 1)
        result = result + coupling * change
    return result


def faces(field):
    padded = with_halo(field, (("slab", 1), ("grp", 2)), 1)
    return jnp.pad(padded, ((0, 0), (0, 0), (0, 0), (1, 1)))


def stresses(carry, field_pad):
    rows_out = []
    for axis_index in range(3):
        upper_v, lower_v = sides(field_pad, axis_index)
        rows_out.append(SPRING_NORMAL * carry * 0.5 * (upper_v[axis_index] - lower_v[axis_index]))
    return jnp.stack(rows_out)


def paired_sum(residual, image):
    return lax.psum((jnp.sum(residual * residual), jnp.sum(residual * image)), ("slab", "grp"))


def lift(signal):
    even = signal[..., 0::2]
    odd = signal[..., 1::2]
    detail = odd - 0.5 * (even + jnp.roll(even, -1, axis=-1))
    approx = even + 0.25 * (jnp.roll(detail, 1, axis=-1) + detail)
    return (approx, detail)


def wavelet(signal):
    pieces = []
    approx = signal
    for level_index in range(LEVELS):
        approx, detail = lift(approx)
        pieces.insert(0, detail)
    return jnp.concatenate([approx] + pieces, axis=-1)


def body(u_now, u_prev, force, stiffness, broken, flags):
    weight = stiffness * (1.0 - CRACK_CUT * spread(broken))
    carry = spread(flags) * weight
    weight_pad = with_halo(weight, (("slab", 0), ("grp", 1)), 1)
    weight_pad = jnp.pad(weight_pad, ((0, 0), (0, 0), (1, 1)))

    def operate(field):
        return springs(field, weight, faces(field), weight_pad)

    for step_index in range(STEPS):
        rhs = MASS_TERM * (2.0 * u_now - u_prev) + force
        guess = u_now
        residual = rhs - operate(guess)
        image = operate(residual)
        norm_now, product = paired_sum(residual, image)
        alpha = norm_now / product
        direction, along = (residual, image)
        for turn_index in range(ITERS):
            guess = guess + alpha * direction
            residual = residual - alpha * along
            if turn_index + 1 < ITERS:
                image = operate(residual)
                norm_next, product = paired_sum(residual, image)
                ratio = norm_next / norm_now
                alpha = norm_next / (product - ratio * norm_next / alpha)
                direction = residual + ratio * direction
                along = image + ratio * along
                norm_now = norm_next
        u_prev = u_now
        u_now = guess
    stress = stresses(carry, faces(u_now))
    fields = jnp.concatenate([u_now, stress], axis=0)
    table_x = block_table(fields.shape[1])
    table_y = block_table(fields.shape[2])
    table_z = block_table(fields.shape[3])
    blockc = jnp.einsum("ax,hxyz->hayz", table_x, fields, precision=lax.Precision.HIGHEST)
    blockc = jnp.einsum("by,hxyz->hxbz", table_y, blockc, precision=lax.Precision.HIGHEST)
    blockc = jnp.einsum("hxyz,cz->hxyc", blockc, table_z, precision=lax.Precision.HIGHEST)
    moved = jnp.transpose(blockc, (0, 2, 3, 1))
    shipped = lax.all_to_all(moved, "slab", split_axis=2, concat_axis=3, tiled=True)
    coeffs = wavelet(shipped)
    return (u_now, coeffs)


MESH = pl.DeviceIdType.MESH
HALO = 4
REACH = 3
SHEAR_REST = SPRING_NORMAL - SPRING_SHEAR


def wavelet_table(count):
    table = np.kron(np.eye(count // 4), cosine_table())
    pieces = []
    approx = table
    for level_index in range(LEVELS):
        even, odd = approx[0::2], approx[1::2]
        detail = odd - 0.5 * (even + np.roll(even, -1, axis=0))
        approx = even + 0.25 * (np.roll(detail, 1, axis=0) + detail)
        pieces.insert(0, detail)
    return np.concatenate([approx] + pieces, axis=0)


def split_table(table):
    high = table.astype(jnp.bfloat16).astype(np.float64)
    return high, (table - high).astype(jnp.bfloat16).astype(np.float64)


def sub_index():
    return lax.broadcasted_iota(jnp.int32, (8, 128), 0)


def lane_index():
    return lax.broadcasted_iota(jnp.int32, (8, 128), 1)


def up_y(a, b):
    ra, rb = pltpu.roll(a, 7, 0), pltpu.roll(b, 7, 0)
    last = sub_index() == 7
    return jnp.where(last, rb, ra), jnp.where(last, ra, rb)


def down_y(a, b):
    ra, rb = pltpu.roll(a, 1, 0), pltpu.roll(b, 1, 0)
    first = sub_index() == 0
    return jnp.where(first, rb, ra), jnp.where(first, ra, rb)


def up_z(v):
    return pltpu.roll(v, 127, 1)


def down_z(v):
    return pltpu.roll(v, 1, 1)


def total(v):
    return jnp.sum(jnp.sum(v, axis=0, keepdims=True), axis=1, keepdims=True)


def kernel(ns, ng, u_in, p_in, f_in, k_in, br_in, fl_in, ez_in, cz_in, gt_in,
           disp_out, coef_out,
           disp_ref, coef_ref, osem, u_ref, p_ref, f_ref, k_ref, br_ref, fl_ref, ez_ref, cz_ref, gt_ref, isem,
           e1a, e1b, s1, h1, e2a, e2b, s2, h2, rqa, rqb, e3a, s3, h3,
           u1a, u1b, carry, dga, dgb, kca, kcb, gath, rows, outb, inb,
           ctake, cland, csend, crecv, send4, recv4, send0, recv0, send1, recv1, send2, recv2, send3, recv3, asend, arecv, tsend, trecv):
    X, Y = u_ref.shape[1], u_ref.shape[2]
    si, gi = lax.axis_index("slab"), lax.axis_index("grp")
    me = si * ng + gi
    count = ns * ng
    fetched = []
    for at, (source, target) in enumerate((
        (br_in, br_ref), (fl_in, fl_ref), (ez_in, ez_ref), (k_in, k_ref), (u_in, u_ref), (p_in, p_ref),
        (f_in, f_ref), (cz_in, cz_ref), (gt_in, gt_ref),
    )):
        fetch = pltpu.make_async_copy(source, target, isem.at[at])
        fetch.start()
        fetched.append(fetch)
    barrier = pltpu.get_barrier_semaphore()

    others = []
    for k in sorted(range(ns), key=lambda k: -min(k, ns - k)):
        for g in range(ng):
            if k or g:
                others.append((lax.rem(si + k, ns), lax.rem(gi + g, ng)))
    for other in others:
        pl.semaphore_signal(barrier, inc=1, device_id=other, device_id_type=MESH)

    sub, lane = sub_index(), lane_index()
    upper = sub < 4

    steps = [(-1, 0), (1, 0), (0, -1), (0, 1), (-1, -1), (-1, 1), (1, -1), (1, 1)]

    def inside(ds, dg):
        ok = None
        if ds:
            ok = (si >= 1) if ds < 0 else (si <= ns - 2)
        if dg:
            more = (gi >= 1) if dg < 0 else (gi <= ng - 2)
            ok = more if ok is None else jnp.logical_and(ok, more)
        return ok

    def copies(ea, dst_a, stage, land, send, recv, low=0, high=None, ways=8, reach=REACH):
        half = X // 2
        edge = HALO // 2
        made = []
        chans = pl.ds(low, (ea.shape[0] if high is None else high) - low)
        for at, (ds, dg) in enumerate(steps[:ways]):
            if dg == 0:
                if ds < 0:
                    source = ea.at[chans, pl.ds(HALO, reach)]
                    target = dst_a.at[chans, pl.ds(HALO + X, reach)]
                else:
                    source = ea.at[chans, pl.ds(HALO + X - reach, reach)]
                    target = dst_a.at[chans, pl.ds(HALO - reach, reach)]
            else:
                side = 0 if dg < 0 else 1
                if ds == 0:
                    source, target = stage.at[side, chans], land.at[side, chans, pl.ds(edge, half)]
                elif ds < 0:
                    source = stage.at[side, chans, pl.ds(0, 1)]
                    target = land.at[side, chans, pl.ds(edge + half, 1)]
                else:
                    source = stage.at[side, chans, pl.ds(half - 1, 1)]
                    target = land.at[side, chans, pl.ds(edge - 1, 1)]
            made.append((ds, dg, pltpu.make_async_remote_copy(
                src_ref=source, dst_ref=target, send_sem=send.at[at], recv_sem=recv.at[at ^ 1 if at < 4 else 11 - at],
                device_id=(si + ds, gi + dg), device_id_type=MESH)))
        return made

    def begin(made):
        for ds, dg, copy in made:
            @pl.when(inside(ds, dg))
            def _():
                copy.start()

    def finish_recv(made, recv):
        for at, (ds, dg) in enumerate(steps[:len(made)]):
            back = made[at ^ 1 if at < 4 else 11 - at][2]

            @pl.when(inside(ds, dg))
            def _():
                back.wait_recv()

    def finish_send(made):
        for ds, dg, copy in made:
            @pl.when(inside(ds, dg))
            def _():
                copy.wait_send()

    def blank(dst_a, land):
        zero_a = jnp.zeros((dst_a.shape[0], HALO) + dst_a.shape[2:], jnp.float32)
        half, edge = X // 2, HALO // 2
        zero_l = jnp.zeros((land.shape[1], edge, 8, 128), jnp.float32)

        @pl.when(si == 0)
        def _():
            dst_a[:, pl.ds(0, HALO)] = zero_a
            for side in range(2):
                land[side, :, pl.ds(0, edge)] = zero_l

        @pl.when(si == ns - 1)
        def _():
            dst_a[:, pl.ds(HALO + X, HALO)] = zero_a
            for side in range(2):
                land[side, :, pl.ds(edge + half, edge)] = zero_l

        for side, edge_here in ((0, gi == ng - 1), (1, gi == 0)):
            @pl.when(edge_here)
            def _(side=side):
                land[side] = jnp.zeros(land.shape[1:], jnp.float32)

    def pack(stage, ch, pair, even, odd):
        stage[0, ch, pair] = jnp.where(upper, even, pltpu.roll(odd, 4, 0))
        stage[1, ch, pair] = jnp.where(upper, pltpu.roll(even, 4, 0), odd)

    def unpack(land, ch, pair):
        high, low = land[0, ch, pair], land[1, ch, pair]
        return (jnp.where(upper, high, pltpu.roll(low, 4, 0)),
                jnp.where(upper, pltpu.roll(high, 4, 0), low))

    def spread_rows(mask):
        wide = jnp.dot(mask.astype(jnp.float32), ez_ref[...], preferred_element_type=jnp.float32)
        return jnp.where(upper, jnp.broadcast_to(wide[0:1], (8, 128)), jnp.broadcast_to(wide[1:2], (8, 128)))

    for at in range(4):
        fetched[at].wait()
    for bx in range(X // 4):
        cut = 1.0 - CRACK_CUT * spread_rows(br_ref[bx])
        flag = spread_rows(fl_ref[bx])
        for at in range(4):
            x = bx * 4 + at
            w = k_ref[x] * cut
            e1a[6, HALO + x] = w
            carry[x] = flag * w

    def own(i, _):
        for c in range(3):
            tiles = []
            for o in range(2):
                x = 2 * i + o
                u = u_ref[c, x]
                f = f_ref[c, x]
                rhs = MASS_TERM * (2.0 * u - p_ref[c, x]) + f
                e1a[c, HALO + x] = u
                e1a[3 + c, HALO + x] = rhs
                e2a[c, HALO + x] = f
                tiles.append((u, rhs, f))
            pack(s1, c, i, tiles[0][0], tiles[1][0])
            pack(s1, 3 + c, i, tiles[0][1], tiles[1][1])
            pack(s2, c, i, tiles[0][2], tiles[1][2])
        pack(s1, 6, i, e1a[6, HALO + 2 * i], e1a[6, HALO + 2 * i + 1])
        return 0

    for at in range(4, 7):
        fetched[at].wait()
    lax.fori_loop(0, X // 2, own, 0)
    blank(e1a, h1)
    blank(e2a, h2)
    blank(e3a, h3)

    def corner_copies():
        made = []
        for at, (ds, dg) in enumerate(steps[4:]):
            side, end = (0 if dg < 0 else 1), (0 if ds < 0 else 1)
            made.append((ds, dg, pltpu.make_async_remote_copy(
                src_ref=ctake.at[side, end], dst_ref=cland.at[side, 1 - end],
                send_sem=csend.at[at], recv_sem=crecv.at[3 - at],
                device_id=(si + ds, gi + dg), device_id_type=MESH)))
        return made

    near = sub % 4 < 2
    for side in range(2):
        for end in range(2):
            for t in range((7 + 1) // 2):
                tile = s1[side, 2 * t, end * (X // 2 - 1)]
                if 2 * t + 1 < 7:
                    other = s1[side, 2 * t + 1, end * (X // 2 - 1)]
                    tile = (jnp.where(near, tile, pltpu.roll(other, 2, 0)) if side == 0
                            else jnp.where(near, pltpu.roll(other, 6, 0), tile))
                ctake[side, end, t] = tile

    def corner_unpack(made):
        for at, (ds, dg) in enumerate(steps[4:]):
            side, end = (0 if dg > 0 else 1), (1 if ds > 0 else 0)
            pair = HALO // 2 + X // 2 if ds > 0 else HALO // 2 - 1
            back = made[3 - at][2]

            @pl.when(inside(ds, dg))
            def _():
                back.wait_recv()
                for ch in range(7):
                    tile = cland[side, end, ch // 2]
                    h1[side, ch, pair] = tile if ch % 2 == 0 else pltpu.roll(tile, 6 if side == 0 else 2, 0)

    corners = corner_copies()
    zeroth = copies(e1a, e1a, s1, h1, send0, recv0, 6, 7, 4)
    first = copies(e1a, e1a, s1, h1, send1, recv1, 0, 3, 4)
    rest = copies(e1a, e1a, s1, h1, send4, recv4, 3, 6, 4, REACH - 1)
    second = copies(e2a, e2a, s2, h2, send2, recv2)
    third = copies(rqa, e3a, s3, h3, send3, recv3)
    pl.semaphore_wait(barrier, count - 1)
    begin(zeroth)
    begin(corners)
    begin(first)
    begin(rest)
    finish_recv(zeroth, recv0)
    corner_unpack(corners)

    def open0(i, _):
        e1b[6, 2 * i], e1b[6, 2 * i + 1] = unpack(h1, 6, i)
        return 0

    def open1(i, _):
        for ch in range(6):
            e1b[ch, 2 * i], e1b[ch, 2 * i + 1] = unpack(h1, ch, i)
        return 0

    lax.fori_loop(0, (X + 2 * HALO) // 2, open0, 0)

    def link(w, other):
        return jnp.where(jnp.minimum(w, other) > 0.0, 0.5 * (w + other), 0.0)

    not_last, not_first = lane < 127, lane > 0

    def coefficients(x, _):
        wa, wb = e1a[6, x], e1b[6, x]
        ya, yb = up_y(wa, wb)
        da, db = down_y(wa, wb)
        for w, wu, wd, yu, yd, dg, kc in (
            (wa, e1a[6, x + 1], e1a[6, x - 1], ya, da, dga, kca),
            (wb, e1b[6, x + 1], e1b[6, x - 1], yb, db, dgb, kcb),
        ):
            zu = jnp.where(not_last, up_z(w), 0.0)
            zd = jnp.where(not_first, down_z(w), 0.0)
            kc[0, x] = link(w, wu)
            kc[1, x] = link(w, yu)
            kc[2, x] = link(w, yd)
            kc[3, x] = link(w, zu)
            kc[4, x] = link(w, zd)
            sx = w + 0.5 * (wu + wd)
            sy = w + 0.5 * (yu + yd)
            sz = w + 0.5 * (zu + zd)
            every = MASS_TERM + SPRING_SHEAR * (sx + sy + sz)
            dg[0, x] = every + SHEAR_REST * sx
            dg[1, x] = every + SHEAR_REST * sy
            dg[2, x] = every + SHEAR_REST * sz
        return 0

    kca[0, HALO - REACH] = link(e1a[6, HALO - REACH], e1a[6, HALO - REACH + 1])
    kcb[0, HALO - REACH] = link(e1b[6, HALO - REACH], e1b[6, HALO - REACH + 1])
    lax.fori_loop(HALO - 2, HALO + X + 2, coefficients, 0)
    finish_recv(first, recv1)
    finish_recv(rest, recv4)
    begin(second)
    lax.fori_loop(0, (X + 2 * HALO) // 2, open1, 0)

    def operate(x, va, vb, base, both=True):
        result = []
        coef = [[kc[j, x] for j in range(5)] + [kc[0, x - 1]] for kc in (kca, kcb)]
        for c in range(3):
            a, b = va[base + c, x], vb[base + c, x]
            ua, ub = up_y(a, b)
            la, lb = down_y(a, b)
            pair = []
            halves = ((a, va, ua, la, coef[0], dga), (b, vb, ub, lb, coef[1], dgb))
            for v, ref, u, l, k, dg in halves if both else halves[:1]:
                parts = (
                    k[0] * ref[base + c, x + 1] + k[5] * ref[base + c, x - 1],
                    k[1] * u + k[2] * l,
                    k[3] * up_z(v) + k[4] * down_z(v),
                )
                every = parts[0] + parts[1] + parts[2]
                pair.append(dg[c, x] * v - (SPRING_SHEAR * every + SHEAR_REST * parts[c]))
            result.append(pair)
        return result

    def solve(step, va, vb, rhs_of):
        def residual(i, _):
            done = []
            for x in (2 * i, 2 * i + 1):
                image = operate(x, va, vb, 0)
                for c in range(3):
                    ra, rb = rhs_of(c, x)
                    done.append((c, x, ra - image[c][0], rb - image[c][1]))
            for c, x, ra, rb in done:
                rqa[c, x] = ra
                rqb[c, x] = rb
            return 0

        lax.fori_loop((HALO - 2) // 2, (HALO + X + 2) // 2, residual, 0)

        def put(x, image):
            for c in range(3):
                rqa[3 + c, x] = image[c][0]
                rqb[3 + c, x] = image[c][1]

        def apply(i, sums):
            rr, rq = sums
            at = (2 * i, 2 * i + 1)
            images = [operate(x, rqa, rqb, 0) for x in at]
            for x, image in zip(at, images):
                for c in range(3):
                    r = rqa[c, x]
                    rr, rq = rr + r * r, rq + r * image[c][0]
            for x, image in zip(at, images):
                put(x, image)
            return rr, rq

        zero = jnp.zeros((8, 128), jnp.float32)
        images = [operate(x, rqa, rqb, 0) for x in (HALO - 1, HALO + X)]
        put(HALO - 1, images[0])
        put(HALO + X, images[1])
        rr, rq = lax.fori_loop(HALO // 2, (HALO + X) // 2, apply, (zero, zero))
        rr, rq = total(rr), total(rq)
        mu = jnp.where(rr > 0.0, rq / jnp.where(rr > 0.0, rr, 1.0), 0.0)

        def centred(i, sums):
            ww, wr, mix, wt = sums
            for x in (2 * i, 2 * i + 1):
                image = operate(x, rqa, rqb, 3, False)
                for c in range(3):
                    r, q, s = rqa[c, x], rqa[3 + c, x], image[c][0]
                    w, t = q - mu * r, s - mu * q
                    ww, wr, mix, wt = ww + w * w, wr + w * r, mix + (r * t + w * q), wt + w * t
            return ww, wr, mix, wt

        sums = lax.fori_loop(HALO // 2, (HALO + X) // 2, centred, (zero,) * 4)
        ww, wr, mix, wt = [total(v) for v in sums]
        one = lax.broadcasted_iota(jnp.int32, (1, 128), 1)
        row = jnp.zeros((1, 128), jnp.float32)
        for at, value in enumerate((rr, rq, mu, ww, wr, mix, wt)):
            row = jnp.where(one == at, value, row)
        gath[step, me] = row

        for other in others:
            pltpu.make_async_remote_copy(
                src_ref=gath.at[step, me], dst_ref=gath.at[step, me], send_sem=asend.at[step], recv_sem=arecv.at[step],
                device_id=other, device_id_type=MESH).start()

    def collect(step):
        block = gath.at[step, pl.ds(0, count - 1)]
        pltpu.make_async_copy(block, block, arecv.at[step]).wait()
        table = gath[step].reshape(count, 128)
        rr, rq, mu, ww, wr, mix, wt = [table[:, at:at + 1] for at in range(7)]

        def down(v):
            return jnp.sum(v, axis=0, keepdims=True)

        norm = down(rr)
        alpha = norm / down(rq)
        rest = 1.0 - alpha * mu
        after = down(alpha * alpha * ww - 2.0 * alpha * rest * wr + rest * rest * rr)
        curved = down(rest * rest * rq - alpha * rest * mix + alpha * alpha * wt)
        ratio = after / norm
        beta = after / (curved - ratio * after / alpha)
        return alpha + beta * (1.0 + ratio), -beta * alpha

    def drain(step):
        block = gath.at[step, pl.ds(0, count - 1)]
        pltpu.make_async_copy(block, block, asend.at[step]).wait()

    solve(0, e1a, e1b, lambda c, x: (e1a[3 + c, x], e1b[3 + c, x]))

    def pack3(i, _):
        for ch in range(6):
            pack(s3, ch, i, rqa[ch, HALO + 2 * i], rqa[ch, HALO + 2 * i + 1])
        return 0

    lax.fori_loop(0, X // 2, pack3, 0)
    begin(third)

    finish_recv(second, recv2)

    def open2(i, _):
        for ch in range(3):
            e2b[ch, 2 * i], e2b[ch, 2 * i + 1] = unpack(h2, ch, i)
        return 0

    lax.fori_loop(0, (X + 2 * HALO) // 2, open2, 0)
    finish_recv(third, recv3)
    c0, c1 = collect(0)

    def step_b(i, _):
        for c in range(3):
            r0, r1 = unpack(h3, c, i)
            q0, q1 = unpack(h3, 3 + c, i)
            u1b[c, 2 * i] = e1b[c, 2 * i] + (c0 * r0 + c1 * q0)
            u1b[c, 2 * i + 1] = e1b[c, 2 * i + 1] + (c0 * r1 + c1 * q1)
        return 0

    lax.fori_loop(0, (X + 2 * HALO) // 2, step_b, 0)

    def step_a(i, _):
        for x in (2 * i, 2 * i + 1):
            for c in range(3):
                u1a[c, x] = e1a[c, x] + (c0 * rqa[c, x] + c1 * rqa[3 + c, x])
        return 0

    lax.fori_loop(HALO // 2, (HALO + X) // 2, step_a, 0)
    for x in list(range(HALO - REACH, HALO)) + list(range(HALO + X, HALO + X + REACH)):
        for c in range(3):
            u1a[c, x] = e1a[c, x] + (c0 * e3a[c, x] + c1 * e3a[3 + c, x])
    finish_send(zeroth)
    finish_send(corners)
    finish_send(rest)
    finish_send(first)
    finish_send(second)
    finish_send(third)

    def rhs2(c, x):
        return (MASS_TERM * (2.0 * u1a[c, x] - e1a[c, x]) + e2a[c, x],
                MASS_TERM * (2.0 * u1b[c, x] - e1b[c, x]) + e2b[c, x])

    solve(1, u1a, u1b, rhs2)
    c0, c1 = collect(1)

    def step2(x, _):
        for c in range(3):
            va = u1a[c, x] + (c0 * rqa[c, x] + c1 * rqa[3 + c, x])
            vb = u1b[c, x] + (c0 * rqb[c, x] + c1 * rqb[3 + c, x])
            u1a[c, x] = va
            u1b[c, x] = vb
        return 0

    step2(HALO - 1, 0)
    step2(HALO + X, 0)

    def step2_own(i, _):
        for x in (2 * i, 2 * i + 1):
            step2(x, 0)
            for c in range(3):
                v = u1a[c, x]
                disp_ref[c, x - HALO] = v
                rows[c, pl.ds(x - HALO, 8, stride=X), :] = v
        return 0

    lax.fori_loop(HALO // 2, (HALO + X) // 2, step2_own, 0)
    outputs = [pltpu.make_async_copy(disp_ref, disp_out, osem.at[6])]
    outputs += [pltpu.make_async_copy(coef_ref.at[c], coef_out.at[c], osem.at[c]) for c in range(6)]
    zrows = coef_ref.shape[2]
    nt = (((1,), (1,)), ((), ()))

    def halves(v):
        high = v.astype(jnp.bfloat16)
        return high, (v - high.astype(jnp.float32)).astype(jnp.bfloat16)

    def transform(c, _):
        high, low = halves(rows[c])
        turned = lax.dot_general(cz_ref[:, 0:256], jnp.concatenate([high, low], axis=1), nt,
                                 preferred_element_type=jnp.float32)
        turned += lax.dot_general(cz_ref[:, 256:384], high, nt, preferred_element_type=jnp.float32)
        for j in range(ns):
            outb[j, c] = turned[j * zrows:(j + 1) * zrows]
        return 0

    def trade(part, i):
        to = lax.rem(si + i, ns)
        return pltpu.make_async_remote_copy(
            src_ref=outb.at[to, pl.ds(3 * part, 3)], dst_ref=inb.at[si, pl.ds(3 * part, 3)],
            send_sem=tsend.at[part, i], recv_sem=trecv.at[part, i],
            device_id=(to, gi), device_id_type=MESH)

    trades = [[trade(part, i) for i in range(1, ns)] for part in range(2)]

    def ship(part):
        lax.fori_loop(3 * part, 3 * part + 3, transform, 0)
        for copy in trades[part]:
            copy.start()
        for c in range(3 * part, 3 * part + 3):
            inb[si, c] = outb[si, c]

    fetched[7].wait()
    ship(0)
    outputs[0].start()

    def finals(i, _):
        for x in (2 * i, 2 * i + 1):
            at = x - HALO
            scale = SPRING_NORMAL * carry[at] * 0.5
            a1, a2, b1 = u1a[1, x], u1a[2, x], u1b[1, x]
            dx = u1a[0, x + 1] - u1a[0, x - 1]
            dy = up_y(a1, b1)[0] - down_y(a1, b1)[0]
            dz = jnp.where(not_last, up_z(a2), 0.0) - jnp.where(not_first, down_z(a2), 0.0)
            for c, d in enumerate((dx, dy, dz)):
                rows[3 + c, pl.ds(at, 8, stride=X), :] = scale * d
        return 0

    lax.fori_loop(HALO // 2, (HALO + X) // 2, finals, 0)
    ship(1)
    fetched[8].wait()

    zlane = lax.broadcasted_iota(jnp.int32, (zrows, 128), 1)
    c1t, c3t = float(np.sqrt(0.5) * np.cos(np.pi / 8)), float(np.sqrt(0.5) * np.cos(3 * np.pi / 8))

    def gather_back(c, _):
        pieces = [inb[j, c] for j in range(ns)]
        gap = ns // 2
        while gap:
            keep = (zlane // (X * gap)) % 2 == 0
            mixed = list(pieces)
            for j in range(ns):
                if (j // gap) % 2 == 0:
                    a, b = pieces[j], pieces[j + gap]
                    mixed[j] = jnp.where(keep, a, pltpu.roll(b, X * gap, 1))
                    mixed[j + gap] = jnp.where(keep, pltpu.roll(a, 128 - X * gap, 1), b)
            pieces = mixed
            gap //= 2
        coded = []
        for b in range(Y // 4):
            v0, v1, v2, v3 = pieces[4 * b:4 * b + 4]
            s03, s12, d03, d12 = v0 + v3, v1 + v2, v0 - v3, v1 - v2
            coded += [0.5 * (s03 + s12), c1t * d03 + c3t * d12, 0.5 * (s03 - s12), c3t * d03 - c1t * d12]
        high, low = halves(jnp.concatenate(coded, axis=0))
        done = jnp.dot(jnp.concatenate([high, low], axis=1), gt_ref[...], preferred_element_type=jnp.float32)
        coef_ref[c] = (done[:, 0:128] + done[:, 128:256]).reshape(Y, zrows, 128)
        return 0

    for part in range(2):
        for copy in trades[part]:
            copy.wait_recv()
        for c in range(3 * part, 3 * part + 3):
            gather_back(c, 0)
            outputs[1 + c].start()
    drain(0)
    drain(1)
    for part in range(2):
        for copy in trades[part]:
            copy.wait_send()
    for copy in outputs:
        copy.wait()


def fused(mesh, u_now, u_prev, force, stiffness, broken, flags):
    ns, ng = mesh.shape["slab"], mesh.shape["grp"]
    _, X, Y, Z = u_now.shape
    xe, pairs, half = X + 2 * HALO, X // 2 + HALO, X // 2
    zrows = Z // ns
    ez = jnp.asarray(np.kron(np.eye(Z // 4), np.ones((1, 4))), jnp.float32)
    czh, czl = split_table(np.kron(np.eye(Z // 4), cosine_table()))
    cz = jnp.asarray(np.concatenate([czh, czh, czl], axis=1), jnp.bfloat16)
    gth, gtl = split_table(wavelet_table(X * ns).T)
    gt = jnp.asarray(np.block([[gth, gtl], [gth, np.zeros_like(gtl)]]), jnp.bfloat16)

    def vm(*shape):
        return pltpu.VMEM(shape, jnp.float32)

    def ext(n):
        return vm(n, xe, Y, Z)

    def stage(n):
        return vm(2, n, half, Y, Z)

    def land(n):
        return vm(2, n, pairs, Y, Z)

    dma = pltpu.SemaphoreType.DMA
    return pl.pallas_call(
        lambda *refs: kernel(ns, ng, *refs),
        name="lattice",
        out_shape=(jax.ShapeDtypeStruct(u_now.shape, jnp.float32),
                   jax.ShapeDtypeStruct((6, Y, zrows, X * ns), jnp.float32)),
        in_specs=[pl.BlockSpec(memory_space=pltpu.MemorySpace.HBM)] * 9,
        out_specs=(pl.BlockSpec(memory_space=pltpu.MemorySpace.HBM),) * 2,
        scratch_shapes=[
            vm(*u_now.shape), vm(6, Y, zrows, X * ns), pltpu.SemaphoreType.DMA((7,)),
            vm(*u_now.shape), vm(*u_now.shape), vm(*u_now.shape), vm(*stiffness.shape),
            pltpu.VMEM(broken.shape, broken.dtype), pltpu.VMEM(flags.shape, flags.dtype),
            vm(*ez.shape), pltpu.VMEM(cz.shape, cz.dtype), pltpu.VMEM(gt.shape, gt.dtype), pltpu.SemaphoreType.DMA((9,)),
            ext(7), ext(7), stage(7), land(7),
            ext(3), ext(3), stage(3), land(3),
            ext(6), ext(6), ext(6), stage(6), land(6),
            ext(3), ext(3), vm(X, Y, Z), ext(3), ext(3), ext(5), ext(5),
            vm(2, ns * ng, 1, 128), vm(6, Y * X, Z), vm(ns, 6, zrows, 128), vm(ns, 6, zrows, 128),
            vm(2, 2, 4, Y, Z), vm(2, 2, 4, Y, Z), dma((4,)), dma((4,)), dma((8,)), dma((8,)),
            dma((8,)), dma((8,)), dma((8,)), dma((8,)), dma((8,)), dma((8,)), dma((8,)), dma((8,)),
            dma((2,)), dma((2,)), dma((2, ns)), dma((2, ns)),
        ],
        compiler_params=pltpu.CompilerParams(collective_id=0, has_side_effects=True, vmem_limit_bytes=60 << 20),
    )(u_now, u_prev, force, stiffness, broken, flags, ez, cz, gt)


def fits(mesh, shape):
    ns, ng = mesh.shape["slab"], mesh.shape["grp"]
    x, y, z = shape[1] // ns, shape[2] // ng, shape[3]
    return y == 8 and z == 128 and x * y == 128 and x * ns == 128 and z % (8 * ns) == 0


def entry(mesh, *args):
    ns, ng = mesh.shape["slab"], mesh.shape["grp"]
    _, x, y, z = args[0].shape
    if fits(mesh, (3, x * ns, y * ng, z)):
        return fused(mesh, *args)
    return body(*args)


def solution(mesh):
    return jax.shard_map(
        lambda *args: entry(mesh, *args),
        mesh=mesh,
        in_specs=(
            P(None, "slab", "grp", None),
            P(None, "slab", "grp", None),
            P(None, "slab", "grp", None),
            P("slab", "grp", None),
            P("slab", "grp", None),
            P("slab", "grp", None),
        ),
        out_specs=(P(None, "slab", "grp", None), P(None, "grp", "slab", None)),
        check_vma=False,
    )
```

```python
import jax
import jax.numpy as jnp
import numpy as np
from jax import lax
from jax.experimental import pallas as pl
from jax.experimental.pallas import tpu as pltpu
from jax.sharding import PartitionSpec as P

STEPS = 2
ITERS = 2
LEVELS = 3


SPRING_NORMAL = 1.0
SPRING_SHEAR = 0.4
MASS_TERM = 1.0
CRACK_CUT = 0.9


def with_halo(block, sides, width):
    for axis, dim in sides:
        count = lax.axis_size(axis)
        forward = [(i, i + 1) for i in range(count - 1)]
        backward = [(target, source) for source, target in forward]
        low = lax.ppermute(
            lax.slice_in_dim(block, block.shape[dim] - width, None, axis=dim), axis, forward
        )
        high = lax.ppermute(lax.slice_in_dim(block, 0, width, axis=dim), axis, backward)
        block = jnp.concatenate([low, block, high], axis=dim)
    return block


def cosine_table():
    freq = np.arange(4)[:, None]
    place = np.arange(4)[None, :]
    factor = np.where(freq == 0, 0.5, np.sqrt(0.5))
    return factor * np.cos(np.pi * (2 * place + 1) * freq / 8.0)


def block_table(count):
    return jnp.asarray(np.kron(np.eye(count // 4), cosine_table()), jnp.float32)


def spread(mask):
    values = mask.astype(jnp.float32)
    size_a, size_b, size_c = values.shape
    wide = jnp.broadcast_to(values[:, None, :, None, :, None], (size_a, 4, size_b, 4, size_c, 4))
    return wide.reshape(size_a * 4, size_b * 4, size_c * 4)


def sides(padded, axis_index):
    leading = padded.ndim - 3

    def cut(offset):
        index_list = [slice(None)] * leading + [slice(1, -1)] * 3
        length = padded.shape[leading + axis_index]
        index_list[leading + axis_index] = slice(1 + offset, length - 1 + offset)
        return padded[tuple(index_list)]

    return (cut(1), cut(-1))


def springs(field, weight, field_pad, weight_pad):
    result = MASS_TERM * field
    for axis_index in range(3):
        upper_v, lower_v = sides(field_pad, axis_index)
        upper_w, lower_w = sides(weight_pad, axis_index)
        k_upper = 0.5 * (weight + upper_w)
        k_lower = 0.5 * (weight + lower_w)
        change = k_upper * (field - upper_v) + k_lower * (field - lower_v)
        coupling = jnp.array(
            [SPRING_NORMAL if comp == axis_index else SPRING_SHEAR for comp in range(3)],
            jnp.float32,
        ).reshape(3, 1, 1, 1)
        result = result + coupling * change
    return result


def faces(field):
    padded = with_halo(field, (("slab", 1), ("grp", 2)), 1)
    return jnp.pad(padded, ((0, 0), (0, 0), (0, 0), (1, 1)))


def stresses(carry, field_pad):
    rows_out = []
    for axis_index in range(3):
        upper_v, lower_v = sides(field_pad, axis_index)
        rows_out.append(SPRING_NORMAL * carry * 0.5 * (upper_v[axis_index] - lower_v[axis_index]))
    return jnp.stack(rows_out)


def paired_sum(residual, image):
    return lax.psum((jnp.sum(residual * residual), jnp.sum(residual * image)), ("slab", "grp"))


def lift(signal):
    even = signal[..., 0::2]
    odd = signal[..., 1::2]
    detail = odd - 0.5 * (even + jnp.roll(even, -1, axis=-1))
    approx = even + 0.25 * (jnp.roll(detail, 1, axis=-1) + detail)
    return (approx, detail)


def wavelet(signal):
    pieces = []
    approx = signal
    for level_index in range(LEVELS):
        approx, detail = lift(approx)
        pieces.insert(0, detail)
    return jnp.concatenate([approx] + pieces, axis=-1)


def body(u_now, u_prev, force, stiffness, broken, flags):
    weight = stiffness * (1.0 - CRACK_CUT * spread(broken))
    carry = spread(flags) * weight
    weight_pad = with_halo(weight, (("slab", 0), ("grp", 1)), 1)
    weight_pad = jnp.pad(weight_pad, ((0, 0), (0, 0), (1, 1)))

    def operate(field):
        return springs(field, weight, faces(field), weight_pad)

    for step_index in range(STEPS):
        rhs = MASS_TERM * (2.0 * u_now - u_prev) + force
        guess = u_now
        residual = rhs - operate(guess)
        image = operate(residual)
        norm_now, product = paired_sum(residual, image)
        alpha = norm_now / product
        direction, along = (residual, image)
        for turn_index in range(ITERS):
            guess = guess + alpha * direction
            residual = residual - alpha * along
            if turn_index + 1 < ITERS:
                image = operate(residual)
                norm_next, product = paired_sum(residual, image)
                ratio = norm_next / norm_now
                alpha = norm_next / (product - ratio * norm_next / alpha)
                direction = residual + ratio * direction
                along = image + ratio * along
                norm_now = norm_next
        u_prev = u_now
        u_now = guess
    stress = stresses(carry, faces(u_now))
    fields = jnp.concatenate([u_now, stress], axis=0)
    table_x = block_table(fields.shape[1])
    table_y = block_table(fields.shape[2])
    table_z = block_table(fields.shape[3])
    blockc = jnp.einsum("ax,hxyz->hayz", table_x, fields, precision=lax.Precision.HIGHEST)
    blockc = jnp.einsum("by,hxyz->hxbz", table_y, blockc, precision=lax.Precision.HIGHEST)
    blockc = jnp.einsum("hxyz,cz->hxyc", blockc, table_z, precision=lax.Precision.HIGHEST)
    moved = jnp.transpose(blockc, (0, 2, 3, 1))
    shipped = lax.all_to_all(moved, "slab", split_axis=2, concat_axis=3, tiled=True)
    coeffs = wavelet(shipped)
    return (u_now, coeffs)


MESH = pl.DeviceIdType.MESH
HALO = 4
REACH = 3
SHEAR_REST = SPRING_NORMAL - SPRING_SHEAR


def wavelet_table(count):
    table = np.kron(np.eye(count // 4), cosine_table())
    pieces = []
    approx = table
    for level_index in range(LEVELS):
        even, odd = approx[0::2], approx[1::2]
        detail = odd - 0.5 * (even + np.roll(even, -1, axis=0))
        approx = even + 0.25 * (np.roll(detail, 1, axis=0) + detail)
        pieces.insert(0, detail)
    return np.concatenate([approx] + pieces, axis=0)


def split_table(table):
    high = table.astype(jnp.bfloat16).astype(np.float64)
    return high, (table - high).astype(jnp.bfloat16).astype(np.float64)


def sub_index():
    return lax.broadcasted_iota(jnp.int32, (8, 128), 0)


def lane_index():
    return lax.broadcasted_iota(jnp.int32, (8, 128), 1)


def up_y(a, b):
    ra, rb = pltpu.roll(a, 7, 0), pltpu.roll(b, 7, 0)
    last = sub_index() == 7
    return jnp.where(last, rb, ra), jnp.where(last, ra, rb)


def down_y(a, b):
    ra, rb = pltpu.roll(a, 1, 0), pltpu.roll(b, 1, 0)
    first = sub_index() == 0
    return jnp.where(first, rb, ra), jnp.where(first, ra, rb)


def up_z(v):
    return pltpu.roll(v, 127, 1)


def down_z(v):
    return pltpu.roll(v, 1, 1)


def total(v):
    return jnp.sum(jnp.sum(v, axis=0, keepdims=True), axis=1, keepdims=True)


def kernel(ns, ng, u_in, p_in, f_in, k_in, br_in, fl_in, ez_in, cz_in, gt_in,
           disp_out, coef_out,
           disp_ref, coef_ref, osem, u_ref, p_ref, f_ref, k_ref, br_ref, fl_ref, ez_ref, cz_ref, gt_ref, isem,
           e1a, e1b, s1, h1, e2a, e2b, s2, h2, rqa, rqb, e3a, s3, h3,
           u1a, u1b, carry, dga, dgb, kca, kcb, gath, rows, outb, inb,
           ctake, cland, csend, crecv, send4, recv4, send0, recv0, send1, recv1, send2, recv2, send3, recv3, asend, arecv, tsend, trecv):
    X, Y = u_ref.shape[1], u_ref.shape[2]
    si, gi = lax.axis_index("slab"), lax.axis_index("grp")
    me = si * ng + gi
    count = ns * ng
    fetched = []
    for at, (source, target) in enumerate((
        (br_in, br_ref), (fl_in, fl_ref), (ez_in, ez_ref), (k_in, k_ref), (u_in, u_ref), (p_in, p_ref),
        (f_in, f_ref), (cz_in, cz_ref), (gt_in, gt_ref),
    )):
        fetch = pltpu.make_async_copy(source, target, isem.at[at])
        fetch.start()
        fetched.append(fetch)
    barrier = pltpu.get_barrier_semaphore()

    others = []
    for k in sorted(range(ns), key=lambda k: -min(k, ns - k)):
        for g in range(ng):
            if k or g:
                others.append((lax.rem(si + k, ns), lax.rem(gi + g, ng)))
    for other in others:
        pl.semaphore_signal(barrier, inc=1, device_id=other, device_id_type=MESH)

    sub, lane = sub_index(), lane_index()
    upper = sub < 4

    steps = [(-1, 0), (1, 0), (0, -1), (0, 1), (-1, -1), (-1, 1), (1, -1), (1, 1)]

    def inside(ds, dg):
        ok = None
        if ds:
            ok = (si >= 1) if ds < 0 else (si <= ns - 2)
        if dg:
            more = (gi >= 1) if dg < 0 else (gi <= ng - 2)
            ok = more if ok is None else jnp.logical_and(ok, more)
        return ok

    def copies(ea, dst_a, stage, land, send, recv, low=0, high=None, ways=8, reach=REACH):
        half = X // 2
        edge = HALO // 2
        made = []
        chans = pl.ds(low, (ea.shape[0] if high is None else high) - low)
        for at, (ds, dg) in enumerate(steps[:ways]):
            if dg == 0:
                if ds < 0:
                    source = ea.at[chans, pl.ds(HALO, reach)]
                    target = dst_a.at[chans, pl.ds(HALO + X, reach)]
                else:
                    source = ea.at[chans, pl.ds(HALO + X - reach, reach)]
                    target = dst_a.at[chans, pl.ds(HALO - reach, reach)]
            else:
                side = 0 if dg < 0 else 1
                if ds == 0:
                    source, target = stage.at[side, chans], land.at[side, chans, pl.ds(edge, half)]
                elif ds < 0:
                    source = stage.at[side, chans, pl.ds(0, 1)]
                    target = land.at[side, chans, pl.ds(edge + half, 1)]
                else:
                    source = stage.at[side, chans, pl.ds(half - 1, 1)]
                    target = land.at[side, chans, pl.ds(edge - 1, 1)]
            made.append((ds, dg, pltpu.make_async_remote_copy(
                src_ref=source, dst_ref=target, send_sem=send.at[at], recv_sem=recv.at[at ^ 1 if at < 4 else 11 - at],
                device_id=(si + ds, gi + dg), device_id_type=MESH)))
        return made

    def begin(made):
        for ds, dg, copy in made:
            @pl.when(inside(ds, dg))
            def _():
                copy.start()

    def finish_recv(made, recv):
        for at, (ds, dg) in enumerate(steps[:len(made)]):
            back = made[at ^ 1 if at < 4 else 11 - at][2]

            @pl.when(inside(ds, dg))
            def _():
                back.wait_recv()

    def finish_send(made):
        for ds, dg, copy in made:
            @pl.when(inside(ds, dg))
            def _():
                copy.wait_send()

    def blank(dst_a, land):
        zero_a = jnp.zeros((dst_a.shape[0], HALO) + dst_a.shape[2:], jnp.float32)
        half, edge = X // 2, HALO // 2
        zero_l = jnp.zeros((land.shape[1], edge, 8, 128), jnp.float32)

        @pl.when(si == 0)
        def _():
            dst_a[:, pl.ds(0, HALO)] = zero_a
            for side in range(2):
                land[side, :, pl.ds(0, edge)] = zero_l

        @pl.when(si == ns - 1)
        def _():
            dst_a[:, pl.ds(HALO + X, HALO)] = zero_a
            for side in range(2):
                land[side, :, pl.ds(edge + half, edge)] = zero_l

        for side, edge_here in ((0, gi == ng - 1), (1, gi == 0)):
            @pl.when(edge_here)
            def _(side=side):
                land[side] = jnp.zeros(land.shape[1:], jnp.float32)

    def pack(stage, ch, pair, even, odd):
        stage[0, ch, pair] = jnp.where(upper, even, pltpu.roll(odd, 4, 0))
        stage[1, ch, pair] = jnp.where(upper, pltpu.roll(even, 4, 0), odd)

    def unpack(land, ch, pair):
        high, low = land[0, ch, pair], land[1, ch, pair]
        return (jnp.where(upper, high, pltpu.roll(low, 4, 0)),
                jnp.where(upper, pltpu.roll(high, 4, 0), low))

    def spread_rows(mask):
        wide = jnp.dot(mask.astype(jnp.float32), ez_ref[...], preferred_element_type=jnp.float32)
        return jnp.where(upper, jnp.broadcast_to(wide[0:1], (8, 128)), jnp.broadcast_to(wide[1:2], (8, 128)))

    for at in range(4):
        fetched[at].wait()
    for bx in range(X // 4):
        cut = 1.0 - CRACK_CUT * spread_rows(br_ref[bx])
        flag = spread_rows(fl_ref[bx])
        for at in range(4):
            x = bx * 4 + at
            w = k_ref[x] * cut
            e1a[6, HALO + x] = w
            carry[x] = flag * w

    def own(i, _):
        for c in range(3):
            tiles = []
            for o in range(2):
                x = 2 * i + o
                u = u_ref[c, x]
                f = f_ref[c, x]
                rhs = MASS_TERM * (2.0 * u - p_ref[c, x]) + f
                e1a[c, HALO + x] = u
                e1a[3 + c, HALO + x] = rhs
                e2a[c, HALO + x] = f
                tiles.append((u, rhs, f))
            pack(s1, c, i, tiles[0][0], tiles[1][0])
            pack(s1, 3 + c, i, tiles[0][1], tiles[1][1])
            pack(s2, c, i, tiles[0][2], tiles[1][2])
        pack(s1, 6, i, e1a[6, HALO + 2 * i], e1a[6, HALO + 2 * i + 1])
        return 0

    for at in range(4, 7):
        fetched[at].wait()
    lax.fori_loop(0, X // 2, own, 0)
    blank(e1a, h1)
    blank(e2a, h2)
    blank(e3a, h3)

    def corner_copies():
        made = []
        for at, (ds, dg) in enumerate(steps[4:]):
            side, end = (0 if dg < 0 else 1), (0 if ds < 0 else 1)
            made.append((ds, dg, pltpu.make_async_remote_copy(
                src_ref=ctake.at[side, end], dst_ref=cland.at[side, 1 - end],
                send_sem=csend.at[at], recv_sem=crecv.at[3 - at],
                device_id=(si + ds, gi + dg), device_id_type=MESH)))
        return made

    near = sub % 4 < 2
    for side in range(2):
        for end in range(2):
            for t in range((7 + 1) // 2):
                tile = s1[side, 2 * t, end * (X // 2 - 1)]
                if 2 * t + 1 < 7:
                    other = s1[side, 2 * t + 1, end * (X // 2 - 1)]
                    tile = (jnp.where(near, tile, pltpu.roll(other, 2, 0)) if side == 0
                            else jnp.where(near, pltpu.roll(other, 6, 0), tile))
                ctake[side, end, t] = tile

    def corner_unpack(made):
        for at, (ds, dg) in enumerate(steps[4:]):
            side, end = (0 if dg > 0 else 1), (1 if ds > 0 else 0)
            pair = HALO // 2 + X // 2 if ds > 0 else HALO // 2 - 1
            back = made[3 - at][2]

            @pl.when(inside(ds, dg))
            def _():
                back.wait_recv()
                for ch in range(7):
                    tile = cland[side, end, ch // 2]
                    h1[side, ch, pair] = tile if ch % 2 == 0 else pltpu.roll(tile, 6 if side == 0 else 2, 0)

    corners = corner_copies()
    zeroth = copies(e1a, e1a, s1, h1, send0, recv0, 6, 7, 4)
    first = copies(e1a, e1a, s1, h1, send1, recv1, 0, 3, 4)
    rest = copies(e1a, e1a, s1, h1, send4, recv4, 3, 6, 4, REACH - 1)
    second = copies(e2a, e2a, s2, h2, send2, recv2)
    third = copies(rqa, e3a, s3, h3, send3, recv3)
    pl.semaphore_wait(barrier, count - 1)
    begin(zeroth)
    begin(corners)
    begin(first)
    begin(rest)
    finish_recv(zeroth, recv0)
    corner_unpack(corners)

    def open0(i, _):
        e1b[6, 2 * i], e1b[6, 2 * i + 1] = unpack(h1, 6, i)
        return 0

    def open1(i, _):
        for ch in range(6):
            e1b[ch, 2 * i], e1b[ch, 2 * i + 1] = unpack(h1, ch, i)
        return 0

    lax.fori_loop(0, (X + 2 * HALO) // 2, open0, 0)

    def link(w, other):
        return jnp.where(jnp.minimum(w, other) > 0.0, 0.5 * (w + other), 0.0)

    not_last, not_first = lane < 127, lane > 0

    def coefficients(x, _):
        wa, wb = e1a[6, x], e1b[6, x]
        ya, yb = up_y(wa, wb)
        da, db = down_y(wa, wb)
        for w, wu, wd, yu, yd, dg, kc in (
            (wa, e1a[6, x + 1], e1a[6, x - 1], ya, da, dga, kca),
            (wb, e1b[6, x + 1], e1b[6, x - 1], yb, db, dgb, kcb),
        ):
            zu = jnp.where(not_last, up_z(w), 0.0)
            zd = jnp.where(not_first, down_z(w), 0.0)
            kc[0, x] = link(w, wu)
            kc[1, x] = link(w, yu)
            kc[2, x] = link(w, yd)
            kc[3, x] = link(w, zu)
            kc[4, x] = link(w, zd)
            sx = w + 0.5 * (wu + wd)
            sy = w + 0.5 * (yu + yd)
            sz = w + 0.5 * (zu + zd)
            every = MASS_TERM + SPRING_SHEAR * (sx + sy + sz)
            dg[0, x] = every + SHEAR_REST * sx
            dg[1, x] = every + SHEAR_REST * sy
            dg[2, x] = every + SHEAR_REST * sz
        return 0

    kca[0, HALO - REACH] = link(e1a[6, HALO - REACH], e1a[6, HALO - REACH + 1])
    kcb[0, HALO - REACH] = link(e1b[6, HALO - REACH], e1b[6, HALO - REACH + 1])
    lax.fori_loop(HALO - 2, HALO + X + 2, coefficients, 0)
    finish_recv(first, recv1)
    finish_recv(rest, recv4)
    begin(second)
    lax.fori_loop(0, (X + 2 * HALO) // 2, open1, 0)

    def operate(x, va, vb, base, both=True):
        result = []
        coef = [[kc[j, x] for j in range(5)] + [kc[0, x - 1]] for kc in (kca, kcb)]
        for c in range(3):
            a, b = va[base + c, x], vb[base + c, x]
            ua, ub = up_y(a, b)
            la, lb = down_y(a, b)
            pair = []
            halves = ((a, va, ua, la, coef[0], dga), (b, vb, ub, lb, coef[1], dgb))
            for v, ref, u, l, k, dg in halves if both else halves[:1]:
                parts = (
                    k[0] * ref[base + c, x + 1] + k[5] * ref[base + c, x - 1],
                    k[1] * u + k[2] * l,
                    k[3] * up_z(v) + k[4] * down_z(v),
                )
                every = parts[0] + parts[1] + parts[2]
                pair.append(dg[c, x] * v - (SPRING_SHEAR * every + SHEAR_REST * parts[c]))
            result.append(pair)
        return result

    def solve(step, va, vb, rhs_of):
        def residual(i, _):
            done = []
            for x in (2 * i, 2 * i + 1):
                image = operate(x, va, vb, 0)
                for c in range(3):
                    ra, rb = rhs_of(c, x)
                    done.append((c, x, ra - image[c][0], rb - image[c][1]))
            for c, x, ra, rb in done:
                rqa[c, x] = ra
                rqb[c, x] = rb
            return 0

        lax.fori_loop((HALO - 2) // 2, (HALO + X + 2) // 2, residual, 0)

        def put(x, image):
            for c in range(3):
                rqa[3 + c, x] = image[c][0]
                rqb[3 + c, x] = image[c][1]

        def apply(i, sums):
            rr, rq = sums
            at = (2 * i, 2 * i + 1)
            images = [operate(x, rqa, rqb, 0) for x in at]
            for x, image in zip(at, images):
                for c in range(3):
                    r = rqa[c, x]
                    rr, rq = rr + r * r, rq + r * image[c][0]
            for x, image in zip(at, images):
                put(x, image)
            return rr, rq

        zero = jnp.zeros((8, 128), jnp.float32)
        images = [operate(x, rqa, rqb, 0) for x in (HALO - 1, HALO + X)]
        put(HALO - 1, images[0])
        put(HALO + X, images[1])
        rr, rq = lax.fori_loop(HALO // 2, (HALO + X) // 2, apply, (zero, zero))
        rr, rq = total(rr), total(rq)
        mu = jnp.where(rr > 0.0, rq / jnp.where(rr > 0.0, rr, 1.0), 0.0)

        def centred(i, sums):
            ww, wr, mix, wt = sums
            for x in (2 * i, 2 * i + 1):
                image = operate(x, rqa, rqb, 3, False)
                for c in range(3):
                    r, q, s = rqa[c, x], rqa[3 + c, x], image[c][0]
                    w, t = q - mu * r, s - mu * q
                    ww, wr, mix, wt = ww + w * w, wr + w * r, mix + (r * t + w * q), wt + w * t
            return ww, wr, mix, wt

        sums = lax.fori_loop(HALO // 2, (HALO + X) // 2, centred, (zero,) * 4)
        ww, wr, mix, wt = [total(v) for v in sums]
        one = lax.broadcasted_iota(jnp.int32, (1, 128), 1)
        row = jnp.zeros((1, 128), jnp.float32)
        for at, value in enumerate((rr, rq, mu, ww, wr, mix, wt)):
            row = jnp.where(one == at, value, row)
        gath[step, me] = row

        for other in others:
            pltpu.make_async_remote_copy(
                src_ref=gath.at[step, me], dst_ref=gath.at[step, me], send_sem=asend.at[step], recv_sem=arecv.at[step],
                device_id=other, device_id_type=MESH).start()

    def collect(step):
        block = gath.at[step, pl.ds(0, count - 1)]
        pltpu.make_async_copy(block, block, arecv.at[step]).wait()
        table = gath[step].reshape(count, 128)
        rr, rq, mu, ww, wr, mix, wt = [table[:, at:at + 1] for at in range(7)]

        def down(v):
            return jnp.sum(v, axis=0, keepdims=True)

        norm = down(rr)
        alpha = norm / down(rq)
        rest = 1.0 - alpha * mu
        after = down(alpha * alpha * ww - 2.0 * alpha * rest * wr + rest * rest * rr)
        curved = down(rest * rest * rq - alpha * rest * mix + alpha * alpha * wt)
        ratio = after / norm
        beta = after / (curved - ratio * after / alpha)
        return alpha + beta * (1.0 + ratio), -beta * alpha

    def drain(step):
        block = gath.at[step, pl.ds(0, count - 1)]
        pltpu.make_async_copy(block, block, asend.at[step]).wait()

    solve(0, e1a, e1b, lambda c, x: (e1a[3 + c, x], e1b[3 + c, x]))

    def pack3(i, _):
        for ch in range(6):
            pack(s3, ch, i, rqa[ch, HALO + 2 * i], rqa[ch, HALO + 2 * i + 1])
        return 0

    lax.fori_loop(0, X // 2, pack3, 0)
    begin(third)

    finish_recv(second, recv2)

    def open2(i, _):
        for ch in range(3):
            e2b[ch, 2 * i], e2b[ch, 2 * i + 1] = unpack(h2, ch, i)
        return 0

    lax.fori_loop(0, (X + 2 * HALO) // 2, open2, 0)
    finish_recv(third, recv3)
    c0, c1 = collect(0)

    def step_b(i, _):
        for c in range(3):
            r0, r1 = unpack(h3, c, i)
            q0, q1 = unpack(h3, 3 + c, i)
            u1b[c, 2 * i] = e1b[c, 2 * i] + (c0 * r0 + c1 * q0)
            u1b[c, 2 * i + 1] = e1b[c, 2 * i + 1] + (c0 * r1 + c1 * q1)
        return 0

    lax.fori_loop(0, (X + 2 * HALO) // 2, step_b, 0)

    def step_a(i, _):
        for x in (2 * i, 2 * i + 1):
            for c in range(3):
                u1a[c, x] = e1a[c, x] + (c0 * rqa[c, x] + c1 * rqa[3 + c, x])
        return 0

    lax.fori_loop(HALO // 2, (HALO + X) // 2, step_a, 0)
    for x in list(range(HALO - REACH, HALO)) + list(range(HALO + X, HALO + X + REACH)):
        for c in range(3):
            u1a[c, x] = e1a[c, x] + (c0 * e3a[c, x] + c1 * e3a[3 + c, x])
    finish_send(zeroth)
    finish_send(corners)
    finish_send(rest)
    finish_send(first)
    finish_send(second)
    finish_send(third)

    def rhs2(c, x):
        return (MASS_TERM * (2.0 * u1a[c, x] - e1a[c, x]) + e2a[c, x],
                MASS_TERM * (2.0 * u1b[c, x] - e1b[c, x]) + e2b[c, x])

    solve(1, u1a, u1b, rhs2)
    c0, c1 = collect(1)

    def step2(x, _):
        for c in range(3):
            va = u1a[c, x] + (c0 * rqa[c, x] + c1 * rqa[3 + c, x])
            vb = u1b[c, x] + (c0 * rqb[c, x] + c1 * rqb[3 + c, x])
            u1a[c, x] = va
            u1b[c, x] = vb
        return 0

    step2(HALO - 1, 0)
    step2(HALO + X, 0)

    def step2_own(i, _):
        for x in (2 * i, 2 * i + 1):
            step2(x, 0)
            for c in range(3):
                v = u1a[c, x]
                disp_ref[c, x - HALO] = v
                rows[c, pl.ds(x - HALO, 8, stride=X), :] = v
        return 0

    lax.fori_loop(HALO // 2, (HALO + X) // 2, step2_own, 0)
    outputs = [pltpu.make_async_copy(disp_ref, disp_out, osem.at[6])]
    outputs += [pltpu.make_async_copy(coef_ref.at[c], coef_out.at[c], osem.at[c]) for c in range(6)]
    zrows = coef_ref.shape[2]
    nt = (((1,), (1,)), ((), ()))

    def halves(v):
        high = v.astype(jnp.bfloat16)
        return high, (v - high.astype(jnp.float32)).astype(jnp.bfloat16)

    def transform(c, _):
        high, low = halves(rows[c])
        turned = lax.dot_general(cz_ref[:, 0:256], jnp.concatenate([high, low], axis=1), nt,
                                 preferred_element_type=jnp.float32)
        turned += lax.dot_general(cz_ref[:, 256:384], high, nt, preferred_element_type=jnp.float32)
        for j in range(ns):
            outb[j, c] = turned[j * zrows:(j + 1) * zrows]
        return 0

    def trade(part, i):
        to = lax.rem(si + i, ns)
        return pltpu.make_async_remote_copy(
            src_ref=outb.at[to, pl.ds(3 * part, 3)], dst_ref=inb.at[si, pl.ds(3 * part, 3)],
            send_sem=tsend.at[part, i], recv_sem=trecv.at[part, i],
            device_id=(to, gi), device_id_type=MESH)

    order = sorted(range(1, ns), key=lambda i: -min(i, ns - i))
    trades = [[trade(part, i) for i in order] for part in range(2)]

    def ship(part):
        lax.fori_loop(3 * part, 3 * part + 3, transform, 0)
        for copy in trades[part]:
            copy.start()
        for c in range(3 * part, 3 * part + 3):
            inb[si, c] = outb[si, c]

    fetched[7].wait()
    ship(0)
    outputs[0].start()

    def finals(i, _):
        for x in (2 * i, 2 * i + 1):
            at = x - HALO
            scale = SPRING_NORMAL * carry[at] * 0.5
            a1, a2, b1 = u1a[1, x], u1a[2, x], u1b[1, x]
            dx = u1a[0, x + 1] - u1a[0, x - 1]
            dy = up_y(a1, b1)[0] - down_y(a1, b1)[0]
            dz = jnp.where(not_last, up_z(a2), 0.0) - jnp.where(not_first, down_z(a2), 0.0)
            for c, d in enumerate((dx, dy, dz)):
                rows[3 + c, pl.ds(at, 8, stride=X), :] = scale * d
        return 0

    lax.fori_loop(HALO // 2, (HALO + X) // 2, finals, 0)
    ship(1)
    fetched[8].wait()

    zlane = lax.broadcasted_iota(jnp.int32, (zrows, 128), 1)
    c1t, c3t = float(np.sqrt(0.5) * np.cos(np.pi / 8)), float(np.sqrt(0.5) * np.cos(3 * np.pi / 8))

    def gather_back(c, _):
        pieces = [inb[j, c] for j in range(ns)]
        gap = ns // 2
        while gap:
            keep = (zlane // (X * gap)) % 2 == 0
            mixed = list(pieces)
            for j in range(ns):
                if (j // gap) % 2 == 0:
                    a, b = pieces[j], pieces[j + gap]
                    mixed[j] = jnp.where(keep, a, pltpu.roll(b, X * gap, 1))
                    mixed[j + gap] = jnp.where(keep, pltpu.roll(a, 128 - X * gap, 1), b)
            pieces = mixed
            gap //= 2
        coded = []
        for b in range(Y // 4):
            v0, v1, v2, v3 = pieces[4 * b:4 * b + 4]
            s03, s12, d03, d12 = v0 + v3, v1 + v2, v0 - v3, v1 - v2
            coded += [0.5 * (s03 + s12), c1t * d03 + c3t * d12, 0.5 * (s03 - s12), c3t * d03 - c1t * d12]
        high, low = halves(jnp.concatenate(coded, axis=0))
        done = jnp.dot(jnp.concatenate([high, low], axis=1), gt_ref[...], preferred_element_type=jnp.float32)
        coef_ref[c] = (done[:, 0:128] + done[:, 128:256]).reshape(Y, zrows, 128)
        return 0

    for part in range(2):
        for copy in trades[part]:
            copy.wait_recv()
        for c in range(3 * part, 3 * part + 3):
            gather_back(c, 0)
            outputs[1 + c].start()
    drain(0)
    drain(1)
    for part in range(2):
        for copy in trades[part]:
            copy.wait_send()
    for copy in outputs:
        copy.wait()


def fused(mesh, u_now, u_prev, force, stiffness, broken, flags):
    ns, ng = mesh.shape["slab"], mesh.shape["grp"]
    _, X, Y, Z = u_now.shape
    xe, pairs, half = X + 2 * HALO, X // 2 + HALO, X // 2
    zrows = Z // ns
    ez = jnp.asarray(np.kron(np.eye(Z // 4), np.ones((1, 4))), jnp.float32)
    czh, czl = split_table(np.kron(np.eye(Z // 4), cosine_table()))
    cz = jnp.asarray(np.concatenate([czh, czh, czl], axis=1), jnp.bfloat16)
    gth, gtl = split_table(wavelet_table(X * ns).T)
    gt = jnp.asarray(np.block([[gth, gtl], [gth, np.zeros_like(gtl)]]), jnp.bfloat16)

    def vm(*shape):
        return pltpu.VMEM(shape, jnp.float32)

    def ext(n):
        return vm(n, xe, Y, Z)

    def stage(n):
        return vm(2, n, half, Y, Z)

    def land(n):
        return vm(2, n, pairs, Y, Z)

    dma = pltpu.SemaphoreType.DMA
    return pl.pallas_call(
        lambda *refs: kernel(ns, ng, *refs),
        name="lattice",
        out_shape=(jax.ShapeDtypeStruct(u_now.shape, jnp.float32),
                   jax.ShapeDtypeStruct((6, Y, zrows, X * ns), jnp.float32)),
        in_specs=[pl.BlockSpec(memory_space=pltpu.MemorySpace.HBM)] * 9,
        out_specs=(pl.BlockSpec(memory_space=pltpu.MemorySpace.HBM),) * 2,
        scratch_shapes=[
            vm(*u_now.shape), vm(6, Y, zrows, X * ns), pltpu.SemaphoreType.DMA((7,)),
            vm(*u_now.shape), vm(*u_now.shape), vm(*u_now.shape), vm(*stiffness.shape),
            pltpu.VMEM(broken.shape, broken.dtype), pltpu.VMEM(flags.shape, flags.dtype),
            vm(*ez.shape), pltpu.VMEM(cz.shape, cz.dtype), pltpu.VMEM(gt.shape, gt.dtype), pltpu.SemaphoreType.DMA((9,)),
            ext(7), ext(7), stage(7), land(7),
            ext(3), ext(3), stage(3), land(3),
            ext(6), ext(6), ext(6), stage(6), land(6),
            ext(3), ext(3), vm(X, Y, Z), ext(3), ext(3), ext(5), ext(5),
            vm(2, ns * ng, 1, 128), vm(6, Y * X, Z), vm(ns, 6, zrows, 128), vm(ns, 6, zrows, 128),
            vm(2, 2, 4, Y, Z), vm(2, 2, 4, Y, Z), dma((4,)), dma((4,)), dma((8,)), dma((8,)),
            dma((8,)), dma((8,)), dma((8,)), dma((8,)), dma((8,)), dma((8,)), dma((8,)), dma((8,)),
            dma((2,)), dma((2,)), dma((2, ns)), dma((2, ns)),
        ],
        compiler_params=pltpu.CompilerParams(collective_id=0, has_side_effects=True, vmem_limit_bytes=60 << 20),
    )(u_now, u_prev, force, stiffness, broken, flags, ez, cz, gt)


def fits(mesh, shape):
    ns, ng = mesh.shape["slab"], mesh.shape["grp"]
    x, y, z = shape[1] // ns, shape[2] // ng, shape[3]
    return y == 8 and z == 128 and x * y == 128 and x * ns == 128 and z % (8 * ns) == 0


def entry(mesh, *args):
    ns, ng = mesh.shape["slab"], mesh.shape["grp"]
    _, x, y, z = args[0].shape
    if fits(mesh, (3, x * ns, y * ng, z)):
        return fused(mesh, *args)
    return body(*args)


def solution(mesh):
    return jax.shard_map(
        lambda *args: entry(mesh, *args),
        mesh=mesh,
        in_specs=(
            P(None, "slab", "grp", None),
            P(None, "slab", "grp", None),
            P(None, "slab", "grp", None),
            P("slab", "grp", None),
            P("slab", "grp", None),
            P("slab", "grp", None),
        ),
        out_specs=(P(None, "slab", "grp", None), P(None, "grp", "slab", None)),
        check_vma=False,
    )
```
